128 devices in a mesh: row: 8 (over x_lo, z), col: 16 (over y, x_hi, core).
Axes of the slice: x: 4 (x_hi: 2, x_lo: 2; x = x_hi * 2 + x_lo), y: 4, z: 4, core: 2. Of those that a mesh axis runs over, the one named last changes fastest.
Arguments:
- grad: bfloat16 [16384, 26624], P(('row', 'col')), may hold values from -6 to 6
- basis_new: bfloat16 [16384, 512], P('row'), may hold values from -0.046875 to 0.046875
- basis_old: bfloat16 [16384, 512], P('row'), may hold values from -0.046875 to 0.046875
- moment_first: float32 [512, 26624], P('row', 'col'), may hold values from -18 to 18
- moment_second: float32 [512, 26624], P('row', 'col'), may hold values from 0.5 to 8
Outputs:
- update: bfloat16 [16384, 26624], P(('row', 'col'))
- first_new: float32 [512, 26624], P('row', 'col')
- second_new: float32 [512, 26624], P('row', 'col')
The draws below stay inside these ranges and needn't reach their ends.
All inputs are finite; a program needn't handle non-finite values.
Results may differ from the reference program's by a relative error of at most 0.0049.
Values may be sent and summed in bfloat16 or wider, within the bound.
No kernel may reach another device: no remote copies, remote signals or barrier semaphores. Data moves between devices by JAX's collectives and lax.ppermute only.
A program may use at most 128 MiB of HBM per device.

```python
import math
import jax
import jax.numpy as jnp
from jax import lax

M = 16384
N = 26624
R = 512
STEP = 10


def block_levels(key, dims, pieces, smallest, top_value):
    factor_of = 1.0
    for dim, blocks in pieces:
        steps = jax.random.uniform(jax.random.fold_in(jax.random.fold_in(key, 6), dim), (blocks,), jnp.float32, smallest / len(pieces), top_value / len(pieces))
        factor_of = factor_of * jnp.repeat(jnp.exp(steps), dims[dim] // blocks).reshape((-1,) + (1,) * (len(dims) - 1 - dim))
    return factor_of


def gaussian(own_key, shape, width, limit, pieces=(), kind=jnp.bfloat16):
    array = width * jax.random.normal(own_key, shape, jnp.float32)
    if pieces:
        array = array * block_levels(own_key, shape, pieces, -0.22, 0.18)
    return jnp.clip(array, -limit, limit).astype(kind)


def setup_inputs(seed: int = 0) -> dict:
    streams_of = jax.random.split(jax.random.key(seed), 6)
    return {
        "grad": gaussian(streams_of[0], (M, N), 1.0, 6.0, ((0, 128),)),
        "basis_new": gaussian(streams_of[1], (M, R), M ** -0.5, 0.046875, ((0, 8),)),
        "basis_old": gaussian(streams_of[2], (M, R), M ** -0.5, 0.046875, ((0, 8),)),
        "moment_first": gaussian(streams_of[3], (R, N), 3.0, 18.0, ((0, 8), (1, 16)), jnp.float32),
        "moment_second": jnp.clip(jnp.exp(math.log(8.0) - 2.7725887 * jax.random.uniform(streams_of[4], (R, N), jnp.float32) ** block_levels(streams_of[4], (R, N), ((0, 8), (1, 16)), -0.2, 0.2)), 0.5, 8.0),
    }


def reference(grad, basis_new, basis_old, moment_first, moment_second):
    margin = jnp.dot(basis_new.T, basis_old, preferred_element_type=jnp.float32)
    projected = jnp.dot(basis_new.T, grad, preferred_element_type=jnp.float32)
    rotated_one = jnp.dot(margin, moment_first, precision=lax.Precision.HIGHEST)
    rotated_two = jnp.dot(margin * margin, moment_second, precision=lax.Precision.HIGHEST)
    first_new = 0.9 * rotated_one + 0.1 * projected
    second_new = 0.999 * rotated_two + 0.001 * projected * projected
    low_step = (first_new / (1.0 - 0.9 ** STEP) / (jnp.sqrt(second_new / (1.0 - 0.999 ** STEP)) + 1e-08)).astype(jnp.bfloat16)
    update = (8.0 * jnp.dot(basis_new, low_step, preferred_element_type=jnp.float32)).astype(jnp.bfloat16)
    return (update, first_new, second_new)
```

```python
import functools

import jax
import jax.numpy as jnp
from jax import lax
from jax.experimental import pallas as pl
from jax.experimental.pallas import tpu as pltpu
from jax.sharding import Mesh, PartitionSpec as P

STEP = 10
BF, F32 = jnp.bfloat16, jnp.float32
NAMES = ("xl", "z", "y", "xh", "core")
ROW = ("xl", "z")
ANY = pl.BlockSpec(memory_space=pl.ANY)
SMEM = pl.BlockSpec(memory_space=pltpu.SMEM)
VMEM = pl.BlockSpec(memory_space=pltpu.VMEM)
DMA = pltpu.SemaphoreType.DMA
OFFSETS = ((0, 0), (2, 0), (2, 1), (1, 0), (3, 0), (1, 1), (3, 1), (0, 1))
PARTS = (("y", "x", "z", 1280, 80), ("z", "y", "x", 1024, 64), ("x", "z", "y", 1024, 64))
SLOT = {"x": 0, "y": 1, "z": 2, "core": 3, "xh": 4}


def place(where, axis):
    return where[SLOT[axis]]


def runs(ring, at, core):
    if ring == "y":
        return [((at * 4 + xh * 2 + core) * 13, 5) for xh in range(2)]
    if ring == "z":
        return [((y * 4 + xh * 2 + core) * 13 + 5 + at, 1) for y in range(4) for xh in range(2)]
    xh, xl = at // 2, at % 2
    return [((y * 4 + xh * 2 + core) * 13 + 9 + 2 * xl, 2) for y in range(4)]


def pieces(part, u_at):
    ring, _, _, chunk, piece = part
    if ring == "x":
        return [(v * 4 * piece + u_at * piece, piece) for v in range(4)]
    return [(u_at * (chunk // 4), chunk // 4)]


def shift(array, ring, step, core_step=None):
    if ring == "x":
        axes, spots = ("xl", "xh"), [(xh * 2 + xl) for xl in range(2) for xh in range(2)]
    else:
        axes, spots = (ring,), list(range(4))
    number = {spot: i for i, spot in enumerate(spots)}
    pairs = [(i, number[(spot + step) % 4]) for i, spot in enumerate(spots)]
    if core_step is not None:
        axes = axes + ("core",)
        pairs = [(2 * a + c, 2 * b + (c + core_step) % 2) for a, b in pairs for c in range(2)]
    return lax.ppermute(array, axes, pairs)


def tiles(first, count):
    return pl.ds(pl.multiple_of(first * 128, 128), count * 128)


def rows_at(first, count):
    return pl.ds(pl.multiple_of(first, 16), count)


def estimate(flops, size):
    return pl.CostEstimate(flops=flops, bytes_accessed=size, transcendentals=0)


def pack_kernel(part, where, grad, *refs):
    outs, held, in_sem, out_sem = refs[:8], refs[8], refs[9], refs[10]
    ring = part[0]
    t, core = place(where, ring), place(where, "core")
    loads = []
    for k, (step, core_step) in enumerate(OFFSETS):
        at, done, mine = (t + step) % 4, 0, []
        for j, (first, count) in enumerate(runs(ring, at, (core + core_step) % 2)):
            copy = pltpu.make_async_copy(
                grad.at[:, tiles(first, count)], held.at[k, :, pl.ds(done, count * 128)], in_sem.at[k, j]
            )
            copy.start()
            mine.append(copy)
            done += count * 128
        loads.append(mine)
    stores = []
    for k in range(8):
        for copy in loads[k]:
            copy.wait()
        copy = pltpu.make_async_copy(held.at[k], outs[k], out_sem.at[k])
        copy.start()
        stores.append(copy)
    for copy in stores:
        copy.wait()


def pack(part, where, grad):
    chunk = part[3]
    return pl.pallas_call(
        functools.partial(pack_kernel, part),
        out_shape=[jax.ShapeDtypeStruct((128, chunk), BF)] * 8,
        in_specs=[SMEM, ANY],
        out_specs=[ANY] * 8,
        scratch_shapes=[pltpu.VMEM((8, 128, chunk), BF), DMA((8, 8)), DMA((8,))],
        cost_estimate=estimate(0, 8 * 128 * chunk * 4),
        name="pack_" + part[0],
    )(where, grad)


def unpack_kernel(part, where, *refs):
    ring = part[0]
    blocks, (out, held, in_sem, out_sem) = refs[:8], refs[-4:]
    t, core = place(where, ring), place(where, "core")
    loads = [pltpu.make_async_copy(blocks[k], held.at[k], in_sem.at[k]) for k in range(8)]
    for copy in loads:
        copy.start()
    stores = []
    for k, (step, core_step) in enumerate(OFFSETS):
        loads[k].wait()
        done = 0
        for j, (first, count) in enumerate(runs(ring, (t + 4 - step) % 4, (core + core_step) % 2)):
            copy = pltpu.make_async_copy(
                held.at[k, :, pl.ds(done, count * 128)], out.at[:, tiles(first, count)], out_sem.at[k, j]
            )
            copy.start()
            stores.append(copy)
            done += count * 128
    for copy in stores:
        copy.wait()


def unpack(part, where, blocks, before, columns):
    chunk = part[3]
    more = [] if before is None else [before]
    return pl.pallas_call(
        functools.partial(unpack_kernel, part),
        out_shape=jax.ShapeDtypeStruct((128, columns), BF),
        in_specs=[SMEM] + [ANY] * (8 + len(more)),
        out_specs=ANY,
        scratch_shapes=[pltpu.VMEM((8, 128, chunk), BF), DMA((8,)), DMA((8, 8))],
        input_output_aliases={9: 0} if more else {},
        cost_estimate=estimate(0, 8 * 128 * chunk * 4),
        name="unpack_" + part[0],
    )(where, *blocks, *more)


def basis_rows(part, where, step, core_step, bases):
    ring = part[0]
    at = (place(where, ring) + step) % 4
    core = (place(where, "core") + core_step) % 2
    if ring == "y":
        base, first = bases[0], at * 4 + place(where, "xh") * 2 + core
    elif ring == "z":
        base, first = bases[step % 4], core
    elif step % 2 == 0:
        base, first = bases[0], place(where, "y") * 4 + (at // 2) * 2 + core
    else:
        base, first = bases[1], (at // 2) * 2 + core
    return base.at[pl.ds(pl.multiple_of(first * 128, 128), 128), :]


def project_kernel(part, count, where, *refs):
    blocks, bases, outs = refs[:8], refs[8 : 8 + count], refs[8 + count : 12 + count]
    held, base, total, in_sem, base_sem, out_sem = refs[12 + count :]
    _, u, _, chunk, _ = part
    copies = []
    for k, (step, core_step) in enumerate(OFFSETS):
        rows = pl.ds(k * 128, 128)
        copies.append(pltpu.make_async_copy(blocks[k], held.at[rows, :], in_sem.at[k]))
        source = basis_rows(part, where, 4 - step, core_step, bases)
        copies.append(pltpu.make_async_copy(source, base.at[rows, :], base_sem.at[k]))
    for copy in copies:
        copy.start()
    for copy in copies:
        copy.wait()

    @pl.loop(0, chunk // 256)
    def _(i):
        columns = pl.ds(pl.multiple_of(i * 256, 256), 256)
        product = lax.dot_general(
            held[:, columns], base[...], (((0,), (0,)), ((), ())), preferred_element_type=F32
        )
        total[columns, :] = product.astype(BF)

    stores = []
    for j in range(4):
        done = 0
        for i, (first, size) in enumerate(pieces(part, (place(where, u) + j) % 4)):
            copy = pltpu.make_async_copy(
                total.at[rows_at(first, size), :], outs[j].at[pl.ds(done, size), :], out_sem.at[j, i]
            )
            copy.start()
            stores.append(copy)
            done += size
    for copy in stores:
        copy.wait()


def project(part, where, blocks, bases):
    chunk = part[3]
    return pl.pallas_call(
        functools.partial(project_kernel, part, len(bases)),
        out_shape=[jax.ShapeDtypeStruct((chunk // 4, 512), BF)] * 4,
        in_specs=[SMEM] + [ANY] * (8 + len(bases)),
        out_specs=[ANY] * 4,
        scratch_shapes=[
            pltpu.VMEM((1024, chunk), BF),
            pltpu.VMEM((1024, 512), BF),
            pltpu.VMEM((chunk, 512), BF),
            DMA((8,)),
            DMA((8,)),
            DMA((4, 4)),
        ],
        cost_estimate=estimate(2 * 1024 * 512 * chunk, 1024 * chunk * 2 + 1024 * 1024 + chunk * 1024),
        name="project_" + part[0],
    )(where, *blocks, *bases)


def add_kernel(part, where, a, b, c, d, *refs):
    outs, total = refs[:4], refs[4]
    _, _, v, _, piece = part
    total[...] = (
        (a[...].astype(F32) + b[...].astype(F32)) + (c[...].astype(F32) + d[...].astype(F32))
    ).astype(BF)
    for j in range(4):
        at = (place(where, v) + j) % 4
        outs[j][...] = total[rows_at(at * piece, piece), :]


def add_up(part, where, arrays):
    _, _, _, chunk, piece = part
    return pl.pallas_call(
        functools.partial(add_kernel, part),
        out_shape=[jax.ShapeDtypeStruct((piece, 512), BF)] * 4,
        in_specs=[SMEM] + [VMEM] * 4,
        out_specs=[VMEM] * 4,
        scratch_shapes=[pltpu.VMEM((chunk // 4, 512), BF)],
        cost_estimate=estimate(3 * chunk * 128, 5 * chunk * 256),
        name="add_" + part[0],
    )(where, *arrays)


def split(value):
    high = value.astype(BF)
    return high, (value - high.astype(F32)).astype(BF)


def step_kernel(*refs):
    sums, (margin, one, two), lows, (first_out, second_out) = refs[:12], refs[12:15], refs[15:18], refs[18:20]
    projected = jnp.concatenate(
        [sum(refs_k[...].astype(F32) for refs_k in sums[4 * p : 4 * p + 4]) for p in range(3)], axis=0
    )
    contract = (((0,), (1,)), ((), ()))
    m = margin[...]
    high, low = split(m)
    moment = one[...].astype(BF)
    rotated_one = lax.dot_general(moment, high, contract, preferred_element_type=F32) + lax.dot_general(
        moment, low, contract, preferred_element_type=F32
    )
    rotated_two = lax.dot_general(
        two[...].astype(BF), (m * m).astype(BF), contract, preferred_element_type=F32
    )
    first_new = 0.9 * rotated_one + 0.1 * projected
    second_new = 0.999 * rotated_two + 0.001 * projected * projected
    low_step = (
        first_new / (1.0 - 0.9**STEP) / (jnp.sqrt(second_new / (1.0 - 0.999**STEP)) + 1e-08)
    ).astype(BF)
    begin = 0
    for ref in lows:
        ref[...] = low_step[begin : begin + ref.shape[0], :]
        begin += ref.shape[0]
    first_out[...] = first_new
    second_out[...] = second_new


def take_step(sums, margin, one, two):
    return pl.pallas_call(
        step_kernel,
        out_shape=[jax.ShapeDtypeStruct((part[4], 512), BF) for part in PARTS]
        + [jax.ShapeDtypeStruct((208, 512), F32)] * 2,
        in_specs=[VMEM] * 15,
        out_specs=[VMEM] * 5,
        cost_estimate=estimate(6 * 208 * 512 * 512, 4 * 2**20),
        name="step",
    )(*sums, margin, one, two)


def join_kernel(part, where, *refs):
    arrays, out = refs[:4], refs[4]
    _, _, v, _, piece = part
    for j in range(4):
        at = (place(where, v) + 4 - j) % 4
        out[rows_at(at * piece, piece), :] = arrays[j][...]


def join(part, where, arrays):
    return pl.pallas_call(
        functools.partial(join_kernel, part),
        out_shape=jax.ShapeDtypeStruct((part[3] // 4, 512), BF),
        in_specs=[SMEM] + [VMEM] * 4,
        out_specs=VMEM,
        cost_estimate=estimate(0, part[3] * 512),
        name="join_" + part[0],
    )(where, *arrays)


def update_kernel(part, count, where, *refs):
    arrays, bases, outs = refs[:4], refs[4 : 4 + count], refs[4 + count : 12 + count]
    low, base, held, in_sem, base_sem, out_sem = refs[12 + count :]
    _, u, _, chunk, _ = part
    copies = []
    for j in range(4):
        done = 0
        for i, (first, size) in enumerate(pieces(part, (place(where, u) + 4 - j) % 4)):
            copies.append(
                pltpu.make_async_copy(
                    arrays[j].at[pl.ds(done, size), :], low.at[rows_at(first, size), :], in_sem.at[j, i]
                )
            )
            done += size
    for k, (step, core_step) in enumerate(OFFSETS):
        source = basis_rows(part, where, step, core_step, bases)
        copies.append(pltpu.make_async_copy(source, base.at[pl.ds(k * 128, 128), :], base_sem.at[k]))
    for copy in copies:
        copy.start()
    for copy in copies:
        copy.wait()

    @pl.loop(0, chunk // 256)
    def _(i):
        columns = pl.ds(pl.multiple_of(i * 256, 256), 256)
        product = lax.dot_general(
            base[...], low[columns, :], (((1,), (1,)), ((), ())), preferred_element_type=F32
        )
        held[:, columns] = (8.0 * product).astype(BF)

    stores = [
        pltpu.make_async_copy(held.at[pl.ds(k * 128, 128), :], outs[k], out_sem.at[k]) for k in range(8)
    ]
    for copy in stores:
        copy.start()
    for copy in stores:
        copy.wait()


def update_blocks(part, where, arrays, bases):
    chunk = part[3]
    return pl.pallas_call(
        functools.partial(update_kernel, part, len(bases)),
        out_shape=[jax.ShapeDtypeStruct((128, chunk), BF)] * 8,
        in_specs=[SMEM] + [ANY] * (4 + len(bases)),
        out_specs=[ANY] * 8,
        scratch_shapes=[
            pltpu.VMEM((chunk, 512), BF),
            pltpu.VMEM((1024, 512), BF),
            pltpu.VMEM((1024, chunk), BF),
            DMA((4, 4)),
            DMA((8,)),
            DMA((8,)),
        ],
        cost_estimate=estimate(2 * 1024 * 512 * chunk, 1024 * chunk * 2 + 1024 * 1024 + chunk * 1024),
        name="update_" + part[0],
    )(where, *arrays, *bases)


def spread(moment):
    own = moment.shape[0]
    a = moment[:, :640].reshape(own, 8, 80)
    b = moment[:, 640:1152].reshape(own, 4, 2, 64).transpose(0, 2, 1, 3).reshape(own, 8, 64)
    c = moment[:, 1152:].reshape(own, 8, 64)
    return jnp.concatenate([a, b, c], axis=-1).transpose(1, 0, 2)


def gather_back(moment):
    own = moment.shape[1]
    moment = moment.transpose(1, 0, 2)
    a = moment[:, :, :80].reshape(own, 640)
    b = moment[:, :, 80:144].reshape(own, 2, 4, 64).transpose(0, 2, 1, 3).reshape(own, 512)
    c = moment[:, :, 144:].reshape(own, 512)
    return jnp.concatenate([a, b, c], axis=-1)


def body(grad, basis_new, basis_old, moment_first, moment_second):
    xl, z, y, xh, core = (lax.axis_index(name).astype(jnp.int32) for name in NAMES)
    spot = lax.broadcasted_iota(jnp.int32, (8,), 0)
    where = jnp.zeros((8,), jnp.int32)
    for i, value in enumerate((xh * 2 + xl, y, z, core, xh)):
        where = jnp.where(spot == i, value, where)

    packed = [pack(part, where, grad) for part in PARTS]
    arrived = [
        [blocks[0]] + [shift(block, part[0], *offset) for block, offset in zip(blocks[1:], OFFSETS[1:])]
        for part, blocks in zip(PARTS, packed)
    ]
    by_z = lax.dynamic_slice_in_dim(basis_new, (y * 2 + xh) * 256, 256, 0)
    by_x = lax.dynamic_slice_in_dim(basis_new, y * 512, 512, 0)
    bases = [
        [basis_new],
        [by_z] + [shift(by_z, "z", 4 - step) for step in range(1, 4)],
        [basis_new, lax.ppermute(by_x, "xl", [(0, 1), (1, 0)])],
    ]
    moments = lax.all_to_all(
        jnp.stack([spread(moment_first), spread(moment_second)], axis=1).astype(BF), ROW, 0, 0, tiled=True
    )
    one, two = moments[:, 0].reshape(512, 208), moments[:, 1].reshape(512, 208)
    margin = lax.psum(jnp.dot(basis_new.T, basis_old, preferred_element_type=F32), ROW)

    sums = []
    for part, blocks, base in zip(PARTS, arrived, bases):
        partial = project(part, where, blocks, base)
        halves = [partial[0]] + [shift(partial[j], part[1], j) for j in range(1, 4)]
        rest = add_up(part, where, halves)
        sums += [rest[0]] + [shift(rest[j], part[2], j) for j in range(1, 4)]

    *lows, first_new, second_new = take_step(sums, margin, one, two)

    sent = []
    for part, low, base in zip(PARTS, lows, bases):
        quarter = join(part, where, [low] + [shift(low, part[2], j) for j in range(1, 4)])
        whole = [quarter] + [shift(quarter, part[1], j) for j in range(1, 4)]
        blocks = update_blocks(part, where, whole, base)
        sent.append(
            [blocks[0]] + [shift(block, part[0], *offset) for block, offset in zip(blocks[1:], OFFSETS[1:])]
        )
    update = None
    for part, blocks in zip(PARTS, sent):
        update = unpack(part, where, blocks, update, grad.shape[1])

    new = jnp.stack([first_new.T.reshape(8, 64, 208), second_new.T.reshape(8, 64, 208)], axis=1)
    new = lax.all_to_all(new.astype(BF), ROW, 0, 0, tiled=True).astype(F32)
    return update, gather_back(new[:, 0]), gather_back(new[:, 1])


def solution(mesh):
    fine = Mesh(mesh.devices.reshape(2, 4, 4, 2, 2), NAMES)
    col = ("y", "xh", "core")
    placed = (P(NAMES, None), P(ROW, None), P(ROW, None), P(ROW, col), P(ROW, col))
    return jax.shard_map(
        body,
        mesh=fine,
        in_specs=placed,
        out_specs=(P(NAMES, None), P(ROW, col), P(ROW, col)),
        check_vma=False,
    )
```

```python
import functools

import jax
import jax.numpy as jnp
from jax import lax
from jax.experimental import pallas as pl
from jax.experimental.pallas import tpu as pltpu
from jax.sharding import Mesh, PartitionSpec as P

STEP = 10
BF, F32 = jnp.bfloat16, jnp.float32
NAMES = ("xl", "z", "y", "xh", "core")
ROW = ("xl", "z")
ANY = pl.BlockSpec(memory_space=pl.ANY)
SMEM = pl.BlockSpec(memory_space=pltpu.SMEM)
VMEM = pl.BlockSpec(memory_space=pltpu.VMEM)
DMA = pltpu.SemaphoreType.DMA
STEPS = (0, 2, 1, 3)
PARTS = (("y", "x", "z", 1280, 80), ("z", "y", "x", 1024, 64), ("x", "z", "y", 1024, 64))
SLOT = {"x": 0, "y": 1, "z": 2, "core": 3, "xh": 4}


def place(where, axis):
    return where[SLOT[axis]]


def chip_runs(ring, at):
    return runs(ring, at, 0) + runs(ring, at, 1)


def runs(ring, at, core):
    if ring == "y":
        return [((at * 4 + xh * 2 + core) * 13, 5) for xh in range(2)]
    if ring == "z":
        return [((y * 4 + xh * 2 + core) * 13 + 5 + at, 1) for y in range(4) for xh in range(2)]
    xh, xl = at // 2, at % 2
    return [((y * 4 + xh * 2 + core) * 13 + 9 + 2 * xl, 2) for y in range(4)]


def pieces(part, u_at):
    ring, _, _, chunk, piece = part
    if ring == "x":
        return [(v * 4 * piece + u_at * piece, piece) for v in range(4)]
    return [(u_at * (chunk // 4), chunk // 4)]


def shift(array, ring, step):
    if ring == "core":
        return lax.ppermute(array, "core", [(0, 1), (1, 0)])
    if ring == "x":
        axes, spots = ("xl", "xh"), [(xh * 2 + xl) for xl in range(2) for xh in range(2)]
    else:
        axes, spots = (ring,), list(range(4))
    number = {spot: i for i, spot in enumerate(spots)}
    return lax.ppermute(array, axes, [(i, number[(spot + step) % 4]) for i, spot in enumerate(spots)])


def tiles(first, count):
    return pl.ds(pl.multiple_of(first * 128, 128), count * 128)


def rows_at(first, count):
    return pl.ds(pl.multiple_of(first, 16), count)


def estimate(flops, size):
    return pl.CostEstimate(flops=flops, bytes_accessed=size, transcendentals=0)


def pack_kernel(part, where, grad, *refs):
    outs, held, in_sem, out_sem = refs[:4], refs[4], refs[5], refs[6]
    ring = part[0]
    t = place(where, ring)
    loads = []
    for k, step in enumerate(STEPS):
        done, mine = 0, []
        for j, (first, count) in enumerate(chip_runs(ring, (t + step) % 4)):
            copy = pltpu.make_async_copy(
                grad.at[:, tiles(first, count)], held.at[k, :, pl.ds(done, count * 128)], in_sem.at[k, j]
            )
            copy.start()
            mine.append(copy)
            done += count * 128
        loads.append(mine)
    stores = []
    for k in range(4):
        for copy in loads[k]:
            copy.wait()
        copy = pltpu.make_async_copy(held.at[k], outs[k], out_sem.at[k])
        copy.start()
        stores.append(copy)
    for copy in stores:
        copy.wait()


def pack(part, where, grad):
    chunk = part[3]
    return pl.pallas_call(
        functools.partial(pack_kernel, part),
        out_shape=[jax.ShapeDtypeStruct((128, 2 * chunk), BF)] * 4,
        in_specs=[SMEM, ANY],
        out_specs=[ANY] * 4,
        scratch_shapes=[pltpu.VMEM((4, 128, 2 * chunk), BF), DMA((4, 16)), DMA((4,))],
        cost_estimate=estimate(0, 8 * 128 * chunk * 4),
        name="pack_" + part[0],
    )(where, grad)


def unpack_kernel(part, where, *refs):
    ring = part[0]
    blocks, (out, held, in_sem, out_sem) = refs[:4], refs[-4:]
    t = place(where, ring)
    loads = [pltpu.make_async_copy(blocks[k], held.at[k], in_sem.at[k]) for k in range(4)]
    for copy in loads:
        copy.start()
    stores = []
    for k, step in enumerate(STEPS):
        loads[k].wait()
        done = 0
        for j, (first, count) in enumerate(chip_runs(ring, (t + 4 - step) % 4)):
            copy = pltpu.make_async_copy(
                held.at[k, :, pl.ds(done, count * 128)], out.at[:, tiles(first, count)], out_sem.at[k, j]
            )
            copy.start()
            stores.append(copy)
            done += count * 128
    for copy in stores:
        copy.wait()


def unpack(part, where, blocks, before, columns):
    chunk = part[3]
    more = [] if before is None else [before]
    return pl.pallas_call(
        functools.partial(unpack_kernel, part),
        out_shape=jax.ShapeDtypeStruct((128, columns), BF),
        in_specs=[SMEM] + [ANY] * (4 + len(more)),
        out_specs=ANY,
        scratch_shapes=[pltpu.VMEM((4, 128, 2 * chunk), BF), DMA((4,)), DMA((4, 16))],
        input_output_aliases={5: 0} if more else {},
        cost_estimate=estimate(0, 8 * 128 * chunk * 4),
        name="unpack_" + part[0],
    )(where, *blocks, *more)


def basis_rows(part, where, step, bases):
    ring = part[0]
    at = (place(where, ring) + step) % 4
    core = place(where, "core")
    if ring == "y":
        base, first = bases[0], at * 4 + place(where, "xh") * 2 + core
    elif ring == "z":
        base, first = bases[step % 4], 0
        if step % 4 == 0:
            first = place(where, "y") * 4 + place(where, "xh") * 2 + core
    elif step % 2 == 0:
        base, first = bases[0], place(where, "y") * 4 + (at // 2) * 2 + core
    else:
        base, first = bases[1], at // 2
    return base.at[pl.ds(pl.multiple_of(first * 128, 128), 128), :]


def project_kernel(part, count, own, where, *refs):
    blocks, bases, refs = refs[:4], refs[4 : 4 + count], refs[4 + count :]
    if own:
        other, outs, (held, base, total, in_sem, base_sem, other_sem, out_sem) = refs[0], refs[1:5], refs[5:]
    else:
        out, held, base, total, in_sem, base_sem, out_sem = refs
    _, u, _, chunk, _ = part
    core = place(where, "core")
    columns = tiles((core if own else 1 - core) * (chunk // 128), chunk // 128)
    copies = []
    for k, step in enumerate(STEPS):
        rows = pl.ds(k * 128, 128)
        copies.append(pltpu.make_async_copy(blocks[k].at[:, columns], held.at[rows, :], in_sem.at[k]))
        source = basis_rows(part, where, 4 - step, bases)
        copies.append(pltpu.make_async_copy(source, base.at[rows, :], base_sem.at[k]))
    if own:
        copies.append(pltpu.make_async_copy(other, total, other_sem))
    for copy in copies:
        copy.start()
    for copy in copies:
        copy.wait()

    @pl.loop(0, chunk // 256)
    def _(i):
        some = pl.ds(pl.multiple_of(i * 256, 256), 256)
        product = lax.dot_general(held[:, some], base[...], (((0,), (0,)), ((), ())), preferred_element_type=F32)
        if own:
            product = product + total[some, :].astype(F32)
        total[some, :] = product.astype(BF)

    if not own:
        copy = pltpu.make_async_copy(total, out, out_sem)
        copy.start()
        copy.wait()
        return
    stores = []
    for j in range(4):
        done = 0
        for i, (first, size) in enumerate(pieces(part, (place(where, u) + j) % 4)):
            copy = pltpu.make_async_copy(
                total.at[rows_at(first, size), :], outs[j].at[pl.ds(done, size), :], out_sem.at[j, i]
            )
            copy.start()
            stores.append(copy)
            done += size
    for copy in stores:
        copy.wait()


def project(part, where, blocks, bases, other=None):
    chunk = part[3]
    own = other is not None
    shapes = [jax.ShapeDtypeStruct((chunk // 4, 512), BF)] * 4 if own else jax.ShapeDtypeStruct((chunk, 512), BF)
    return pl.pallas_call(
        functools.partial(project_kernel, part, len(bases), own),
        out_shape=shapes,
        in_specs=[SMEM] + [ANY] * (4 + len(bases) + own),
        out_specs=[ANY] * 4 if own else ANY,
        scratch_shapes=[
            pltpu.VMEM((512, chunk), BF),
            pltpu.VMEM((512, 512), BF),
            pltpu.VMEM((chunk, 512), BF),
            DMA((4,)),
            DMA((4,)),
        ]
        + ([DMA, DMA((4, 4))] if own else [DMA]),
        cost_estimate=estimate(2 * 512 * 512 * chunk, 512 * chunk * 2 + 512 * 1024 + chunk * 1024),
        name=("project_own_" if own else "project_other_") + part[0],
    )(where, *blocks, *bases, *([other] if own else []))


def add_kernel(part, where, a, b, c, d, *refs):
    outs, total = refs[:4], refs[4]
    _, _, v, _, piece = part
    total[...] = (
        (a[...].astype(F32) + b[...].astype(F32)) + (c[...].astype(F32) + d[...].astype(F32))
    ).astype(BF)
    for j in range(4):
        at = (place(where, v) + j) % 4
        outs[j][...] = total[rows_at(at * piece, piece), :]


def add_up(part, where, arrays):
    _, _, _, chunk, piece = part
    return pl.pallas_call(
        functools.partial(add_kernel, part),
        out_shape=[jax.ShapeDtypeStruct((piece, 512), BF)] * 4,
        in_specs=[SMEM] + [VMEM] * 4,
        out_specs=[VMEM] * 4,
        scratch_shapes=[pltpu.VMEM((chunk // 4, 512), BF)],
        cost_estimate=estimate(3 * chunk * 128, 5 * chunk * 256),
        name="add_" + part[0],
    )(where, *arrays)


def step_kernel(where, *refs):
    sums, (own, other, one, two), lows = refs[:12], refs[12:16], refs[16:19]
    first_out, second_out, margin = refs[19:]
    core = place(where, "core")
    margin[rows_at(core * 256, 256), :] = own[...]
    margin[rows_at(256 - core * 256, 256), :] = other[...]
    projected = jnp.concatenate(
        [sum(ref[...].astype(F32) for ref in sums[4 * p : 4 * p + 4]) for p in range(3)], axis=0
    )
    contract = (((0,), (1,)), ((), ()))
    rotated_one = lax.dot_general(one[...], margin[...], contract, preferred_element_type=F32)
    wide = margin[...].astype(F32)
    rotated_two = lax.dot_general(two[...], (wide * wide).astype(BF), contract, preferred_element_type=F32)
    first_new = 0.9 * rotated_one + 0.1 * projected
    second_new = 0.999 * rotated_two + 0.001 * projected * projected
    low_step = (
        first_new / (1.0 - 0.9**STEP) / (jnp.sqrt(second_new / (1.0 - 0.999**STEP)) + 1e-08)
    ).astype(BF)
    begin = 0
    for ref in lows:
        ref[...] = low_step[begin : begin + ref.shape[0], :]
        begin += ref.shape[0]
    first_out[...] = first_new
    second_out[...] = second_new


def take_step(where, sums, *rest):
    return pl.pallas_call(
        step_kernel,
        out_shape=[jax.ShapeDtypeStruct((part[4], 512), BF) for part in PARTS]
        + [jax.ShapeDtypeStruct((208, 512), F32)] * 2,
        in_specs=[SMEM] + [VMEM] * 16,
        out_specs=[VMEM] * 5,
        scratch_shapes=[pltpu.VMEM((512, 512), BF)],
        cost_estimate=estimate(4 * 208 * 512 * 512, 4 * 2**20),
        name="step",
    )(where, *sums, *rest)


def join_kernel(part, where, *refs):
    arrays, out = refs[:4], refs[4]
    _, _, v, _, piece = part
    for j in range(4):
        at = (place(where, v) + 4 - j) % 4
        out[rows_at(at * piece, piece), :] = arrays[j][...]


def join(part, where, arrays):
    return pl.pallas_call(
        functools.partial(join_kernel, part),
        out_shape=jax.ShapeDtypeStruct((part[3] // 4, 512), BF),
        in_specs=[SMEM] + [VMEM] * 4,
        out_specs=VMEM,
        cost_estimate=estimate(0, part[3] * 512),
        name="join_" + part[0],
    )(where, *arrays)


def update_kernel(part, count, where, *refs):
    arrays, bases, outs = refs[:8], refs[8 : 8 + count], refs[8 + count : 12 + count]
    low, base, held, in_sem, base_sem, out_sem = refs[12 + count :]
    _, u, _, chunk, _ = part
    core = place(where, "core")
    copies = []
    for c in range(2):
        begin = (core if c == 0 else 1 - core) * chunk
        for j in range(4):
            done = 0
            for i, (first, size) in enumerate(pieces(part, (place(where, u) + 4 - j) % 4)):
                copies.append(
                    pltpu.make_async_copy(
                        arrays[4 * c + j].at[pl.ds(done, size), :],
                        low.at[rows_at(begin + first, size), :],
                        in_sem.at[4 * c + j, i],
                    )
                )
                done += size
    for k, step in enumerate(STEPS):
        source = basis_rows(part, where, step, bases)
        copies.append(pltpu.make_async_copy(source, base.at[pl.ds(k * 128, 128), :], base_sem.at[k]))
    for copy in copies:
        copy.start()
    for copy in copies:
        copy.wait()

    @pl.loop(0, chunk // 128)
    def _(i):
        columns = pl.ds(pl.multiple_of(i * 256, 256), 256)
        product = lax.dot_general(base[...], low[columns, :], (((1,), (1,)), ((), ())), preferred_element_type=F32)
        held[:, columns] = (8.0 * product).astype(BF)

    stores = [pltpu.make_async_copy(held.at[pl.ds(k * 128, 128), :], outs[k], out_sem.at[k]) for k in range(4)]
    for copy in stores:
        copy.start()
    for copy in stores:
        copy.wait()


def update_blocks(part, where, arrays, bases):
    chunk = part[3]
    return pl.pallas_call(
        functools.partial(update_kernel, part, len(bases)),
        out_shape=[jax.ShapeDtypeStruct((128, 2 * chunk), BF)] * 4,
        in_specs=[SMEM] + [ANY] * (8 + len(bases)),
        out_specs=[ANY] * 4,
        scratch_shapes=[
            pltpu.VMEM((2 * chunk, 512), BF),
            pltpu.VMEM((512, 512), BF),
            pltpu.VMEM((512, 2 * chunk), BF),
            DMA((8, 4)),
            DMA((4,)),
            DMA((4,)),
        ],
        cost_estimate=estimate(2 * 1024 * 512 * chunk, 1024 * chunk * 2 + 512 * 1024 + chunk * 2048),
        name="update_" + part[0],
    )(where, *arrays, *bases)


def spread(moment):
    own = moment.shape[0]
    a = moment[:, :640].reshape(own, 8, 80)
    b = moment[:, 640:1152].reshape(own, 4, 2, 64).transpose(0, 2, 1, 3).reshape(own, 8, 64)
    c = moment[:, 1152:].reshape(own, 8, 64)
    return jnp.concatenate([a, b, c], axis=-1).transpose(1, 0, 2)


def gather_back(moment):
    own = moment.shape[1]
    moment = moment.transpose(1, 0, 2)
    a = moment[:, :, :80].reshape(own, 640)
    b = moment[:, :, 80:144].reshape(own, 2, 4, 64).transpose(0, 2, 1, 3).reshape(own, 512)
    c = moment[:, :, 144:].reshape(own, 512)
    return jnp.concatenate([a, b, c], axis=-1)


def body(grad, basis_new, basis_old, moment_first, moment_second):
    xl, z, y, xh, core = (lax.axis_index(name).astype(jnp.int32) for name in NAMES)
    spot = lax.broadcasted_iota(jnp.int32, (8,), 0)
    where = jnp.zeros((8,), jnp.int32)
    for i, value in enumerate((xh * 2 + xl, y, z, core, xh)):
        where = jnp.where(spot == i, value, where)

    packed = [pack(part, where, grad) for part in PARTS]
    arrived = [
        [blocks[0]] + [shift(block, part[0], step) for block, step in zip(blocks[1:], STEPS[1:])]
        for part, blocks in zip(PARTS, packed)
    ]
    by_core = basis_new.reshape(4, 2, 2, 128, 512)
    by_x = lax.dynamic_index_in_dim(lax.dynamic_index_in_dim(by_core, core, 2, False), y, 0, False)
    by_z = lax.dynamic_index_in_dim(by_x, xh, 0, False)
    bases = [
        [basis_new],
        [basis_new] + [shift(by_z, "z", 4 - step) for step in range(1, 4)],
        [basis_new, lax.ppermute(by_x.reshape(256, 512), "xl", [(0, 1), (1, 0)])],
    ]

    half = lax.dynamic_slice_in_dim(basis_new, core * 256, 256, 1)
    margin = jnp.dot(half.T, basis_old, preferred_element_type=F32).astype(BF).reshape(8, 32, 512)
    margin = jnp.pad(margin, ((0, 0), (0, 0), (0, 112))).reshape(8, 32, 3, 208).transpose(0, 2, 1, 3)
    moments = jnp.concatenate(
        [spread(moment_first).astype(BF), spread(moment_second).astype(BF), margin.reshape(8, 96, 208)], axis=1
    )
    moments = lax.all_to_all(moments, ROW, 0, 0, tiled=True)
    one, two = moments[:, :64].reshape(512, 208), moments[:, 64:128].reshape(512, 208)
    margin = jnp.sum(moments[:, 128:].astype(F32), axis=0).astype(BF)
    margin = margin.reshape(3, 32, 208).transpose(1, 0, 2).reshape(32, 624)[:, :512]
    margin = lax.all_to_all(jnp.broadcast_to(margin, (8, 32, 512)), ROW, 0, 0, tiled=True).reshape(256, 512)
    margin_other = shift(margin, "core", 1)

    totals = []
    for part, blocks, base in zip(PARTS, arrived, bases):
        other = shift(project(part, where, blocks, base), "core", 1)
        partial = project(part, where, blocks, base, other)
        halves = [partial[0]] + [shift(partial[j], part[1], j) for j in range(1, 4)]
        rest = add_up(part, where, halves)
        totals += [rest[0]] + [shift(rest[j], part[2], j) for j in range(1, 4)]

    *lows, first_new, second_new = take_step(where, totals, margin, margin_other, one, two)

    sent = []
    for part, low, base in zip(PARTS, lows, bases):
        quarter = join(part, where, [low] + [shift(low, part[2], j) for j in range(1, 4)])
        whole = [quarter] + [shift(quarter, part[1], j) for j in range(1, 4)]
        whole = whole + [shift(array, "core", 1) for array in whole]
        blocks = update_blocks(part, where, whole, base)
        sent.append([blocks[0]] + [shift(block, part[0], step) for block, step in zip(blocks[1:], STEPS[1:])])
    update = None
    for part, blocks in zip(PARTS, sent):
        update = unpack(part, where, blocks, update, grad.shape[1])

    new = jnp.stack([first_new.T.reshape(8, 64, 208), second_new.T.reshape(8, 64, 208)], axis=1)
    new = lax.all_to_all(new.astype(BF), ROW, 0, 0, tiled=True).astype(F32)
    return update, gather_back(new[:, 0]), gather_back(new[:, 1])


def solution(mesh):
    fine = Mesh(mesh.devices.reshape(2, 4, 4, 2, 2), NAMES)
    col = ("y", "xh", "core")
    placed = (P(NAMES, None), P(ROW, None), P(ROW, None), P(ROW, col), P(ROW, col))
    return jax.shard_map(
        body,
        mesh=fine,
        in_specs=placed,
        out_specs=(P(NAMES, None), P(ROW, col), P(ROW, col)),
        check_vma=False,
    )
```

```python
import functools
import itertools

import jax
import jax.numpy as jnp
from jax import lax
from jax.experimental import pallas as pl
from jax.experimental.pallas import tpu as pltpu
from jax.sharding import Mesh, PartitionSpec as P

STEP = 10
BF, F32 = jnp.bfloat16, jnp.float32
NAMES = ("xl", "z", "y", "xh", "core")
SIZES = (2, 4, 4, 2, 2)
ROW = ("xl", "z")
ANY = pl.BlockSpec(memory_space=pl.ANY)
SMEM = pl.BlockSpec(memory_space=pltpu.SMEM)
VMEM = pl.BlockSpec(memory_space=pltpu.VMEM)
DMA = pltpu.SemaphoreType.DMA
STEPS = (0, 2, 1, 3)
WIDTH = {"y": 2048, "z": 2048, "x": 2560}
GROUPS = ((2048, 128), (1280, 80))
SLOT = {"x": 0, "y": 1, "z": 2, "core": 3, "xh": 4, "u0": 5, "v0": 6, "u1": 2, "v1": 1}
SPOTS = [dict(zip(NAMES, spot)) for spot in itertools.product(*(range(n) for n in SIZES))]


def place(where, axis):
    return where[SLOT[axis]]


def ring_shift(spot, ring, step):
    spot = dict(spot)
    if ring == "x":
        x = (spot["xh"] * 2 + spot["xl"] + step) % 4
        spot["xh"], spot["xl"] = x // 2, x % 2
    elif ring == "core":
        spot["core"] = 1 - spot["core"]
    else:
        spot[ring] = (spot[ring] + step) % 4
    return spot


def shift(array, rings, step):
    pairs = []
    for spot in SPOTS:
        target = ring_shift(spot, rings[spot["core"]], step)
        pairs.append((SPOTS.index(spot), SPOTS.index(target)))
    return lax.ppermute(array, NAMES, pairs)


RINGS = {ring: (ring, ring) for ring in ("x", "y", "z", "core")}
U = (("x", "y"), ("z", "z"))
V = (("z", "x"), ("y", "y"))


def runs(ring, at):
    out, done = [], 0
    if ring == "y":
        for xh in range(2):
            out.append((done, (at * 4 + xh * 2) * 1664, 1024))
            done += 1024
    elif ring == "z":
        for y, xh, xl in itertools.product(range(4), range(2), range(2)):
            out.append((done, (y * 4 + xh * 2 + 1) * 1664 + (xl * 4 + at) * 128, 128))
            done += 128
    else:
        xh, xl = at // 2, at % 2
        for core, y in itertools.product(range(2), range(4)):
            out.append((core * 1280 + y * 256, (y * 4 + xh * 2 + core) * 1664 + (8 + 2 * xl) * 128, 256))
    return out


def pieces(group, u_at):
    if group == 0:
        return [(u_at * 512, 512)]
    return [one for v in range(4) for one in ((v * 256 + u_at * 64, 64), (1024 + v * 64 + u_at * 16, 16))]


def rows_at(first, count):
    return pl.ds(pl.multiple_of(first, 16), count)


def estimate(flops, size):
    return pl.CostEstimate(flops=flops, bytes_accessed=size, transcendentals=0)


def start_all(copies):
    for copy in copies:
        copy.start()
    return copies


def wait_all(copies):
    for copy in copies:
        copy.wait()


def turned(tile):
    return pltpu.roll(tile.astype(F32), 64, 1).astype(BF)


def pack_kernel(ring, where, grad, *refs):
    outs, (held, in_sem, out_sem), more = refs[:4], refs[4:7], refs[7:]
    loads = [
        [
            pltpu.make_async_copy(grad.at[:, pl.ds(source, count)], held.at[at, :, pl.ds(to, count)], in_sem.at[at, j])
            for j, (to, source, count) in enumerate(runs(ring, at))
        ]
        for at in range(4)
    ]
    for copies in loads:
        start_all(copies)
    if ring == "x":
        ends, end_sem = more
        copies = start_all(
            [pltpu.make_async_copy(grad.at[:, pl.ds(b * 1664 + 1536, 128)], ends.at[b], end_sem.at[b]) for b in range(16)]
        )
        wait_all(copies)
        left = lax.broadcasted_iota(jnp.int32, (128, 128), 1) < 64
        for xh, core, pair in itertools.product(range(2), range(2), range(2)):
            one, two = (ends[(2 * pair + i) * 4 + xh * 2 + core] for i in range(2))
            columns = pl.ds(core * 1280 + 1024 + pair * 128, 128)
            held[xh * 2, :, columns] = jnp.where(left, one, turned(two))
            held[xh * 2 + 1, :, columns] = jnp.where(left, turned(one), two)
    for copies in loads:
        wait_all(copies)
    t = place(where, ring)
    wait_all(
        start_all([pltpu.make_async_copy(held.at[(t + step) % 4], outs[k], out_sem.at[k]) for k, step in enumerate(STEPS)])
    )


def pack(ring, where, grad):
    width = WIDTH[ring]
    return pl.pallas_call(
        functools.partial(pack_kernel, ring),
        out_shape=[jax.ShapeDtypeStruct((128, width), BF)] * 4,
        in_specs=[SMEM, ANY],
        out_specs=[ANY] * 4,
        scratch_shapes=[pltpu.VMEM((4, 128, width), BF), DMA((4, 16)), DMA((4,))]
        + ([pltpu.VMEM((16, 128, 128), BF), DMA((16,))] if ring == "x" else []),
        cost_estimate=estimate(0, 4 * 128 * width * 4),
        name="pack_" + ring,
    )(where, grad)


def unpack_kernel(ring, where, *refs):
    blocks = refs[:4]
    if ring == "x":
        out, held, in_sem, out_sem, ends, end_sem = refs[-6:]
    else:
        out, held, in_sem, out_sem = refs[-4:]
    t = place(where, ring)
    wait_all(
        start_all(
            [
                pltpu.make_async_copy(blocks[k], held.at[(t + 4 - step) % 4], in_sem.at[k])
                for k, step in enumerate(STEPS)
            ]
        )
    )
    stores = [
        pltpu.make_async_copy(held.at[at, :, pl.ds(to, count)], out.at[:, pl.ds(source, count)], out_sem.at[at, j])
        for at in range(4)
        for j, (to, source, count) in enumerate(runs(ring, at))
    ]
    start_all(stores)
    if ring == "x":
        left = lax.broadcasted_iota(jnp.int32, (128, 128), 1) < 64
        for xh, core, pair in itertools.product(range(2), range(2), range(2)):
            columns = pl.ds(core * 1280 + 1024 + pair * 128, 128)
            one, two = held[xh * 2, :, columns], held[xh * 2 + 1, :, columns]
            block = 2 * pair * 4 + xh * 2 + core
            ends[block] = jnp.where(left, one, turned(two))
            ends[block + 4] = jnp.where(left, turned(one), two)
        wait_all(
            start_all(
                [pltpu.make_async_copy(ends.at[b], out.at[:, pl.ds(b * 1664 + 1536, 128)], end_sem.at[b]) for b in range(16)]
            )
        )
    wait_all(stores)


def unpack(ring, where, blocks, before, columns):
    width = WIDTH[ring]
    more = [] if before is None else [before]
    return pl.pallas_call(
        functools.partial(unpack_kernel, ring),
        out_shape=jax.ShapeDtypeStruct((128, columns), BF),
        in_specs=[SMEM] + [ANY] * (4 + len(more)),
        out_specs=ANY,
        scratch_shapes=[pltpu.VMEM((4, 128, width), BF), DMA((4,)), DMA((4, 16))]
        + ([pltpu.VMEM((16, 128, 128), BF), DMA((16,))] if ring == "x" else []),
        input_output_aliases={5: 0} if more else {},
        cost_estimate=estimate(0, 4 * 128 * width * 4),
        name="unpack_" + ring,
    )(where, *blocks, *more)


def basis_rows(ring, where, step, bases):
    y, xh, core = place(where, "y"), place(where, "xh"), place(where, "core")
    base = bases[0]
    if ring == "y":
        first = ((y + step) % 4) * 4 + xh * 2 + core
    elif ring == "z":
        first = y * 4 + xh * 2 + core
        if step % 4:
            base, first = bases[step % 4], 0
    else:
        at = (place(where, "x") + step) % 4
        first = y * 4 + (at // 2) * 2 + core
        if step % 2:
            base, first = bases[4], at // 2
    return base.at[pl.ds(pl.multiple_of(first * 128, 128), 128), :]


def load_blocks(ring, where, blocks, columns, bases, held, base, in_sem, base_sem):
    copies = []
    for k, step in enumerate(STEPS):
        rows = pl.ds(k * 128, 128)
        copies.append(pltpu.make_async_copy(blocks[k].at[:, columns], held.at[rows, :], in_sem.at[k]))
        source = basis_rows(ring, where, 4 - step, bases)
        copies.append(pltpu.make_async_copy(source, base.at[rows, :], base_sem.at[k]))
    return copies


def project_kernel(group, own, where, *refs):
    count = 8 if group == 0 else 4
    blocks, bases, refs = refs[:count], refs[count : count + 5], refs[count + 5 :]
    if own:
        other, outs, (held, base, total, in_sem, base_sem, other_sem, out_sem) = refs[0], refs[1:5], refs[5:]
    else:
        out, held, base, total, in_sem, base_sem, out_sem = refs
    chunk = GROUPS[group][0]
    core = place(where, "core")
    scratch = (bases, held, base, in_sem, base_sem)
    if own:
        copy = pltpu.make_async_copy(other, total, other_sem)
        copy.start()
    if group == 0:
        on_y = core == (0 if own else 1)
        for ring, mine, chosen in (("y", blocks[:4], on_y), ("z", blocks[4:], jnp.logical_not(on_y))):

            @pl.when(chosen)
            def _():
                wait_all(start_all(load_blocks(ring, where, mine, pl.ds(0, chunk), *scratch)))

    else:
        first = (core if own else 1 - core) * chunk
        columns = pl.ds(pl.multiple_of(first, 128), chunk)
        wait_all(start_all(load_blocks("x", where, blocks, columns, *scratch)))
    if own:
        copy.wait()

    @pl.loop(0, chunk // 256)
    def _(i):
        some = pl.ds(pl.multiple_of(i * 256, 256), 256)
        product = lax.dot_general(held[:, some], base[...], (((0,), (0,)), ((), ())), preferred_element_type=F32)
        if own:
            product = product + total[some, :].astype(F32)
        total[some, :] = product.astype(BF)

    if not own:
        wait_all(start_all([pltpu.make_async_copy(total, out, out_sem)]))
        return
    stores = []
    for j in range(4):
        done = 0
        for i, (first, size) in enumerate(pieces(group, (place(where, "u%d" % group) + j) % 4)):
            stores.append(
                pltpu.make_async_copy(
                    total.at[rows_at(first, size), :], outs[j].at[pl.ds(done, size), :], out_sem.at[j, i]
                )
            )
            done += size
    wait_all(start_all(stores))


def project(group, where, blocks, bases, other=None):
    chunk = GROUPS[group][0]
    own = other is not None
    shapes = [jax.ShapeDtypeStruct((chunk // 4, 512), BF)] * 4 if own else jax.ShapeDtypeStruct((chunk, 512), BF)
    return pl.pallas_call(
        functools.partial(project_kernel, group, own),
        out_shape=shapes,
        in_specs=[SMEM] + [ANY] * (len(blocks) + len(bases) + own),
        out_specs=[ANY] * 4 if own else ANY,
        scratch_shapes=[
            pltpu.VMEM((512, chunk), BF),
            pltpu.VMEM((512, 512), BF),
            pltpu.VMEM((chunk, 512), BF),
            DMA((4,)),
            DMA((4,)),
        ]
        + ([DMA, DMA((4, 8))] if own else [DMA]),
        cost_estimate=estimate(2 * 512 * 512 * chunk, 512 * chunk * 2 + 512 * 1024 + chunk * 1024),
        name="project_%s_%d" % ("own" if own else "other", group),
    )(where, *blocks, *bases, *([other] if own else []))


def add_kernel(group, where, a, b, c, d, *refs):
    outs, total = refs[:4], refs[4]
    piece = GROUPS[group][1]
    total[...] = (
        (a[...].astype(F32) + b[...].astype(F32)) + (c[...].astype(F32) + d[...].astype(F32))
    ).astype(BF)
    for j in range(4):
        at = (place(where, "v%d" % group) + j) % 4
        outs[j][...] = total[rows_at(at * piece, piece), :]


def add_up(group, where, arrays):
    chunk, piece = GROUPS[group]
    return pl.pallas_call(
        functools.partial(add_kernel, group),
        out_shape=[jax.ShapeDtypeStruct((piece, 512), BF)] * 4,
        in_specs=[SMEM] + [VMEM] * 4,
        out_specs=[VMEM] * 4,
        scratch_shapes=[pltpu.VMEM((chunk // 4, 512), BF)],
        cost_estimate=estimate(3 * chunk * 128, 5 * chunk * 256),
        name="add_%d" % group,
    )(where, *arrays)


def step_kernel(where, *refs):
    sums, (own, other, one, one_low, two), lows = refs[:8], refs[8:13], refs[13:15]
    first_out, second_out, margin = refs[15:]
    core = place(where, "core")
    margin[rows_at(core * 256, 256), :] = own[...]
    margin[rows_at(256 - core * 256, 256), :] = other[...]
    projected = jnp.concatenate(
        [sum(ref[...].astype(F32) for ref in sums[4 * g : 4 * g + 4]) for g in range(2)], axis=0
    )
    contract = (((0,), (1,)), ((), ()))
    rotated_one = lax.dot_general(one[...], margin[...], contract, preferred_element_type=F32)
    rotated_one = rotated_one + lax.dot_general(one_low[...], margin[...], contract, preferred_element_type=F32)
    wide = margin[...].astype(F32)
    rotated_two = lax.dot_general(two[...], (wide * wide).astype(BF), contract, preferred_element_type=F32)
    first_new = 0.9 * rotated_one + 0.1 * projected
    second_new = 0.999 * rotated_two + 0.001 * projected * projected
    low_step = (
        first_new / (1.0 - 0.9**STEP) / (jnp.sqrt(second_new / (1.0 - 0.999**STEP)) + 1e-08)
    ).astype(BF)
    begin = 0
    for ref in lows:
        ref[...] = low_step[begin : begin + ref.shape[0], :]
        begin += ref.shape[0]
    first_out[...] = first_new
    second_out[...] = second_new


def take_step(where, sums, *rest):
    return pl.pallas_call(
        step_kernel,
        out_shape=[jax.ShapeDtypeStruct((piece, 512), BF) for _, piece in GROUPS]
        + [jax.ShapeDtypeStruct((208, 512), F32)] * 2,
        in_specs=[SMEM] + [VMEM] * 13,
        out_specs=[VMEM] * 4,
        scratch_shapes=[pltpu.VMEM((512, 512), BF)],
        cost_estimate=estimate(6 * 208 * 512 * 512, 4 * 2**20),
        name="step",
    )(where, *sums, *rest)


def join_kernel(group, where, *refs):
    arrays, out = refs[:4], refs[4]
    piece = GROUPS[group][1]
    for j in range(4):
        at = (place(where, "v%d" % group) + 4 - j) % 4
        out[rows_at(at * piece, piece), :] = arrays[j][...]


def join(group, where, arrays):
    chunk = GROUPS[group][0]
    return pl.pallas_call(
        functools.partial(join_kernel, group),
        out_shape=jax.ShapeDtypeStruct((chunk // 4, 512), BF),
        in_specs=[SMEM] + [VMEM] * 4,
        out_specs=VMEM,
        cost_estimate=estimate(0, chunk * 512),
        name="join_%d" % group,
    )(where, *arrays)


def low_copies(group, where, arrays, begin, low, in_sem, core_of_arrays):
    if group == 0:
        u = jnp.where(core_of_arrays == 0, place(where, "x"), place(where, "y"))
    else:
        u = place(where, "u1")
    copies = []
    for j in range(4):
        done = 0
        for i, (first, size) in enumerate(pieces(group, (u + 4 - j) % 4)):
            copies.append(
                pltpu.make_async_copy(
                    arrays[j].at[pl.ds(done, size), :], low.at[rows_at(begin + first, size), :], in_sem.at[j, i]
                )
            )
            done += size
    return copies


def update_kernel(ring, where, *refs):
    own, other, bases, outs = refs[:4], refs[4:8], refs[8:13], refs[13:17]
    low, base, held, in_sem, other_sem, base_sem, out_sem = refs[17:]
    core = place(where, "core")
    width = WIDTH[ring]
    copies = []
    for k, step in enumerate(STEPS):
        source = basis_rows(ring, where, step, bases)
        copies.append(pltpu.make_async_copy(source, base.at[pl.ds(k * 128, 128), :], base_sem.at[k]))
    start_all(copies)
    if ring == "x":
        more = low_copies(1, where, own, core * 1280, low, in_sem, core)
        more += low_copies(1, where, other, (1 - core) * 1280, low, other_sem, 1 - core)
        wait_all(start_all(more))
    else:
        part_core = 0 if ring == "y" else 1
        for arrays, chosen in ((own, core == part_core), (other, core != part_core)):

            @pl.when(chosen)
            def _():
                wait_all(start_all(low_copies(0, where, arrays, 0, low, in_sem, jnp.int32(part_core))))

    wait_all(copies)

    @pl.loop(0, width // 256)
    def _(i):
        columns = pl.ds(pl.multiple_of(i * 256, 256), 256)
        product = lax.dot_general(base[...], low[columns, :], (((1,), (1,)), ((), ())), preferred_element_type=F32)
        held[:, columns] = (8.0 * product).astype(BF)

    wait_all(
        start_all([pltpu.make_async_copy(held.at[pl.ds(k * 128, 128), :], outs[k], out_sem.at[k]) for k in range(4)])
    )


def update_blocks(ring, where, arrays, bases):
    width = WIDTH[ring]
    return pl.pallas_call(
        functools.partial(update_kernel, ring),
        out_shape=[jax.ShapeDtypeStruct((128, width), BF)] * 4,
        in_specs=[SMEM] + [ANY] * (8 + len(bases)),
        out_specs=[ANY] * 4,
        scratch_shapes=[
            pltpu.VMEM((width, 512), BF),
            pltpu.VMEM((512, 512), BF),
            pltpu.VMEM((512, width), BF),
            DMA((4, 8)),
            DMA((4, 8)),
            DMA((4,)),
            DMA((4,)),
        ],
        cost_estimate=estimate(2 * 512 * 512 * width, 512 * width * 2 + 512 * 1024 + width * 1024),
        name="update_" + ring,
    )(where, *arrays, *bases)


def spread(moment):
    own = moment.shape[0]
    parts = [moment[:, :1024].reshape(own, 8, 128), moment[:, 1024:1536].reshape(own, 8, 64), moment[:, 1536:].reshape(own, 8, 16)]
    return jnp.concatenate(parts, axis=-1).transpose(1, 0, 2)


def gather_back(moment):
    own = moment.shape[1]
    moment = moment.transpose(1, 0, 2)
    parts = [moment[:, :, :128].reshape(own, 1024), moment[:, :, 128:192].reshape(own, 512), moment[:, :, 192:].reshape(own, 128)]
    return jnp.concatenate(parts, axis=-1)


def exchange(blocks, rings):
    return [blocks[0]] + [shift(block, rings, step) for block, step in zip(blocks[1:], STEPS[1:])]


def body(grad, basis_new, basis_old, moment_first, moment_second):
    xl, z, y, xh, core = (lax.axis_index(name).astype(jnp.int32) for name in NAMES)
    x = xh * 2 + xl
    spot = lax.broadcasted_iota(jnp.int32, (8,), 0)
    where = jnp.zeros((8,), jnp.int32)
    for i, value in enumerate((x, y, z, core, xh, jnp.where(core == 0, x, y), jnp.where(core == 0, z, x))):
        where = jnp.where(spot == i, value, where)

    arrived = {}
    for ring in ("x", "y", "z"):
        arrived[ring] = exchange(pack(ring, where, grad), RINGS[ring])
    by_core = basis_new.reshape(4, 2, 2, 128, 512)
    by_x = lax.dynamic_index_in_dim(lax.dynamic_index_in_dim(by_core, core, 2, False), y, 0, False)
    by_z = lax.dynamic_index_in_dim(by_x, xh, 0, False)
    bases = [basis_new] + [shift(by_z, RINGS["z"], 4 - step) for step in range(1, 4)]
    bases.append(lax.ppermute(by_x.reshape(256, 512), "xl", [(0, 1), (1, 0)]))

    half = lax.dynamic_slice_in_dim(basis_new, core * 256, 256, 1)
    margin = jnp.dot(half.T, basis_old, preferred_element_type=F32).astype(BF).reshape(8, 32, 512)
    margin = jnp.pad(margin, ((0, 0), (0, 0), (0, 112))).reshape(8, 32, 3, 208).transpose(0, 2, 1, 3)
    first = spread(moment_first)
    first_high = first.astype(BF)
    first_low = (first - first_high.astype(F32)).astype(BF)
    moments = jnp.concatenate(
        [first_high, first_low, spread(moment_second).astype(BF), margin.reshape(8, 96, 208)], axis=1
    )
    moments = lax.all_to_all(moments, ROW, 0, 0, tiled=True)
    one, one_low, two = (moments[:, i * 64 : i * 64 + 64].reshape(512, 208) for i in range(3))
    margin = jnp.sum(moments[:, 192:].astype(F32), axis=0).astype(BF)
    margin = margin.reshape(3, 32, 208).transpose(1, 0, 2).reshape(32, 624)[:, :512]
    margin = lax.all_to_all(jnp.broadcast_to(margin, (8, 32, 512)), ROW, 0, 0, tiled=True).reshape(256, 512)
    margin_other = shift(margin, RINGS["core"], 1)

    totals = {}
    for group, blocks in ((1, arrived["x"]), (0, arrived["y"] + arrived["z"])):
        other = shift(project(group, where, blocks, bases), RINGS["core"], 1)
        partial = project(group, where, blocks, bases, other)
        halves = [partial[0]] + [shift(partial[j], U[group], j) for j in range(1, 4)]
        rest = add_up(group, where, halves)
        totals[group] = [rest[0]] + [shift(rest[j], V[group], j) for j in range(1, 4)]

    *lows, first_new, second_new = take_step(
        where, totals[0] + totals[1], margin, margin_other, one, one_low, two
    )

    sent = {}
    for group, rings in ((1, ("x",)), (0, ("y", "z"))):
        low = lows[group]
        quarter = join(group, where, [low] + [shift(low, V[group], j) for j in range(1, 4)])
        whole = [quarter] + [shift(quarter, U[group], j) for j in range(1, 4)]
        whole = whole + [shift(array, RINGS["core"], 1) for array in whole]
        for ring in rings:
            sent[ring] = exchange(update_blocks(ring, where, whole, bases), RINGS[ring])
    update = None
    for ring in ("x", "y", "z"):
        update = unpack(ring, where, sent[ring], update, grad.shape[1])

    new = jnp.stack([first_new.T.reshape(8, 64, 208), second_new.T.reshape(8, 64, 208)], axis=1)
    new = lax.all_to_all(new.astype(BF), ROW, 0, 0, tiled=True).astype(F32)
    return update, gather_back(new[:, 0]), gather_back(new[:, 1])


def solution(mesh):
    fine = Mesh(mesh.devices.reshape(SIZES), NAMES)
    col = ("y", "xh", "core")
    placed = (P(NAMES, None), P(ROW, None), P(ROW, None), P(ROW, col), P(ROW, col))
    return jax.shard_map(
        body,
        mesh=fine,
        in_specs=placed,
        out_specs=(P(NAMES, None), P(ROW, col), P(ROW, col)),
        check_vma=False,
    )
```

```python
import functools
import itertools

import jax
import jax.numpy as jnp
from jax import lax
from jax.experimental import pallas as pl
from jax.experimental.pallas import tpu as pltpu
from jax.sharding import Mesh, PartitionSpec as P


STEP = 10
BF, F32 = jnp.bfloat16, jnp.float32
NAMES = ("xl", "z", "y", "xh", "core")
SIZES = (2, 4, 4, 2, 2)
ROW = ("xl", "z")
ANY = pl.BlockSpec(memory_space=pl.ANY)
SMEM = pl.BlockSpec(memory_space=pltpu.SMEM)
VMEM = pl.BlockSpec(memory_space=pltpu.VMEM)
DMA = pltpu.SemaphoreType.DMA
STEPS = (0, 2, 1, 3)
WIDTH = {"y": 2048, "z": 2048, "x": 2560}
GROUPS = ((2048, 128), (1280, 80))
TILE = (512, 640)
SLOT = {"x": 0, "y": 1, "z": 2, "core": 3, "xh": 4, "u0": 5, "v0": 6, "u1": 2, "v1": 1}
SPOTS = [dict(zip(NAMES, spot)) for spot in itertools.product(*(range(n) for n in SIZES))]


def place(where, axis):
    return where[SLOT[axis]]


def ring_shift(spot, ring, step):
    spot = dict(spot)
    if ring == "x":
        x = (spot["xh"] * 2 + spot["xl"] + step) % 4
        spot["xh"], spot["xl"] = x // 2, x % 2
    elif ring == "core":
        spot["core"] = 1 - spot["core"]
    else:
        spot[ring] = (spot[ring] + step) % 4
    return spot


def shift(array, rings, step):
    pairs = []
    for spot in SPOTS:
        target = ring_shift(spot, rings[spot["core"]], step)
        pairs.append((SPOTS.index(spot), SPOTS.index(target)))
    return lax.ppermute(array, NAMES, pairs)


RINGS = {ring: (ring, ring) for ring in ("x", "y", "z", "core")}
U = (("x", "y"), ("z", "z"))
V = (("z", "x"), ("y", "y"))


def runs(ring, at):
    out, done = [], 0
    if ring == "y":
        for xh in range(2):
            out.append((done, (at * 4 + xh * 2) * 1664, 1024))
            done += 1024
    elif ring == "z":
        for y, xh, xl in itertools.product(range(4), range(2), range(2)):
            out.append((done, (y * 4 + xh * 2 + 1) * 1664 + (xl * 4 + at) * 128, 128))
            done += 128
    else:
        xh, xl = at // 2, at % 2
        for core, y in itertools.product(range(2), range(4)):
            out.append((core * 1280 + y * 256, (y * 4 + xh * 2 + core) * 1664 + (8 + 2 * xl) * 128, 256))
    return out


def pieces(group, u_at):
    if group == 0:
        return [(u_at * 512, 512)]
    return [one for v in range(4) for one in ((v * 256 + u_at * 64, 64), (1024 + v * 64 + u_at * 16, 16))]


def rows_at(first, count):
    return pl.ds(pl.multiple_of(first, 16), count)


def estimate(flops, size):
    return pl.CostEstimate(flops=flops, bytes_accessed=size, transcendentals=0)


def start_all(copies):
    for copy in copies:
        copy.start()
    return copies


def wait_all(copies):
    for copy in copies:
        copy.wait()


def turned(tile):
    return pltpu.roll(tile.astype(F32), 64, 1).astype(BF)


def pack_kernel(ring, where, grad, *refs):
    outs, (held, in_sem, out_sem), more = refs[:4], refs[4:7], refs[7:]
    loads = [
        [
            pltpu.make_async_copy(grad.at[:, pl.ds(source, count)], held.at[at, :, pl.ds(to, count)], in_sem.at[at, j])
            for j, (to, source, count) in enumerate(runs(ring, at))
        ]
        for at in range(4)
    ]
    for copies in loads:
        start_all(copies)
    if ring == "x":
        ends, end_sem = more
        copies = start_all(
            [pltpu.make_async_copy(grad.at[:, pl.ds(b * 1664 + 1536, 128)], ends.at[b], end_sem.at[b]) for b in range(16)]
        )
        wait_all(copies)
        left = lax.broadcasted_iota(jnp.int32, (128, 128), 1) < 64
        for xh, core, pair in itertools.product(range(2), range(2), range(2)):
            one, two = (ends[(2 * pair + i) * 4 + xh * 2 + core] for i in range(2))
            columns = pl.ds(core * 1280 + 1024 + pair * 128, 128)
            held[xh * 2, :, columns] = jnp.where(left, one, turned(two))
            held[xh * 2 + 1, :, columns] = jnp.where(left, turned(one), two)
    for copies in loads:
        wait_all(copies)
    t = place(where, ring)
    wait_all(
        start_all([pltpu.make_async_copy(held.at[(t + step) % 4], outs[k], out_sem.at[k]) for k, step in enumerate(STEPS)])
    )


def pack(ring, where, grad):
    width = WIDTH[ring]
    return pl.pallas_call(
        functools.partial(pack_kernel, ring),
        out_shape=[jax.ShapeDtypeStruct((128, width), BF)] * 4,
        in_specs=[SMEM, ANY],
        out_specs=[ANY] * 4,
        scratch_shapes=[pltpu.VMEM((4, 128, width), BF), DMA((4, 16)), DMA((4,))]
        + ([pltpu.VMEM((16, 128, 128), BF), DMA((16,))] if ring == "x" else []),
        cost_estimate=estimate(0, 4 * 128 * width * 4),
    )(where, grad)


def unpack_kernel(ring, where, *refs):
    blocks = refs[:4]
    if ring == "x":
        out, held, in_sem, out_sem, ends, end_sem = refs[-6:]
    else:
        out, held, in_sem, out_sem = refs[-4:]
    t = place(where, ring)
    wait_all(
        start_all(
            [
                pltpu.make_async_copy(blocks[k], held.at[(t + 4 - step) % 4], in_sem.at[k])
                for k, step in enumerate(STEPS)
            ]
        )
    )
    stores = [
        pltpu.make_async_copy(held.at[at, :, pl.ds(to, count)], out.at[:, pl.ds(source, count)], out_sem.at[at, j])
        for at in range(4)
        for j, (to, source, count) in enumerate(runs(ring, at))
    ]
    start_all(stores)
    if ring == "x":
        left = lax.broadcasted_iota(jnp.int32, (128, 128), 1) < 64
        for xh, core, pair in itertools.product(range(2), range(2), range(2)):
            columns = pl.ds(core * 1280 + 1024 + pair * 128, 128)
            one, two = held[xh * 2, :, columns], held[xh * 2 + 1, :, columns]
            block = 2 * pair * 4 + xh * 2 + core
            ends[block] = jnp.where(left, one, turned(two))
            ends[block + 4] = jnp.where(left, turned(one), two)
        wait_all(
            start_all(
                [pltpu.make_async_copy(ends.at[b], out.at[:, pl.ds(b * 1664 + 1536, 128)], end_sem.at[b]) for b in range(16)]
            )
        )
    wait_all(stores)


def unpack(ring, where, blocks, before, columns):
    width = WIDTH[ring]
    more = [] if before is None else [before]
    return pl.pallas_call(
        functools.partial(unpack_kernel, ring),
        out_shape=jax.ShapeDtypeStruct((128, columns), BF),
        in_specs=[SMEM] + [ANY] * (4 + len(more)),
        out_specs=ANY,
        scratch_shapes=[pltpu.VMEM((4, 128, width), BF), DMA((4,)), DMA((4, 16))]
        + ([pltpu.VMEM((16, 128, 128), BF), DMA((16,))] if ring == "x" else []),
        input_output_aliases={5: 0} if more else {},
        cost_estimate=estimate(0, 4 * 128 * width * 4),
    )(where, *blocks, *more)


def basis_rows(ring, where, step, bases):
    y, xh, core = place(where, "y"), place(where, "xh"), place(where, "core")
    base = bases[0]
    if ring == "y":
        first = ((y + step) % 4) * 4 + xh * 2 + core
    elif ring == "z":
        first = y * 4 + xh * 2 + core
        if step % 4:
            base, first = bases[step % 4], 0
    else:
        at = (place(where, "x") + step) % 4
        first = y * 4 + (at // 2) * 2 + core
        if step % 2:
            base, first = bases[4], at // 2
    return base.at[pl.ds(pl.multiple_of(first * 128, 128), 128), :]


def load_blocks(ring, where, blocks, columns, bases, held, base, in_sem, base_sem):
    copies = []
    for k, step in enumerate(STEPS):
        rows = pl.ds(k * 128, 128)
        copies.append(pltpu.make_async_copy(blocks[k].at[:, columns], held.at[rows, :], in_sem.at[k]))
        source = basis_rows(ring, where, 4 - step, bases)
        copies.append(pltpu.make_async_copy(source, base.at[rows, :], base_sem.at[k]))
    return copies


def project_kernel(group, own, where, *refs):
    count = 8 if group == 0 else 4
    blocks, bases, refs = refs[:count], refs[count : count + 5], refs[count + 5 :]
    if own:
        other, outs, (held, base, total, in_sem, base_sem, other_sem, out_sem) = refs[0], refs[1:5], refs[5:]
    else:
        out, held, base, total, in_sem, base_sem, out_sem = refs
    chunk = GROUPS[group][0]
    core = place(where, "core")
    scratch = (bases, held, base, in_sem, base_sem)
    if own:
        copy = pltpu.make_async_copy(other, total, other_sem)
        copy.start()
    if group == 0:
        on_y = core == (0 if own else 1)
        for ring, mine, chosen in (("y", blocks[:4], on_y), ("z", blocks[4:], jnp.logical_not(on_y))):

            @pl.when(chosen)
            def _():
                wait_all(start_all(load_blocks(ring, where, mine, pl.ds(0, chunk), *scratch)))

    else:
        first = (core if own else 1 - core) * chunk
        columns = pl.ds(pl.multiple_of(first, 128), chunk)
        wait_all(start_all(load_blocks("x", where, blocks, columns, *scratch)))
    if own:
        copy.wait()

    tile = TILE[group]

    @pl.loop(0, chunk // tile)
    def _(i):
        some = pl.ds(pl.multiple_of(i * tile, tile), tile)
        product = lax.dot_general(held[:, some], base[...], (((0,), (0,)), ((), ())), preferred_element_type=F32)
        if own:
            product = product + total[some, :].astype(F32)
        total[some, :] = product.astype(BF)

    if not own:
        wait_all(start_all([pltpu.make_async_copy(total, out, out_sem)]))
        return
    stores = []
    for j in range(4):
        done = 0
        for i, (first, size) in enumerate(pieces(group, (place(where, "u%d" % group) + j) % 4)):
            stores.append(
                pltpu.make_async_copy(
                    total.at[rows_at(first, size), :], outs[j].at[pl.ds(done, size), :], out_sem.at[j, i]
                )
            )
            done += size
    wait_all(start_all(stores))


def project(group, where, blocks, bases, other=None):
    chunk = GROUPS[group][0]
    own = other is not None
    shapes = [jax.ShapeDtypeStruct((chunk // 4, 512), BF)] * 4 if own else jax.ShapeDtypeStruct((chunk, 512), BF)
    return pl.pallas_call(
        functools.partial(project_kernel, group, own),
        out_shape=shapes,
        in_specs=[SMEM] + [ANY] * (len(blocks) + len(bases) + own),
        out_specs=[ANY] * 4 if own else ANY,
        scratch_shapes=[
            pltpu.VMEM((512, chunk), BF),
            pltpu.VMEM((512, 512), BF),
            pltpu.VMEM((chunk, 512), BF),
            DMA((4,)),
            DMA((4,)),
        ]
        + ([DMA, DMA((4, 8))] if own else [DMA]),
        cost_estimate=estimate(2 * 512 * 512 * chunk, 512 * chunk * 2 + 512 * 1024 + chunk * 1024),
    )(where, *blocks, *bases, *([other] if own else []))


def add_kernel(group, where, a, b, c, d, *refs):
    outs, total = refs[:4], refs[4]
    piece = GROUPS[group][1]
    total[...] = (
        (a[...].astype(F32) + b[...].astype(F32)) + (c[...].astype(F32) + d[...].astype(F32))
    ).astype(BF)
    for j in range(4):
        at = (place(where, "v%d" % group) + j) % 4
        outs[j][...] = total[rows_at(at * piece, piece), :]


def add_up(group, where, arrays):
    chunk, piece = GROUPS[group]
    return pl.pallas_call(
        functools.partial(add_kernel, group),
        out_shape=[jax.ShapeDtypeStruct((piece, 512), BF)] * 4,
        in_specs=[SMEM] + [VMEM] * 4,
        out_specs=[VMEM] * 4,
        scratch_shapes=[pltpu.VMEM((chunk // 4, 512), BF)],
        cost_estimate=estimate(3 * chunk * 128, 5 * chunk * 256),
    )(where, *arrays)


def step_kernel(where, *refs):
    sums, (own, other, one, one_low, two), lows = refs[:8], refs[8:13], refs[13:15]
    first_out, second_out, margin = refs[15:]
    core = place(where, "core")
    margin[rows_at(core * 256, 256), :] = own[...]
    margin[rows_at(256 - core * 256, 256), :] = other[...]
    projected = jnp.concatenate(
        [sum(ref[...].astype(F32) for ref in sums[4 * g : 4 * g + 4]) for g in range(2)], axis=0
    )
    contract = (((0,), (1,)), ((), ()))
    rotated_one = lax.dot_general(one[...], margin[...], contract, preferred_element_type=F32)
    rotated_one = rotated_one + lax.dot_general(one_low[...], margin[...], contract, preferred_element_type=F32)
    wide = margin[...].astype(F32)
    rotated_two = lax.dot_general(two[...], (wide * wide).astype(BF), contract, preferred_element_type=F32)
    first_new = 0.9 * rotated_one + 0.1 * projected
    second_new = 0.999 * rotated_two + 0.001 * projected * projected
    low_step = (
        first_new / (1.0 - 0.9**STEP) / (jnp.sqrt(second_new / (1.0 - 0.999**STEP)) + 1e-08)
    ).astype(BF)
    begin = 0
    for ref in lows:
        ref[...] = low_step[begin : begin + ref.shape[0], :]
        begin += ref.shape[0]
    first_out[...] = first_new
    second_out[...] = second_new


def take_step(where, sums, *rest):
    return pl.pallas_call(
        step_kernel,
        out_shape=[jax.ShapeDtypeStruct((piece, 512), BF) for _, piece in GROUPS]
        + [jax.ShapeDtypeStruct((208, 512), F32)] * 2,
        in_specs=[SMEM] + [VMEM] * 13,
        out_specs=[VMEM] * 4,
        scratch_shapes=[pltpu.VMEM((512, 512), BF)],
        cost_estimate=estimate(6 * 208 * 512 * 512, 4 * 2**20),
        name="step",
    )(where, *sums, *rest)


def join_kernel(group, where, *refs):
    arrays, out = refs[:4], refs[4]
    piece = GROUPS[group][1]
    for j in range(4):
        at = (place(where, "v%d" % group) + 4 - j) % 4
        out[rows_at(at * piece, piece), :] = arrays[j][...]


def join(group, where, arrays):
    chunk = GROUPS[group][0]
    return pl.pallas_call(
        functools.partial(join_kernel, group),
        out_shape=jax.ShapeDtypeStruct((chunk // 4, 512), BF),
        in_specs=[SMEM] + [VMEM] * 4,
        out_specs=VMEM,
        cost_estimate=estimate(0, chunk * 512),
    )(where, *arrays)


def low_copies(group, where, arrays, begin, low, in_sem, core_of_arrays):
    if group == 0:
        u = jnp.where(core_of_arrays == 0, place(where, "x"), place(where, "y"))
    else:
        u = place(where, "u1")
    copies = []
    for j in range(4):
        done = 0
        for i, (first, size) in enumerate(pieces(group, (u + 4 - j) % 4)):
            copies.append(
                pltpu.make_async_copy(
                    arrays[j].at[pl.ds(done, size), :], low.at[rows_at(begin + first, size), :], in_sem.at[j, i]
                )
            )
            done += size
    return copies


def update_kernel(ring, where, *refs):
    own, other, bases, outs = refs[:4], refs[4:8], refs[8:13], refs[13:17]
    low, base, held, in_sem, other_sem, base_sem, out_sem = refs[17:]
    core = place(where, "core")
    width = WIDTH[ring]
    copies = []
    for k, step in enumerate(STEPS):
        source = basis_rows(ring, where, step, bases)
        copies.append(pltpu.make_async_copy(source, base.at[pl.ds(k * 128, 128), :], base_sem.at[k]))
    start_all(copies)
    if ring == "x":
        more = low_copies(1, where, own, core * 1280, low, in_sem, core)
        more += low_copies(1, where, other, (1 - core) * 1280, low, other_sem, 1 - core)
        wait_all(start_all(more))
    else:
        part_core = 0 if ring == "y" else 1
        for arrays, chosen in ((own, core == part_core), (other, core != part_core)):

            @pl.when(chosen)
            def _():
                wait_all(start_all(low_copies(0, where, arrays, 0, low, in_sem, jnp.int32(part_core))))

    wait_all(copies)

    @pl.loop(0, width // 512)
    def _(i):
        columns = pl.ds(pl.multiple_of(i * 512, 512), 512)
        product = lax.dot_general(base[...], low[columns, :], (((1,), (1,)), ((), ())), preferred_element_type=F32)
        held[:, columns] = (8.0 * product).astype(BF)

    wait_all(
        start_all([pltpu.make_async_copy(held.at[pl.ds(k * 128, 128), :], outs[k], out_sem.at[k]) for k in range(4)])
    )


def update_blocks(ring, where, arrays, bases):
    width = WIDTH[ring]
    return pl.pallas_call(
        functools.partial(update_kernel, ring),
        out_shape=[jax.ShapeDtypeStruct((128, width), BF)] * 4,
        in_specs=[SMEM] + [ANY] * (8 + len(bases)),
        out_specs=[ANY] * 4,
        scratch_shapes=[
            pltpu.VMEM((width, 512), BF),
            pltpu.VMEM((512, 512), BF),
            pltpu.VMEM((512, width), BF),
            DMA((4, 8)),
            DMA((4, 8)),
            DMA((4,)),
            DMA((4,)),
        ],
        cost_estimate=estimate(2 * 512 * 512 * width, 512 * width * 2 + 512 * 1024 + width * 1024),
    )(where, *arrays, *bases)


def spread(moment):
    own = moment.shape[0]
    parts = [moment[:, :1024].reshape(own, 8, 128), moment[:, 1024:1536].reshape(own, 8, 64), moment[:, 1536:].reshape(own, 8, 16)]
    return jnp.concatenate(parts, axis=-1).transpose(1, 0, 2)


def gather_back(moment):
    own = moment.shape[1]
    moment = moment.transpose(1, 0, 2)
    parts = [moment[:, :, :128].reshape(own, 1024), moment[:, :, 128:192].reshape(own, 512), moment[:, :, 192:].reshape(own, 128)]
    return jnp.concatenate(parts, axis=-1)


def exchange(blocks, rings):
    return [blocks[0]] + [shift(block, rings, step) for block, step in zip(blocks[1:], STEPS[1:])]


def compute(grad, basis_new, basis_old, moment_first, moment_second):
    xl, z, y, xh, core = (lax.axis_index(name).astype(jnp.int32) for name in NAMES)
    x = xh * 2 + xl
    spot = lax.broadcasted_iota(jnp.int32, (8,), 0)
    where = jnp.zeros((8,), jnp.int32)
    for i, value in enumerate((x, y, z, core, xh, jnp.where(core == 0, x, y), jnp.where(core == 0, z, x))):
        where = jnp.where(spot == i, value, where)

    arrived = {}
    for ring in ("x", "y", "z"):
        blocks = pack(ring, where, grad)
        arrived[ring] = exchange(blocks, RINGS[ring])
    by_core = basis_new.reshape(4, 2, 2, 128, 512)
    by_x = lax.dynamic_index_in_dim(lax.dynamic_index_in_dim(by_core, core, 2, False), y, 0, False)
    by_z = lax.dynamic_index_in_dim(by_x, xh, 0, False)
    bases = [basis_new] + [shift(by_z, RINGS["z"], 4 - step) for step in range(1, 4)]
    bases.append(lax.ppermute(by_x.reshape(256, 512), "xl", [(0, 1), (1, 0)]))

    half = lax.dynamic_slice_in_dim(basis_new, core * 256, 256, 1)
    margin = jnp.dot(half.T, basis_old, preferred_element_type=F32).astype(BF).reshape(8, 32, 512)
    margin = jnp.pad(margin, ((0, 0), (0, 0), (0, 112))).reshape(8, 32, 3, 208).transpose(0, 2, 1, 3)
    first = spread(moment_first)
    first_high = first.astype(BF)
    first_low = (first - first_high.astype(F32)).astype(BF)
    moments = jnp.concatenate(
        [first_high, first_low, spread(moment_second).astype(BF), margin.reshape(8, 96, 208)], axis=1
    )
    moments = lax.all_to_all(moments, ROW, 0, 0, tiled=True)
    one, one_low, two = (moments[:, i * 64 : i * 64 + 64].reshape(512, 208) for i in range(3))
    margin = jnp.sum(moments[:, 192:].astype(F32), axis=0).astype(BF)
    margin = margin.reshape(3, 32, 208).transpose(1, 0, 2).reshape(32, 624)[:, :512]
    margin = jnp.broadcast_to(margin, (8, 32, 512))
    margin = lax.all_to_all(margin, ROW, 0, 0, tiled=True).reshape(256, 512)
    margin_other = shift(margin, RINGS["core"], 1)

    totals = {}
    for group, blocks in ((1, arrived["x"]), (0, arrived["y"] + arrived["z"])):
        other = project(group, where, blocks, bases)
        other = shift(other, RINGS["core"], 1)
        partial = project(group, where, blocks, bases, other)
        halves = [partial[0]] + [shift(partial[j], U[group], j) for j in (2, 1, 3)]
        rest = add_up(group, where, halves)
        totals[group] = [rest[0]] + [shift(rest[j], V[group], j) for j in (2, 1, 3)]

    *lows, first_new, second_new = take_step(
        where, totals[0] + totals[1], margin, margin_other, one, one_low, two
    )

    sent = {}
    for group, rings in ((1, ("x",)), (0, ("y", "z"))):
        low = lows[group]
        quarters = [low] + [shift(low, V[group], j) for j in range(1, 4)]
        quarter = join(group, where, quarters)
        whole = [quarter] + [shift(quarter, U[group], j) for j in range(1, 4)]
        whole = whole + [shift(array, RINGS["core"], 1) for array in whole]
        for ring in rings:
            blocks = update_blocks(ring, where, whole, bases)
            sent[ring] = exchange(blocks, RINGS[ring])
    update = None
    for ring in ("x", "y", "z"):
        update = unpack(ring, where, sent[ring], update, grad.shape[1])

    new = jnp.stack([first_new.T.reshape(8, 64, 208), second_new.T.reshape(8, 64, 208)], axis=1).astype(BF)
    new = lax.all_to_all(new, ROW, 0, 0, tiled=True).astype(F32)
    return update, gather_back(new[:, 0]), gather_back(new[:, 1])


def solution(mesh):
    fine = Mesh(mesh.devices.reshape(SIZES), NAMES)
    col = ("y", "xh", "core")
    placed = (P(NAMES, None), P(ROW, None), P(ROW, None), P(ROW, col), P(ROW, col))
    return jax.shard_map(
        compute,
        mesh=fine,
        in_specs=placed,
        out_specs=(P(NAMES, None), P(ROW, col), P(ROW, col)),
        check_vma=False,
    )
```

```python
import functools
import itertools

import jax
import jax.numpy as jnp
from jax import lax
from jax.experimental import pallas as pl
from jax.experimental.pallas import tpu as pltpu
from jax.sharding import Mesh, PartitionSpec as P


STEP = 10
BF, F32 = jnp.bfloat16, jnp.float32
NAMES = ("xl", "z", "y", "xh", "core")
SIZES = (2, 4, 4, 2, 2)
ROW = ("xl", "z")
ANY = pl.BlockSpec(memory_space=pl.ANY)
SMEM = pl.BlockSpec(memory_space=pltpu.SMEM)
VMEM = pl.BlockSpec(memory_space=pltpu.VMEM)
DMA = pltpu.SemaphoreType.DMA
STEPS = (0, 1, 3, 2)
WIDTH = {"y": 2048, "z": 2048, "x": 2560}
GROUPS = ((2048, 128), (1280, 80))
TILE = (512, 640)
SLOT = {"x": 0, "y": 1, "z": 2, "core": 3, "xh": 4, "u0": 5, "v0": 6, "u1": 2, "v1": 1}
SPOTS = [dict(zip(NAMES, spot)) for spot in itertools.product(*(range(n) for n in SIZES))]


def place(where, axis):
    return where[SLOT[axis]]


def ring_shift(spot, ring, step):
    spot = dict(spot)
    if ring == "x":
        x = (spot["xh"] * 2 + spot["xl"] + step) % 4
        spot["xh"], spot["xl"] = x // 2, x % 2
    elif ring == "core":
        spot["core"] = 1 - spot["core"]
    else:
        spot[ring] = (spot[ring] + step) % 4
    return spot


def shift(array, rings, step):
    pairs = []
    for spot in SPOTS:
        target = ring_shift(spot, rings[spot["core"]], step)
        pairs.append((SPOTS.index(spot), SPOTS.index(target)))
    return lax.ppermute(array, NAMES, pairs)


RINGS = {ring: (ring, ring) for ring in ("x", "y", "z", "core")}
U = (("x", "y"), ("z", "z"))
V = (("z", "x"), ("y", "y"))


def runs(ring, at):
    out, done = [], 0
    if ring == "y":
        for xh in range(2):
            out.append((done, (at * 4 + xh * 2) * 1664, 1024))
            done += 1024
    elif ring == "z":
        for y, xh, xl in itertools.product(range(4), range(2), range(2)):
            out.append((done, (y * 4 + xh * 2 + 1) * 1664 + (xl * 4 + at) * 128, 128))
            done += 128
    else:
        xh, xl = at // 2, at % 2
        for core, y in itertools.product(range(2), range(4)):
            out.append((core * 1280 + y * 256, (y * 4 + xh * 2 + core) * 1664 + (8 + 2 * xl) * 128, 256))
    return out


def pieces(group, u_at):
    if group == 0:
        return [(u_at * 512, 512)]
    return [one for v in range(4) for one in ((v * 256 + u_at * 64, 64), (1024 + v * 64 + u_at * 16, 16))]


def rows_at(first, count):
    return pl.ds(pl.multiple_of(first, 16), count)


def estimate(flops, size):
    return pl.CostEstimate(flops=flops, bytes_accessed=size, transcendentals=0)


def start_all(copies):
    for copy in copies:
        copy.start()
    return copies


def wait_all(copies):
    for copy in copies:
        copy.wait()


def wait_for(ref, sem):
    pltpu.make_async_copy(ref, ref, sem).wait()


def turned(tile):
    return pltpu.roll(tile.astype(F32), 64, 1).astype(BF)


def pack_kernel(ring, where, grad, *refs):
    outs, (held, in_sem, out_sem), more = refs[:4], refs[4:7], refs[7:]
    if ring == "x":
        ends, end_sem = more
        end_copies = start_all(
            [pltpu.make_async_copy(grad.at[:, pl.ds(b * 1664 + 1536, 128)], ends.at[b], end_sem.at[b]) for b in range(16)]
        )
    for at in range(4):
        start_all(
            [
                pltpu.make_async_copy(grad.at[:, pl.ds(source, count)], held.at[at, :, pl.ds(to, count)], in_sem.at[at])
                for to, source, count in runs(ring, at)
            ]
        )
    whole = held
    if ring == "x":
        wait_all(end_copies)
        left = lax.broadcasted_iota(jnp.int32, (128, 128), 1) < 64
        for xh, core, pair in itertools.product(range(2), range(2), range(2)):
            one, two = (ends[(2 * pair + i) * 4 + xh * 2 + core] for i in range(2))
            columns = pl.ds(core * 1280 + 1024 + pair * 128, 128)
            held[xh * 2, :, columns] = jnp.where(left, one, turned(two))
            held[xh * 2 + 1, :, columns] = jnp.where(left, turned(one), two)
        whole = held.at[:, :, pl.ds(0, 2048)]
    t = place(where, ring)
    stores = []
    for k, step in enumerate(STEPS):
        at = (t + step) % 4
        wait_for(whole.at[at], in_sem.at[at])
        copy = pltpu.make_async_copy(held.at[at], outs[k], out_sem.at[k])
        copy.start()
        stores.append(copy)
    wait_all(stores)


def pack(ring, where, grad):
    width = WIDTH[ring]
    return pl.pallas_call(
        functools.partial(pack_kernel, ring),
        out_shape=[jax.ShapeDtypeStruct((128, width), BF)] * 4,
        in_specs=[SMEM, ANY],
        out_specs=[ANY] * 4,
        scratch_shapes=[pltpu.VMEM((4, 128, width), BF), DMA((4,)), DMA((4,))]
        + ([pltpu.VMEM((16, 128, 128), BF), DMA((16,))] if ring == "x" else []),
        cost_estimate=estimate(0, 4 * 128 * width * 4),
    )(where, grad)


def unpack_kernel(ring, where, *refs):
    blocks = refs[:4]
    if ring == "x":
        out, held, in_sem, out_sem, ends, end_sem = refs[-6:]
    else:
        out, held, in_sem, out_sem = refs[-4:]
    t = place(where, ring)
    start_all(
        [
            pltpu.make_async_copy(blocks[k], held.at[(t + 4 - step) % 4], in_sem.at[(t + 4 - step) % 4])
            for k, step in enumerate(STEPS)
        ]
    )
    stores = []
    for at in range(4):
        wait_for(held.at[at], in_sem.at[at])
        stores += start_all(
            [
                pltpu.make_async_copy(held.at[at, :, pl.ds(to, count)], out.at[:, pl.ds(source, count)], out_sem.at[at, j])
                for j, (to, source, count) in enumerate(runs(ring, at))
            ]
        )
    if ring == "x":
        left = lax.broadcasted_iota(jnp.int32, (128, 128), 1) < 64
        for xh, core, pair in itertools.product(range(2), range(2), range(2)):
            columns = pl.ds(core * 1280 + 1024 + pair * 128, 128)
            one, two = held[xh * 2, :, columns], held[xh * 2 + 1, :, columns]
            block = 2 * pair * 4 + xh * 2 + core
            ends[block] = jnp.where(left, one, turned(two))
            ends[block + 4] = jnp.where(left, turned(one), two)
        stores += start_all(
            [pltpu.make_async_copy(ends.at[b], out.at[:, pl.ds(b * 1664 + 1536, 128)], end_sem.at[b]) for b in range(16)]
        )
    wait_all(stores)


def unpack(ring, where, blocks, before, columns):
    width = WIDTH[ring]
    more = [] if before is None else [before]
    return pl.pallas_call(
        functools.partial(unpack_kernel, ring),
        out_shape=jax.ShapeDtypeStruct((128, columns), BF),
        in_specs=[SMEM] + [ANY] * (4 + len(more)),
        out_specs=ANY,
        scratch_shapes=[pltpu.VMEM((4, 128, width), BF), DMA((4,)), DMA((4, 16))]
        + ([pltpu.VMEM((16, 128, 128), BF), DMA((16,))] if ring == "x" else []),
        input_output_aliases={5: 0} if more else {},
        cost_estimate=estimate(0, 4 * 128 * width * 4),
    )(where, *blocks, *more)


def basis_rows(ring, where, step, bases):
    y, xh, core = place(where, "y"), place(where, "xh"), place(where, "core")
    base = bases[0]
    if ring == "y":
        first = ((y + step) % 4) * 4 + xh * 2 + core
    elif ring == "z":
        first = y * 4 + xh * 2 + core
        if step % 4:
            base, first = bases[step % 4], 0
    else:
        at = (place(where, "x") + step) % 4
        first = y * 4 + (at // 2) * 2 + core
        if step % 2:
            base, first = bases[4], at // 2
    return base.at[pl.ds(pl.multiple_of(first * 128, 128), 128), :]


def start_blocks(ring, where, blocks, first, chunk, tile, bases, held, base, in_sem, base_sem):
    for k, step in enumerate(STEPS):
        source = basis_rows(ring, where, 4 - step, bases)
        pltpu.make_async_copy(source, base.at[pl.ds(k * 128, 128), :], base_sem).start()
    for i in range(chunk // tile):
        for k in range(4):
            columns = pl.ds(pl.multiple_of(first + i * tile, 128), tile)
            target = held.at[pl.ds(k * 128, 128), pl.ds(i * tile, tile)]
            pltpu.make_async_copy(blocks[k].at[:, columns], target, in_sem.at[i]).start()


def project_kernel(group, own, where, *refs):
    count = 8 if group == 0 else 4
    blocks, bases, refs = refs[:count], refs[count : count + 5], refs[count + 5 :]
    if own:
        other, outs, (held, base, total, in_sem, base_sem, other_sem, out_sem) = refs[0], refs[1:5], refs[5:]
    else:
        out, held, base, total, in_sem, base_sem, out_sem = refs
    chunk, tile = GROUPS[group][0], TILE[group]
    core = place(where, "core")
    scratch = (chunk, tile, bases, held, base, in_sem, base_sem)
    if group == 0:
        on_y = core == (0 if own else 1)
        for ring, mine, chosen in (("y", blocks[:4], on_y), ("z", blocks[4:], jnp.logical_not(on_y))):

            @pl.when(chosen)
            def _():
                start_blocks(ring, where, mine, 0, *scratch)

    else:
        start_blocks("x", where, blocks, (core if own else 1 - core) * chunk, *scratch)
    if own:
        copy = pltpu.make_async_copy(other, total, other_sem)
        copy.start()
        copy.wait()
    wait_for(base, base_sem)

    @pl.loop(0, chunk // tile)
    def _(i):
        some = pl.ds(pl.multiple_of(i * tile, tile), tile)
        wait_for(held.at[:, some], in_sem.at[i])
        product = lax.dot_general(held[:, some], base[...], (((0,), (0,)), ((), ())), preferred_element_type=F32)
        if own:
            product = product + total[some, :].astype(F32)
        total[some, :] = product.astype(BF)
        if not own:
            pltpu.make_async_copy(total.at[some, :], out.at[some, :], out_sem).start()

    if not own:
        wait_for(total, out_sem)
        return
    stores = []
    for j in range(4):
        done = 0
        for i, (first, size) in enumerate(pieces(group, (place(where, "u%d" % group) + j) % 4)):
            stores.append(
                pltpu.make_async_copy(
                    total.at[rows_at(first, size), :], outs[j].at[pl.ds(done, size), :], out_sem.at[j, i]
                )
            )
            done += size
    wait_all(start_all(stores))


def project(group, where, blocks, bases, other=None):
    chunk = GROUPS[group][0]
    own = other is not None
    shapes = [jax.ShapeDtypeStruct((chunk // 4, 512), BF)] * 4 if own else jax.ShapeDtypeStruct((chunk, 512), BF)
    return pl.pallas_call(
        functools.partial(project_kernel, group, own),
        out_shape=shapes,
        in_specs=[SMEM] + [ANY] * (len(blocks) + len(bases) + own),
        out_specs=[ANY] * 4 if own else ANY,
        scratch_shapes=[
            pltpu.VMEM((512, chunk), BF),
            pltpu.VMEM((512, 512), BF),
            pltpu.VMEM((chunk, 512), BF),
            DMA((4,)),
            DMA,
        ]
        + ([DMA, DMA((4, 8))] if own else [DMA]),
        cost_estimate=estimate(2 * 512 * 512 * chunk, 512 * chunk * 2 + 512 * 1024 + chunk * 1024),
    )(where, *blocks, *bases, *([other] if own else []))


def add_kernel(group, where, a, b, c, d, *refs):
    outs, total = refs[:4], refs[4]
    piece = GROUPS[group][1]
    total[...] = (
        (a[...].astype(F32) + b[...].astype(F32)) + (c[...].astype(F32) + d[...].astype(F32))
    ).astype(BF)
    for j in range(4):
        at = (place(where, "v%d" % group) + j) % 4
        outs[j][...] = total[rows_at(at * piece, piece), :]


def add_up(group, where, arrays):
    chunk, piece = GROUPS[group]
    return pl.pallas_call(
        functools.partial(add_kernel, group),
        out_shape=[jax.ShapeDtypeStruct((piece, 512), BF)] * 4,
        in_specs=[SMEM] + [VMEM] * 4,
        out_specs=[VMEM] * 4,
        scratch_shapes=[pltpu.VMEM((chunk // 4, 512), BF)],
        cost_estimate=estimate(3 * chunk * 128, 5 * chunk * 256),
    )(where, *arrays)


def moments_kernel(where, first, second, new, old, out, half, old_held, sem):
    core = place(where, "core")
    columns = pl.ds(pl.multiple_of(core * 256, 256), 256)
    copies = start_all([pltpu.make_async_copy(new.at[:, columns], half, sem.at[0]), pltpu.make_async_copy(old, old_held, sem.at[1])])
    left = lax.broadcasted_iota(jnp.int32, (64, 128), 1) < 64
    for q in range(8):
        for ref, begin in ((first, 0), (second, 128)):
            one = ref[:, q * 128 : q * 128 + 128]
            two = ref[:, 1024 + q // 2 * 128 : 1152 + q // 2 * 128]
            if q % 2:
                two = pltpu.roll(two, 64, 1)
            two = jnp.where(left, two, pltpu.roll(ref[:, 1536:1664], (192 - q * 16) % 128, 1))
            for i, value in enumerate((one, two)):
                high = value.astype(BF)
                out[q, begin : begin + 64, i * 128 : i * 128 + 128] = high
                if begin == 0:
                    out[q, 64:128, i * 128 : i * 128 + 128] = (value - high.astype(F32)).astype(BF)
    wait_all(copies)
    margin = lax.dot_general(half[...], old_held[...], (((0,), (0,)), ((), ())), preferred_element_type=F32)
    margin = margin.astype(BF)
    for q in range(8):
        for i in range(2):
            out[q, 192 + 32 * i : 224 + 32 * i, :] = margin[q * 32 : q * 32 + 32, i * 256 : i * 256 + 256]


def cut_moments(where, first, second, new, old):
    return pl.pallas_call(
        moments_kernel,
        out_shape=jax.ShapeDtypeStruct((8, 256, 256), BF),
        in_specs=[SMEM, VMEM, VMEM, ANY, ANY],
        out_specs=VMEM,
        scratch_shapes=[pltpu.VMEM((2048, 256), BF), pltpu.VMEM((2048, 512), BF), DMA((2,))],
        cost_estimate=estimate(2 * 2048 * 256 * 512, 6 * 2**20),
        name="cut_moments",
    )(where, first, second, new, old)


def margin_kernel(moments, out, held, sem):
    copy = pltpu.make_async_copy(moments.at[:, pl.ds(192, 64), :], held, sem)
    copy.start()
    copy.wait()
    total = held[0].astype(F32)
    for i in range(1, 8):
        total = total + held[i].astype(F32)
    total = total.astype(BF)
    for i in range(8):
        out[i, :, 0:256] = total[:32]
        out[i, :, 256:512] = total[32:]


def sum_margin(moments):
    return pl.pallas_call(
        margin_kernel,
        out_shape=jax.ShapeDtypeStruct((8, 32, 512), BF),
        in_specs=[ANY],
        out_specs=VMEM,
        scratch_shapes=[pltpu.VMEM((8, 64, 256), BF), DMA],
        cost_estimate=estimate(8 * 64 * 256, 2**19),
        name="sum_margin",
    )(moments)


def step_kernel(where, *refs):
    sums, (own, other, moments), lows = refs[:8], refs[8:11], refs[11:13]
    first_out, second_out, margin = refs[13:]
    core = place(where, "core")
    margin[rows_at(core * 256, 256), :] = own[...]
    margin[rows_at(256 - core * 256, 256), :] = other[...]
    projected = jnp.concatenate(
        [sum(ref[...].astype(F32) for ref in sums[4 * g : 4 * g + 4]) for g in range(2)], axis=0
    )
    contract = (((0,), (1,)), ((), ()))
    one, one_low, two = (moments[:, i * 64 : i * 64 + 64, :].reshape(512, 256) for i in range(3))
    rotated_one = lax.dot_general(one, margin[...], contract, preferred_element_type=F32)
    rotated_one = rotated_one + lax.dot_general(one_low, margin[...], contract, preferred_element_type=F32)
    wide = margin[...].astype(F32)
    rotated_two = lax.dot_general(two, (wide * wide).astype(BF), contract, preferred_element_type=F32)
    first_new = 0.9 * rotated_one[:208] + 0.1 * projected
    second_new = 0.999 * rotated_two[:208] + 0.001 * projected * projected
    low_step = (
        first_new / (1.0 - 0.9**STEP) / (jnp.sqrt(second_new / (1.0 - 0.999**STEP)) + 1e-08)
    ).astype(BF)
    begin = 0
    for ref in lows:
        ref[...] = low_step[begin : begin + ref.shape[0], :]
        begin += ref.shape[0]
    first_out[...] = first_new
    second_out[...] = second_new


def take_step(where, sums, *rest):
    return pl.pallas_call(
        step_kernel,
        out_shape=[jax.ShapeDtypeStruct((piece, 512), BF) for _, piece in GROUPS]
        + [jax.ShapeDtypeStruct((208, 512), F32)] * 2,
        in_specs=[SMEM] + [VMEM] * 11,
        out_specs=[VMEM] * 4,
        scratch_shapes=[pltpu.VMEM((512, 512), BF)],
        cost_estimate=estimate(6 * 208 * 512 * 512, 4 * 2**20),
        name="step",
    )(where, *sums, *rest)


def turn_kernel(first, second, out, wide):
    wide[208:, :] = jnp.zeros((48, 512), F32)
    for i, ref in enumerate((first, second)):
        wide[:208, :] = ref[...]
        out[:, i * 64 : i * 64 + 64, :] = wide[...].T.astype(BF).reshape(8, 64, 256)


def turn_back(first, second):
    return pl.pallas_call(
        turn_kernel,
        out_shape=jax.ShapeDtypeStruct((8, 128, 256), BF),
        in_specs=[VMEM] * 2,
        out_specs=VMEM,
        scratch_shapes=[pltpu.VMEM((256, 512), F32)],
        cost_estimate=estimate(208 * 1024, 3 * 2**19),
        name="turn_back",
    )(first, second)


def finish_kernel(new, *outs):
    lane = lax.broadcasted_iota(jnp.int32, (64, 128), 1)
    for i, out in enumerate(outs):
        rest = []
        for q in range(8):
            block = new[q, i * 64 : i * 64 + 64, :].astype(F32)
            out[:, q * 128 : q * 128 + 128] = block[:, :128]
            rest.append(block[:, 128:])
        for j in range(4):
            out[:, 1024 + j * 128 : 1152 + j * 128] = jnp.where(lane < 64, rest[2 * j], pltpu.roll(rest[2 * j + 1], 64, 1))
        last = pltpu.roll(rest[0], 64, 1)
        for q in range(1, 8):
            last = jnp.where(lane // 16 == q, pltpu.roll(rest[q], (64 + q * 16) % 128, 1) if q != 4 else rest[q], last)
        out[:, 1536:1664] = last


def finish(new):
    return pl.pallas_call(
        finish_kernel,
        out_shape=[jax.ShapeDtypeStruct((64, 1664), F32)] * 2,
        in_specs=[VMEM],
        out_specs=[VMEM] * 2,
        cost_estimate=estimate(64 * 1664 * 4, 3 * 2**19),
        name="finish",
    )(new)


def join_kernel(group, where, *refs):
    arrays, out = refs[:4], refs[4]
    piece = GROUPS[group][1]
    for j in range(4):
        at = (place(where, "v%d" % group) + 4 - j) % 4
        out[rows_at(at * piece, piece), :] = arrays[j][...]


def join(group, where, arrays):
    chunk = GROUPS[group][0]
    return pl.pallas_call(
        functools.partial(join_kernel, group),
        out_shape=jax.ShapeDtypeStruct((chunk // 4, 512), BF),
        in_specs=[SMEM] + [VMEM] * 4,
        out_specs=VMEM,
        cost_estimate=estimate(0, chunk * 512),
    )(where, *arrays)


def low_copies(group, where, arrays, begin, low, in_sem, core_of_arrays):
    if group == 0:
        u = jnp.where(core_of_arrays == 0, place(where, "x"), place(where, "y"))
    else:
        u = place(where, "u1")
    copies = []
    for j in range(4):
        done = 0
        at = (u + 4 - j) % 4
        for first, size in pieces(group, at):
            copies.append(
                pltpu.make_async_copy(
                    arrays[j].at[pl.ds(done, size), :], low.at[rows_at(begin + first, size), :], in_sem.at[at]
                )
            )
            done += size
    return copies


def update_kernel(ring, where, *refs):
    own, other, bases, outs = refs[:4], refs[4:8], refs[8:13], refs[13:17]
    low, base, held, in_sem, other_sem, base_sem, out_sem = refs[17:]
    core = place(where, "core")
    width = WIDTH[ring]
    for k, step in enumerate(STEPS):
        source = basis_rows(ring, where, step, bases)
        pltpu.make_async_copy(source, base.at[pl.ds(k * 128, 128), :], base_sem).start()
    if ring == "x":
        start_all(low_copies(1, where, own, core * 1280, low, in_sem, core))
        start_all(low_copies(1, where, other, (1 - core) * 1280, low, other_sem, 1 - core))
        for at in range(4):
            wait_for(low.at[pl.ds(0, 320), :], in_sem.at[at])
            wait_for(low.at[pl.ds(0, 320), :], other_sem.at[at])
    else:
        part_core = 0 if ring == "y" else 1
        for arrays, chosen in ((own, core == part_core), (other, core != part_core)):

            @pl.when(chosen)
            def _():
                start_all(low_copies(0, where, arrays, 0, low, in_sem, jnp.int32(part_core)))

    wait_for(base, base_sem)

    @pl.loop(0, width // 512)
    def _(i):
        columns = pl.ds(pl.multiple_of(i * 512, 512), 512)
        if ring != "x":
            wait_for(low.at[columns, :], in_sem.at[i])
        product = lax.dot_general(base[...], low[columns, :], (((1,), (1,)), ((), ())), preferred_element_type=F32)
        held[:, columns] = (8.0 * product).astype(BF)
        for k in range(4):
            pltpu.make_async_copy(
                held.at[pl.ds(k * 128, 128), columns], outs[k].at[:, columns], out_sem.at[k]
            ).start()

    for k in range(4):
        wait_for(held.at[pl.ds(k * 128, 128), :], out_sem.at[k])


def update_blocks(ring, where, arrays, bases):
    width = WIDTH[ring]
    return pl.pallas_call(
        functools.partial(update_kernel, ring),
        out_shape=[jax.ShapeDtypeStruct((128, width), BF)] * 4,
        in_specs=[SMEM] + [ANY] * (8 + len(bases)),
        out_specs=[ANY] * 4,
        scratch_shapes=[
            pltpu.VMEM((width, 512), BF),
            pltpu.VMEM((512, 512), BF),
            pltpu.VMEM((512, width), BF),
            DMA((4,)),
            DMA((4,)),
            DMA,
            DMA((4,)),
        ],
        cost_estimate=estimate(2 * 512 * 512 * width, 512 * width * 2 + 512 * 1024 + width * 1024),
    )(where, *arrays, *bases)


def exchange(blocks, rings):
    return [blocks[0]] + [shift(block, rings, step) for block, step in zip(blocks[1:], STEPS[1:])]


def ordered(arrays, rings):
    out = dict([(0, arrays[0])] + [(j, shift(arrays[j], rings, j)) for j in STEPS[1:]])
    return [out[j] for j in range(4)]


def compute(grad, basis_new, basis_old, moment_first, moment_second):
    xl, z, y, xh, core = (lax.axis_index(name).astype(jnp.int32) for name in NAMES)
    x = xh * 2 + xl
    spot = lax.broadcasted_iota(jnp.int32, (8,), 0)
    where = jnp.zeros((8,), jnp.int32)
    for i, value in enumerate((x, y, z, core, xh, jnp.where(core == 0, x, y), jnp.where(core == 0, z, x))):
        where = jnp.where(spot == i, value, where)

    arrived = {}
    for ring in ("x", "y", "z"):
        blocks = pack(ring, where, grad)
        arrived[ring] = exchange(blocks, RINGS[ring])
    by_core = basis_new.reshape(4, 2, 2, 128, 512)
    by_x = lax.dynamic_index_in_dim(lax.dynamic_index_in_dim(by_core, core, 2, False), y, 0, False)
    by_z = lax.dynamic_index_in_dim(by_x, xh, 0, False)
    bases = [basis_new] + [shift(by_z, RINGS["z"], 4 - step) for step in range(1, 4)]
    bases.append(lax.ppermute(by_x.reshape(256, 512), "xl", [(0, 1), (1, 0)]))

    moments = cut_moments(where, moment_first, moment_second, basis_new, basis_old)
    moments = lax.all_to_all(moments, ROW, 0, 0, tiled=True)
    margin = sum_margin(moments)
    margin = lax.all_to_all(margin, ROW, 0, 0, tiled=True).reshape(256, 512)
    margin_other = shift(margin, RINGS["core"], 1)

    totals = {}
    for group, blocks in ((1, arrived["x"]), (0, arrived["y"] + arrived["z"])):
        other = project(group, where, blocks, bases)
        other = shift(other, RINGS["core"], 1)
        partial = project(group, where, blocks, bases, other)
        halves = ordered(partial, U[group])
        rest = add_up(group, where, halves)
        totals[group] = ordered(rest, V[group])

    *lows, first_new, second_new = take_step(where, totals[0] + totals[1], margin, margin_other, moments)

    sent = {}
    for group, rings in ((1, ("x",)), (0, ("y", "z"))):
        low = lows[group]
        quarters = ordered([low] * 4, V[group])
        quarter = join(group, where, quarters)
        whole = ordered([quarter] * 4, U[group])
        whole = whole + [shift(array, RINGS["core"], 1) for array in whole]
        for ring in rings:
            blocks = update_blocks(ring, where, whole, bases)
            sent[ring] = exchange(blocks, RINGS[ring])
    update = None
    for ring in ("x", "y", "z"):
        update = unpack(ring, where, sent[ring], update, grad.shape[1])

    new = turn_back(first_new, second_new)
    new = lax.all_to_all(new, ROW, 0, 0, tiled=True)
    first, second = finish(new)
    return update, first, second


def solution(mesh):
    fine = Mesh(mesh.devices.reshape(SIZES), NAMES)
    col = ("y", "xh", "core")
    placed = (P(NAMES, None), P(ROW, None), P(ROW, None), P(ROW, col), P(ROW, col))
    return jax.shard_map(
        compute,
        mesh=fine,
        in_specs=placed,
        out_specs=(P(NAMES, None), P(ROW, col), P(ROW, col)),
        check_vma=False,
    )
```

```python
import functools
import itertools

import jax
import jax.numpy as jnp
from jax import lax
from jax.experimental import pallas as pl
from jax.experimental.pallas import tpu as pltpu
from jax.sharding import Mesh, PartitionSpec as P


STEP = 10
BF, F32 = jnp.bfloat16, jnp.float32
NAMES = ("xl", "z", "y", "xh", "core")
SIZES = (2, 4, 4, 2, 2)
ROW = ("xl", "z")
ANY = pl.BlockSpec(memory_space=pl.ANY)
SMEM = pl.BlockSpec(memory_space=pltpu.SMEM)
VMEM = pl.BlockSpec(memory_space=pltpu.VMEM)
HBM = pl.BlockSpec(memory_space=pltpu.HBM)
DMA = pltpu.SemaphoreType.DMA
LIMIT = pltpu.CompilerParams(vmem_limit_bytes=16 * 2**20)
STEPS = (0, 1, 3, 2)
WIDTH = {"y": 2048, "z": 2048, "x": 2560}
EXTRA = {"y": 0, "z": 512, "x": 512}
GROUPS = ((2048, 128), (1280, 80))
TILE = (512, 640)
SLOT = {"x": 0, "y": 1, "z": 2, "core": 3, "xh": 4, "u0": 5, "v0": 6, "u1": 2, "v1": 1}
SPOTS = [dict(zip(NAMES, spot)) for spot in itertools.product(*(range(n) for n in SIZES))]


def place(where, axis):
    return where[SLOT[axis]]


def ring_shift(spot, ring, step):
    spot = dict(spot)
    if ring == "x":
        x = (spot["xh"] * 2 + spot["xl"] + step) % 4
        spot["xh"], spot["xl"] = x // 2, x % 2
    elif ring == "core":
        spot["core"] = 1 - spot["core"]
    else:
        spot[ring] = (spot[ring] + step) % 4
    return spot


def shift(array, rings, step):
    pairs = []
    for spot in SPOTS:
        target = ring_shift(spot, rings[spot["core"]], step)
        pairs.append((SPOTS.index(spot), SPOTS.index(target)))
    return lax.ppermute(array, NAMES, pairs)


RINGS = {ring: (ring, ring) for ring in ("x", "y", "z", "core")}
U = (("x", "y"), ("z", "z"))
V = (("z", "x"), ("y", "y"))


def runs(ring, at):
    out, done = [], 0
    if ring == "y":
        for xh in range(2):
            out.append((done, (at * 4 + xh * 2) * 1664, 1024))
            done += 1024
    elif ring == "z":
        for y, xh, xl in itertools.product(range(4), range(2), range(2)):
            out.append((done, (y * 4 + xh * 2 + 1) * 1664 + (xl * 4 + at) * 128, 128))
            done += 128
    else:
        xh, xl = at // 2, at % 2
        for core, y in itertools.product(range(2), range(4)):
            out.append((core * 1280 + y * 256, (y * 4 + xh * 2 + core) * 1664 + (8 + 2 * xl) * 128, 256))
    return out


def pieces(group, u_at):
    if group == 0:
        return [(u_at * 512, 512)]
    return [one for v in range(4) for one in ((v * 256 + u_at * 64, 64), (1024 + v * 64 + u_at * 16, 16))]


def rows_at(first, count):
    return pl.ds(pl.multiple_of(first, 16), count)


def estimate(flops, size):
    return pl.CostEstimate(flops=flops, bytes_accessed=size, transcendentals=0)


def start_all(copies):
    for copy in copies:
        copy.start()
    return copies


def wait_all(copies):
    for copy in copies:
        copy.wait()


def wait_for(ref, sem):
    pltpu.make_async_copy(ref, ref, sem).wait()


def turned(tile):
    return pltpu.roll(tile.astype(F32), 64, 1).astype(BF)


def pack_kernel(ring, where, grad, basis, *refs):
    outs, (held, in_sem, out_sem), more = refs[:4], refs[4:7], refs[7:]
    if ring == "x":
        ends, end_sem = more
        end_copies = start_all(
            [pltpu.make_async_copy(grad.at[:, pl.ds(b * 1664 + 1536, 128)], ends.at[b], end_sem.at[b]) for b in range(16)]
        )
    for at in range(4):
        start_all(
            [
                pltpu.make_async_copy(grad.at[:, pl.ds(source, count)], held.at[at, :, pl.ds(to, count)], in_sem.at[at])
                for to, source, count in runs(ring, at)
            ]
        )
        if EXTRA[ring]:
            rows = basis_rows("x", where, 0, basis)
            pltpu.make_async_copy(rows, held.at[at, :, pl.ds(WIDTH[ring], 512)], in_sem.at[at]).start()
    whole = held
    if ring == "x":
        wait_all(end_copies)
        left = lax.broadcasted_iota(jnp.int32, (128, 128), 1) < 64
        for xh, core, pair in itertools.product(range(2), range(2), range(2)):
            one, two = (ends[(2 * pair + i) * 4 + xh * 2 + core] for i in range(2))
            columns = pl.ds(core * 1280 + 1024 + pair * 128, 128)
            held[xh * 2, :, columns] = jnp.where(left, one, turned(two))
            held[xh * 2 + 1, :, columns] = jnp.where(left, turned(one), two)
        whole = held.at[:, :, pl.ds(0, 2560)]
    t = place(where, ring)
    stores = []
    for k, step in enumerate(STEPS):
        at = (t + step) % 4
        wait_for(whole.at[at], in_sem.at[at])
        copy = pltpu.make_async_copy(held.at[at], outs[k], out_sem.at[k])
        copy.start()
        stores.append(copy)
    wait_all(stores)


def pack(ring, where, grad, basis):
    width = WIDTH[ring] + EXTRA[ring]
    return pl.pallas_call(
        functools.partial(pack_kernel, ring),
        out_shape=[jax.ShapeDtypeStruct((128, width), BF)] * 4,
        in_specs=[SMEM, HBM, ANY],
        out_specs=[ANY] * 4,
        scratch_shapes=[pltpu.VMEM((4, 128, width), BF), DMA((4,)), DMA((4,))]
        + ([pltpu.VMEM((16, 128, 128), BF), DMA((16,))] if ring == "x" else []),
        compiler_params=LIMIT,
        cost_estimate=estimate(0, 4 * 128 * width * 4),
    )(where, grad, basis)


def unpack_kernel(ring, where, *refs):
    blocks = refs[:4]
    if ring == "x":
        out, held, in_sem, out_sem, ends, end_sem = refs[-6:]
    else:
        out, held, in_sem, out_sem = refs[-4:]
    t = place(where, ring)
    start_all(
        [
            pltpu.make_async_copy(blocks[k], held.at[(t + 4 - step) % 4], in_sem.at[(t + 4 - step) % 4])
            for k, step in enumerate(STEPS)
        ]
    )
    stores = []
    for at in range(4):
        wait_for(held.at[at], in_sem.at[at])
        stores += start_all(
            [
                pltpu.make_async_copy(held.at[at, :, pl.ds(to, count)], out.at[:, pl.ds(source, count)], out_sem.at[at, j])
                for j, (to, source, count) in enumerate(runs(ring, at))
            ]
        )
    if ring == "x":
        left = lax.broadcasted_iota(jnp.int32, (128, 128), 1) < 64
        for xh, core, pair in itertools.product(range(2), range(2), range(2)):
            columns = pl.ds(core * 1280 + 1024 + pair * 128, 128)
            one, two = held[xh * 2, :, columns], held[xh * 2 + 1, :, columns]
            block = 2 * pair * 4 + xh * 2 + core
            ends[block] = jnp.where(left, one, turned(two))
            ends[block + 4] = jnp.where(left, turned(one), two)
        stores += start_all(
            [pltpu.make_async_copy(ends.at[b], out.at[:, pl.ds(b * 1664 + 1536, 128)], end_sem.at[b]) for b in range(16)]
        )
    wait_all(stores)


def unpack(ring, where, blocks, before, columns):
    width = WIDTH[ring]
    more = [] if before is None else [before]
    return pl.pallas_call(
        functools.partial(unpack_kernel, ring),
        out_shape=jax.ShapeDtypeStruct((128, columns), BF),
        in_specs=[SMEM] + [ANY] * (4 + len(more)),
        out_specs=ANY,
        scratch_shapes=[pltpu.VMEM((4, 128, width), BF), DMA((4,)), DMA((4, 16))]
        + ([pltpu.VMEM((16, 128, 128), BF), DMA((16,))] if ring == "x" else []),
        input_output_aliases={5: 0} if more else {},
        compiler_params=LIMIT,
        cost_estimate=estimate(0, 4 * 128 * width * 4),
    )(where, *blocks, *more)


def basis_rows(ring, where, step, base):
    y, xh, core = place(where, "y"), place(where, "xh"), place(where, "core")
    if ring == "y":
        y = (y + step) % 4
    return base.at[pl.ds(pl.multiple_of((y * 4 + xh * 2 + core) * 128, 128), 128), :]


def start_blocks(ring, where, blocks, first, chunk, tile, basis, held, base, in_sem, base_sem):
    for k, step in enumerate(STEPS):
        if EXTRA[ring]:
            source = blocks[k].at[:, pl.ds(WIDTH[ring], 512)]
        else:
            source = basis_rows(ring, where, 4 - step, basis)
        pltpu.make_async_copy(source, base.at[pl.ds(k * 128, 128), :], base_sem).start()
    for i in range(chunk // tile):
        for k in range(4):
            columns = pl.ds(pl.multiple_of(first + i * tile, 128), tile)
            target = held.at[pl.ds(k * 128, 128), pl.ds(i * tile, tile)]
            pltpu.make_async_copy(blocks[k].at[:, columns], target, in_sem.at[i]).start()


def project_kernel(group, own, where, *refs):
    count = 8 if group == 0 else 4
    blocks, basis, refs = refs[:count], refs[count], refs[count + 1 :]
    if own:
        other, outs, (held, base, total, in_sem, base_sem, other_sem, out_sem) = refs[0], refs[1:5], refs[5:]
    else:
        out, held, base, total, in_sem, base_sem, out_sem = refs
    chunk, tile = GROUPS[group][0], TILE[group]
    core = place(where, "core")
    scratch = (chunk, tile, basis, held, base, in_sem, base_sem)
    if group == 0:
        on_y = core == (0 if own else 1)
        for ring, mine, chosen in (("y", blocks[:4], on_y), ("z", blocks[4:], jnp.logical_not(on_y))):

            @pl.when(chosen)
            def _():
                start_blocks(ring, where, mine, 0, *scratch)

    else:
        start_blocks("x", where, blocks, (core if own else 1 - core) * chunk, *scratch)
    if own:
        copy = pltpu.make_async_copy(other, total, other_sem)
        copy.start()
        copy.wait()
    wait_for(base, base_sem)

    @pl.loop(0, chunk // tile)
    def _(i):
        some = pl.ds(pl.multiple_of(i * tile, tile), tile)
        wait_for(held.at[:, some], in_sem.at[i])
        product = lax.dot_general(held[:, some], base[...], (((0,), (0,)), ((), ())), preferred_element_type=F32)
        if own:
            product = product + total[some, :].astype(F32)
        total[some, :] = product.astype(BF)
        if not own:
            pltpu.make_async_copy(total.at[some, :], out.at[some, :], out_sem).start()

    if not own:
        wait_for(total, out_sem)
        return
    stores = []
    for j in range(4):
        done = 0
        for i, (first, size) in enumerate(pieces(group, (place(where, "u%d" % group) + j) % 4)):
            stores.append(
                pltpu.make_async_copy(
                    total.at[rows_at(first, size), :], outs[j].at[pl.ds(done, size), :], out_sem.at[j, i]
                )
            )
            done += size
    wait_all(start_all(stores))


def project(group, where, blocks, basis, other=None):
    chunk = GROUPS[group][0]
    own = other is not None
    shapes = [jax.ShapeDtypeStruct((chunk // 4, 512), BF)] * 4 if own else jax.ShapeDtypeStruct((chunk, 512), BF)
    return pl.pallas_call(
        functools.partial(project_kernel, group, own),
        out_shape=shapes,
        in_specs=[SMEM] + [ANY] * (len(blocks) + 1 + own),
        out_specs=[ANY] * 4 if own else ANY,
        scratch_shapes=[
            pltpu.VMEM((512, chunk), BF),
            pltpu.VMEM((512, 512), BF),
            pltpu.VMEM((chunk, 512), BF),
            DMA((4,)),
            DMA,
        ]
        + ([DMA, DMA((4, 8))] if own else [DMA]),
        compiler_params=LIMIT,
        cost_estimate=estimate(2 * 512 * 512 * chunk, 512 * chunk * 2 + 512 * 1024 + chunk * 1024),
    )(where, *blocks, basis, *([other] if own else []))


def add_kernel(group, where, a, b, c, d, *refs):
    outs, total = refs[:4], refs[4]
    piece = GROUPS[group][1]
    total[...] = (
        (a[...].astype(F32) + b[...].astype(F32)) + (c[...].astype(F32) + d[...].astype(F32))
    ).astype(BF)
    for j in range(4):
        at = (place(where, "v%d" % group) + j) % 4
        outs[j][...] = total[rows_at(at * piece, piece), :]


def add_up(group, where, arrays):
    chunk, piece = GROUPS[group]
    return pl.pallas_call(
        functools.partial(add_kernel, group),
        out_shape=[jax.ShapeDtypeStruct((piece, 512), BF)] * 4,
        in_specs=[SMEM] + [VMEM] * 4,
        out_specs=[VMEM] * 4,
        scratch_shapes=[pltpu.VMEM((chunk // 4, 512), BF)],
        compiler_params=LIMIT,
        cost_estimate=estimate(3 * chunk * 128, 5 * chunk * 256),
    )(where, *arrays)


def moments_kernel(where, first, second, new, old, out, half, old_held, sem):
    core = place(where, "core")
    columns = pl.ds(pl.multiple_of(core * 256, 256), 256)
    copies = start_all([pltpu.make_async_copy(new.at[:, columns], half, sem.at[0]), pltpu.make_async_copy(old, old_held, sem.at[1])])
    left = lax.broadcasted_iota(jnp.int32, (64, 128), 1) < 64
    for q in range(8):
        for ref, begin in ((first, 0), (second, 128)):
            one = ref[:, q * 128 : q * 128 + 128]
            two = ref[:, 1024 + q // 2 * 128 : 1152 + q // 2 * 128]
            if q % 2:
                two = pltpu.roll(two, 64, 1)
            two = jnp.where(left, two, pltpu.roll(ref[:, 1536:1664], (192 - q * 16) % 128, 1))
            for i, value in enumerate((one, two)):
                high = value.astype(BF)
                out[q, begin : begin + 64, i * 128 : i * 128 + 128] = high
                if begin == 0:
                    out[q, 64:128, i * 128 : i * 128 + 128] = (value - high.astype(F32)).astype(BF)
    wait_all(copies)
    margin = lax.dot_general(half[...], old_held[...], (((0,), (0,)), ((), ())), preferred_element_type=F32)
    margin = margin.astype(BF)
    for q in range(8):
        for i in range(2):
            out[q, 192 + 32 * i : 224 + 32 * i, :] = margin[q * 32 : q * 32 + 32, i * 256 : i * 256 + 256]


def cut_moments(where, first, second, new, old):
    return pl.pallas_call(
        moments_kernel,
        out_shape=jax.ShapeDtypeStruct((8, 256, 256), BF),
        in_specs=[SMEM, VMEM, VMEM, ANY, ANY],
        out_specs=VMEM,
        scratch_shapes=[pltpu.VMEM((2048, 256), BF), pltpu.VMEM((2048, 512), BF), DMA((2,))],
        compiler_params=LIMIT,
        cost_estimate=estimate(2 * 2048 * 256 * 512, 6 * 2**20),
        name="cut_moments",
    )(where, first, second, new, old)


def margin_kernel(moments, out, held, sem):
    copy = pltpu.make_async_copy(moments.at[:, pl.ds(192, 64), :], held, sem)
    copy.start()
    copy.wait()
    total = held[0].astype(F32)
    for i in range(1, 8):
        total = total + held[i].astype(F32)
    total = total.astype(BF)
    for i in range(8):
        out[i, :, 0:256] = total[:32]
        out[i, :, 256:512] = total[32:]


def sum_margin(moments):
    return pl.pallas_call(
        margin_kernel,
        out_shape=jax.ShapeDtypeStruct((8, 32, 512), BF),
        in_specs=[ANY],
        out_specs=VMEM,
        scratch_shapes=[pltpu.VMEM((8, 64, 256), BF), DMA],
        compiler_params=LIMIT,
        cost_estimate=estimate(8 * 64 * 256, 2**19),
        name="sum_margin",
    )(moments)


def step_kernel(where, *refs):
    sums, (own, other, moments), lows = refs[:8], refs[8:11], refs[11:13]
    first_out, second_out, margin = refs[13:]
    core = place(where, "core")
    margin[rows_at(core * 256, 256), :] = own[...]
    margin[rows_at(256 - core * 256, 256), :] = other[...]
    projected = jnp.concatenate(
        [sum(ref[...].astype(F32) for ref in sums[4 * g : 4 * g + 4]) for g in range(2)], axis=0
    )
    contract = (((0,), (1,)), ((), ()))
    one, one_low, two = (moments[:, i * 64 : i * 64 + 64, :].reshape(512, 256) for i in range(3))
    rotated_one = lax.dot_general(one, margin[...], contract, preferred_element_type=F32)
    rotated_one = rotated_one + lax.dot_general(one_low, margin[...], contract, preferred_element_type=F32)
    wide = margin[...].astype(F32)
    rotated_two = lax.dot_general(two, (wide * wide).astype(BF), contract, preferred_element_type=F32)
    first_new = 0.9 * rotated_one[:208] + 0.1 * projected
    second_new = 0.999 * rotated_two[:208] + 0.001 * projected * projected
    low_step = (
        first_new / (1.0 - 0.9**STEP) / (jnp.sqrt(second_new / (1.0 - 0.999**STEP)) + 1e-08)
    ).astype(BF)
    begin = 0
    for ref in lows:
        ref[...] = low_step[begin : begin + ref.shape[0], :]
        begin += ref.shape[0]
    first_out[...] = first_new
    second_out[...] = second_new


def take_step(where, sums, *rest):
    return pl.pallas_call(
        step_kernel,
        out_shape=[jax.ShapeDtypeStruct((piece, 512), BF) for _, piece in GROUPS]
        + [jax.ShapeDtypeStruct((208, 512), F32)] * 2,
        in_specs=[SMEM] + [VMEM] * 11,
        out_specs=[VMEM] * 4,
        scratch_shapes=[pltpu.VMEM((512, 512), BF)],
        compiler_params=LIMIT,
        cost_estimate=estimate(6 * 208 * 512 * 512, 4 * 2**20),
        name="step",
    )(where, *sums, *rest)


def turn_kernel(first, second, out, wide):
    wide[208:, :] = jnp.zeros((48, 512), F32)
    for i, ref in enumerate((first, second)):
        wide[:208, :] = ref[...]
        out[:, i * 64 : i * 64 + 64, :] = wide[...].T.astype(BF).reshape(8, 64, 256)


def turn_back(first, second):
    return pl.pallas_call(
        turn_kernel,
        out_shape=jax.ShapeDtypeStruct((8, 128, 256), BF),
        in_specs=[VMEM] * 2,
        out_specs=VMEM,
        scratch_shapes=[pltpu.VMEM((256, 512), F32)],
        compiler_params=LIMIT,
        cost_estimate=estimate(208 * 1024, 3 * 2**19),
        name="turn_back",
    )(first, second)


def finish_kernel(new, *outs):
    lane = lax.broadcasted_iota(jnp.int32, (64, 128), 1)
    for i, out in enumerate(outs):
        rest = []
        for q in range(8):
            block = new[q, i * 64 : i * 64 + 64, :].astype(F32)
            out[:, q * 128 : q * 128 + 128] = block[:, :128]
            rest.append(block[:, 128:])
        for j in range(4):
            out[:, 1024 + j * 128 : 1152 + j * 128] = jnp.where(lane < 64, rest[2 * j], pltpu.roll(rest[2 * j + 1], 64, 1))
        last = pltpu.roll(rest[0], 64, 1)
        for q in range(1, 8):
            last = jnp.where(lane // 16 == q, pltpu.roll(rest[q], (64 + q * 16) % 128, 1) if q != 4 else rest[q], last)
        out[:, 1536:1664] = last


def finish(new):
    return pl.pallas_call(
        finish_kernel,
        out_shape=[jax.ShapeDtypeStruct((64, 1664), F32)] * 2,
        in_specs=[VMEM],
        out_specs=[VMEM] * 2,
        compiler_params=LIMIT,
        cost_estimate=estimate(64 * 1664 * 4, 3 * 2**19),
        name="finish",
    )(new)


def join_kernel(group, where, *refs):
    arrays, out = refs[:4], refs[4]
    piece = GROUPS[group][1]
    for j in range(4):
        at = (place(where, "v%d" % group) + 4 - j) % 4
        out[rows_at(at * piece, piece), :] = arrays[j][...]


def join(group, where, arrays):
    chunk = GROUPS[group][0]
    return pl.pallas_call(
        functools.partial(join_kernel, group),
        out_shape=jax.ShapeDtypeStruct((chunk // 4, 512), BF),
        in_specs=[SMEM] + [VMEM] * 4,
        out_specs=VMEM,
        compiler_params=LIMIT,
        cost_estimate=estimate(0, chunk * 512),
    )(where, *arrays)


def low_copies(group, where, arrays, begin, low, in_sem, core_of_arrays):
    if group == 0:
        u = jnp.where(core_of_arrays == 0, place(where, "x"), place(where, "y"))
    else:
        u = place(where, "u1")
    copies = []
    for j in range(4):
        done = 0
        at = (u + 4 - j) % 4
        for first, size in pieces(group, at):
            copies.append(
                pltpu.make_async_copy(
                    arrays[j].at[pl.ds(done, size), :], low.at[rows_at(begin + first, size), :], in_sem.at[at]
                )
            )
            done += size
    return copies


def update_kernel(ring, where, *refs):
    count = 4 if EXTRA[ring] else 1
    own, other, bases, outs = refs[:4], refs[4:8], refs[8 : 8 + count], refs[8 + count : 12 + count]
    low, base, held, in_sem, other_sem, base_sem, out_sem = refs[12 + count :]
    core = place(where, "core")
    width = WIDTH[ring]
    for k, step in enumerate(STEPS):
        if EXTRA[ring]:
            source = bases[STEPS.index((4 - step) % 4)].at[:, pl.ds(width, 512)]
        else:
            source = basis_rows(ring, where, step, bases[0])
        pltpu.make_async_copy(source, base.at[pl.ds(k * 128, 128), :], base_sem).start()
    if ring == "x":
        start_all(low_copies(1, where, own, core * 1280, low, in_sem, core))
        start_all(low_copies(1, where, other, (1 - core) * 1280, low, other_sem, 1 - core))
        for at in range(4):
            wait_for(low.at[pl.ds(0, 320), :], in_sem.at[at])
            wait_for(low.at[pl.ds(0, 320), :], other_sem.at[at])
    else:
        part_core = 0 if ring == "y" else 1
        for arrays, chosen in ((own, core == part_core), (other, core != part_core)):

            @pl.when(chosen)
            def _():
                start_all(low_copies(0, where, arrays, 0, low, in_sem, jnp.int32(part_core)))

    wait_for(base, base_sem)

    @pl.loop(0, width // 512)
    def _(i):
        columns = pl.ds(pl.multiple_of(i * 512, 512), 512)
        if ring != "x":
            wait_for(low.at[columns, :], in_sem.at[i])
        product = lax.dot_general(base[...], low[columns, :], (((1,), (1,)), ((), ())), preferred_element_type=F32)
        held[:, columns] = (8.0 * product).astype(BF)
        for k in range(4):
            pltpu.make_async_copy(
                held.at[pl.ds(k * 128, 128), columns], outs[k].at[:, columns], out_sem.at[k]
            ).start()

    for k in range(4):
        wait_for(held.at[pl.ds(k * 128, 128), :], out_sem.at[k])


def update_blocks(ring, where, arrays, bases):
    width = WIDTH[ring]
    return pl.pallas_call(
        functools.partial(update_kernel, ring),
        out_shape=[jax.ShapeDtypeStruct((128, width), BF)] * 4,
        in_specs=[SMEM] + [ANY] * (8 + len(bases)),
        out_specs=[ANY] * 4,
        scratch_shapes=[
            pltpu.VMEM((width, 512), BF),
            pltpu.VMEM((512, 512), BF),
            pltpu.VMEM((512, width), BF),
            DMA((4,)),
            DMA((4,)),
            DMA,
            DMA((4,)),
        ],
        compiler_params=LIMIT,
        cost_estimate=estimate(2 * 512 * 512 * width, 512 * width * 2 + 512 * 1024 + width * 1024),
    )(where, *arrays, *bases)


def exchange(blocks, rings):
    return [blocks[0]] + [shift(block, rings, step) for block, step in zip(blocks[1:], STEPS[1:])]


def ordered(arrays, rings):
    out = dict([(0, arrays[0])] + [(j, shift(arrays[j], rings, j)) for j in STEPS[1:]])
    return [out[j] for j in range(4)]


def compute(grad, basis_new, basis_old, moment_first, moment_second):
    xl, z, y, xh, core = (lax.axis_index(name).astype(jnp.int32) for name in NAMES)
    x = xh * 2 + xl
    spot = lax.broadcasted_iota(jnp.int32, (8,), 0)
    where = jnp.zeros((8,), jnp.int32)
    for i, value in enumerate((x, y, z, core, xh, jnp.where(core == 0, x, y), jnp.where(core == 0, z, x))):
        where = jnp.where(spot == i, value, where)

    arrived = {}
    for ring in ("x", "z", "y"):
        blocks = pack(ring, where, grad, basis_new)
        arrived[ring] = exchange(blocks, RINGS[ring])

    moments = cut_moments(where, moment_first, moment_second, basis_new, basis_old)
    moments = lax.all_to_all(moments, ROW, 0, 0, tiled=True)
    margin = sum_margin(moments)
    margin = lax.all_to_all(margin, ROW, 0, 0, tiled=True).reshape(256, 512)
    margin_other = shift(margin, RINGS["core"], 1)

    totals = {}
    for group, blocks in ((1, arrived["x"]), (0, arrived["y"] + arrived["z"])):
        other = project(group, where, blocks, basis_new)
        other = shift(other, RINGS["core"], 1)
        partial = project(group, where, blocks, basis_new, other)
        halves = ordered(partial, U[group])
        rest = add_up(group, where, halves)
        totals[group] = ordered(rest, V[group])

    *lows, first_new, second_new = take_step(where, totals[0] + totals[1], margin, margin_other, moments)

    sent = {}
    for group, rings in ((1, ("x",)), (0, ("y", "z"))):
        low = lows[group]
        quarters = ordered([low] * 4, V[group])
        quarter = join(group, where, quarters)
        whole = ordered([quarter] * 4, U[group])
        whole = whole + [shift(array, RINGS["core"], 1) for array in whole]
        for ring in rings:
            blocks = update_blocks(ring, where, whole, arrived[ring] if EXTRA[ring] else [basis_new])
            sent[ring] = exchange(blocks, RINGS[ring])
    update = None
    for ring in ("x", "y", "z"):
        update = unpack(ring, where, sent[ring], update, grad.shape[1])

    new = turn_back(first_new, second_new)
    new = lax.all_to_all(new, ROW, 0, 0, tiled=True)
    first, second = finish(new)
    return update, first, second


def solution(mesh):
    fine = Mesh(mesh.devices.reshape(SIZES), NAMES)
    col = ("y", "xh", "core")
    placed = (P(NAMES, None), P(ROW, None), P(ROW, None), P(ROW, col), P(ROW, col))
    return jax.shard_map(
        compute,
        mesh=fine,
        in_specs=placed,
        out_specs=(P(NAMES, None), P(ROW, col), P(ROW, col)),
        check_vma=False,
    )
```

```python
import functools
import itertools

import jax
import jax.numpy as jnp
from jax import lax
from jax.experimental import pallas as pl
from jax.experimental.pallas import tpu as pltpu
from jax.sharding import Mesh, PartitionSpec as P


STEP = 10
BF, F32 = jnp.bfloat16, jnp.float32
NAMES = ("xl", "z", "y", "xh", "core")
SIZES = (2, 4, 4, 2, 2)
ROW = ("xl", "z")
ANY = pl.BlockSpec(memory_space=pl.ANY)
SMEM = pl.BlockSpec(memory_space=pltpu.SMEM)
VMEM = pl.BlockSpec(memory_space=pltpu.VMEM)
HBM = pl.BlockSpec(memory_space=pltpu.HBM)
DMA = pltpu.SemaphoreType.DMA
LIMIT = pltpu.CompilerParams(vmem_limit_bytes=16 * 2**20)
ALL_OF_IT = pltpu.CompilerParams(vmem_limit_bytes=60 * 1024 * 1024)


def blocks_of(count, shape):
    return [pltpu.HBM(shape, BF)] + [jax.ShapeDtypeStruct(shape, BF)] * (count - 1)


STEPS = (0, 1, 3, 2)
WIDTH = {"y": 2048, "z": 2048, "x": 2560}
EXTRA = {"y": 0, "z": 512, "x": 512}


def with_basis(ring, step):
    return ring == "z" or (ring == "x" and step % 2 == 1)


GROUPS = ((2048, 128), (1280, 80))
TILE = (512, 640)
SLOT = {"x": 0, "y": 1, "z": 2, "core": 3, "xh": 4, "u0": 5, "v0": 6, "u1": 2, "v1": 1}
SPOTS = [dict(zip(NAMES, spot)) for spot in itertools.product(*(range(n) for n in SIZES))]


def place(where, axis):
    return where[SLOT[axis]]


def ring_shift(spot, ring, step):
    spot = dict(spot)
    if ring == "x":
        x = (spot["xh"] * 2 + spot["xl"] + step) % 4
        spot["xh"], spot["xl"] = x // 2, x % 2
    elif ring == "core":
        spot["core"] = 1 - spot["core"]
    else:
        spot[ring] = (spot[ring] + step) % 4
    return spot


def shift(array, rings, step):
    pairs = []
    for spot in SPOTS:
        target = ring_shift(spot, rings[spot["core"]], step)
        pairs.append((SPOTS.index(spot), SPOTS.index(target)))
    return lax.ppermute(array, NAMES, pairs)


RINGS = {ring: (ring, ring) for ring in ("x", "y", "z", "core")}
U = (("x", "y"), ("z", "z"))
V = (("z", "x"), ("y", "y"))


def runs(ring, at):
    out, done = [], 0
    if ring == "y":
        for xh in range(2):
            out.append((done, (at * 4 + xh * 2) * 1664, 1024))
            done += 1024
    elif ring == "z":
        for y, xh, xl in itertools.product(range(4), range(2), range(2)):
            out.append((done, (y * 4 + xh * 2 + 1) * 1664 + (xl * 4 + at) * 128, 128))
            done += 128
    else:
        xh, xl = at // 2, at % 2
        for core, y in itertools.product(range(2), range(4)):
            out.append((core * 1280 + y * 256, (y * 4 + xh * 2 + core) * 1664 + (8 + 2 * xl) * 128, 256))
    return out


def pieces(group, u_at):
    if group == 0:
        return [(u_at * 512, 512)]
    return [one for v in range(4) for one in ((v * 256 + u_at * 64, 64), (1024 + v * 64 + u_at * 16, 16))]


def rows_at(first, count):
    return pl.ds(pl.multiple_of(first, 16), count)


def estimate(flops, size):
    return pl.CostEstimate(flops=flops, bytes_accessed=size, transcendentals=0)


def start_all(copies):
    for copy in copies:
        copy.start()
    return copies


def wait_all(copies):
    for copy in copies:
        copy.wait()


def wait_for(ref, sem):
    pltpu.make_async_copy(ref, ref, sem).wait()


def turned(tile):
    return pltpu.roll(tile.astype(F32), 64, 1).astype(BF)


def pack_kernel(ring, where, grad, basis, *refs):
    outs, (held, in_sem, out_sem), more = refs[:4], refs[4:7], refs[7:]
    if ring == "x":
        ends, end_sem = more
        end_copies = start_all(
            [pltpu.make_async_copy(grad.at[:, pl.ds(b * 1664 + 1536, 128)], ends.at[b], end_sem.at[b]) for b in range(16)]
        )
    for at in range(4):
        start_all(
            [
                pltpu.make_async_copy(grad.at[:, pl.ds(source, count)], held.at[at, :, pl.ds(to, count)], in_sem.at[at])
                for to, source, count in runs(ring, at)
            ]
        )
        if EXTRA[ring]:
            rows = basis_rows("x", where, 0, basis)
            pltpu.make_async_copy(rows, held.at[at, :, pl.ds(WIDTH[ring], 512)], in_sem.at[at]).start()
    whole = held
    if ring == "x":
        wait_all(end_copies)
        left = lax.broadcasted_iota(jnp.int32, (128, 128), 1) < 64
        for xh, core, pair in itertools.product(range(2), range(2), range(2)):
            one, two = (ends[(2 * pair + i) * 4 + xh * 2 + core] for i in range(2))
            columns = pl.ds(core * 1280 + 1024 + pair * 128, 128)
            held[xh * 2, :, columns] = jnp.where(left, one, turned(two))
            held[xh * 2 + 1, :, columns] = jnp.where(left, turned(one), two)
        whole = held.at[:, :, pl.ds(0, 2560)]
    t = place(where, ring)
    stores = []
    for k, step in enumerate(STEPS):
        at = (t + step) % 4
        wait_for(whole.at[at], in_sem.at[at])
        source = held.at[at] if with_basis(ring, step) else held.at[at, :, pl.ds(0, WIDTH[ring])]
        copy = pltpu.make_async_copy(source, outs[k], out_sem.at[k])
        copy.start()
        stores.append(copy)
    wait_all(stores)


def pack(ring, where, grad, basis):
    width = WIDTH[ring] + EXTRA[ring]
    return pl.pallas_call(
        functools.partial(pack_kernel, ring),
        out_shape=[
            (jax.ShapeDtypeStruct if step else pltpu.HBM)((128, WIDTH[ring] + 512 * with_basis(ring, step)), BF)
            for step in STEPS
        ],
        in_specs=[SMEM, ANY, ANY],
        out_specs=[ANY] * 4,
        scratch_shapes=[pltpu.VMEM((4, 128, width), BF), DMA((4,)), DMA((4,))]
        + ([pltpu.VMEM((16, 128, 128), BF), DMA((16,))] if ring == "x" else []),
        compiler_params=ALL_OF_IT if ring == "x" else LIMIT,
        cost_estimate=estimate(0, 4 * 128 * width * 4),
    )(where, grad, basis)


def unpack_kernel(ring, where, *refs):
    blocks = refs[:4]
    if ring == "x":
        out, held, in_sem, out_sem, ends, end_sem = refs[-6:]
    else:
        out, held, in_sem, out_sem = refs[-4:]
    t = place(where, ring)
    if ring != "x":
        stores = []
        for k, step in enumerate(STEPS):
            for j, (to, source, count) in enumerate(runs(ring, (t + 4 - step) % 4)):
                columns = pl.ds(pl.multiple_of(source, 128), count)
                stores.append(pltpu.make_async_copy(blocks[k].at[:, pl.ds(to, count)], out.at[:, columns], out_sem.at[k, j]))
        wait_all(start_all(stores))
        return
    start_all(
        [
            pltpu.make_async_copy(blocks[k], held.at[(t + 4 - step) % 4], in_sem.at[(t + 4 - step) % 4])
            for k, step in enumerate(STEPS)
        ]
    )
    stores = []
    for at in range(4):
        wait_for(held.at[at], in_sem.at[at])
        stores += start_all(
            [
                pltpu.make_async_copy(held.at[at, :, pl.ds(to, count)], out.at[:, pl.ds(source, count)], out_sem.at[at, j])
                for j, (to, source, count) in enumerate(runs(ring, at))
            ]
        )
    if ring == "x":
        left = lax.broadcasted_iota(jnp.int32, (128, 128), 1) < 64
        for xh, core, pair in itertools.product(range(2), range(2), range(2)):
            columns = pl.ds(core * 1280 + 1024 + pair * 128, 128)
            one, two = held[xh * 2, :, columns], held[xh * 2 + 1, :, columns]
            block = 2 * pair * 4 + xh * 2 + core
            ends[block] = jnp.where(left, one, turned(two))
            ends[block + 4] = jnp.where(left, turned(one), two)
        stores += start_all(
            [pltpu.make_async_copy(ends.at[b], out.at[:, pl.ds(b * 1664 + 1536, 128)], end_sem.at[b]) for b in range(16)]
        )
    wait_all(stores)


def unpack(ring, where, blocks, before, columns):
    width = WIDTH[ring]
    more = [] if before is None else [before]
    return pl.pallas_call(
        functools.partial(unpack_kernel, ring),
        out_shape=jax.ShapeDtypeStruct((128, columns), BF),
        in_specs=[SMEM] + [ANY if ring == "x" else VMEM] * 4 + [ANY] * len(more),
        out_specs=ANY,
        scratch_shapes=[pltpu.VMEM((4, 128, width if ring == "x" else 128), BF), DMA((4,)), DMA((4, 16))]
        + ([pltpu.VMEM((16, 128, 128), BF), DMA((16,))] if ring == "x" else []),
        input_output_aliases={5: 0} if more else {},
        compiler_params=LIMIT,
        cost_estimate=estimate(0, 4 * 128 * width * 4),
    )(where, *blocks, *more)


def basis_rows(ring, where, step, base):
    y, xh, core = place(where, "y"), place(where, "xh"), place(where, "core")
    if ring == "y":
        y = (y + step) % 4
    elif step % 4 == 2:
        xh = 1 - xh
    return base.at[pl.ds(pl.multiple_of((y * 4 + xh * 2 + core) * 128, 128), 128), :]


def start_blocks(ring, where, blocks, first, chunk, tile, basis, held, base, in_sem, base_sem):
    for k, step in enumerate(STEPS):
        if with_basis(ring, step):
            source = blocks[k].at[:, pl.ds(WIDTH[ring], 512)]
        else:
            source = basis_rows(ring, where, 4 - step, basis)
        pltpu.make_async_copy(source, base.at[pl.ds(k * 128, 128), :], base_sem).start()
    for i in range(chunk // tile):
        for k in range(4):
            columns = pl.ds(pl.multiple_of(first + i * tile, 128), tile)
            target = held.at[pl.ds(k * 128, 128), pl.ds(i * tile, tile)]
            pltpu.make_async_copy(blocks[k].at[:, columns], target, in_sem.at[i]).start()


def project_kernel(group, own, where, *refs):
    count = 8 if group == 0 else 4
    blocks, basis, refs = refs[:count], refs[count], refs[count + 1 :]
    if own:
        other, outs, (held, base, total, in_sem, base_sem, other_sem, out_sem) = refs[0], refs[1:5], refs[5:]
    else:
        out, held, base, total, in_sem, base_sem, out_sem = refs
    chunk, tile = GROUPS[group][0], TILE[group]
    core = place(where, "core")
    scratch = (chunk, tile, basis, held, base, in_sem, base_sem)
    if group == 0:
        on_y = core == (0 if own else 1)
        for ring, mine, chosen in (("y", blocks[:4], on_y), ("z", blocks[4:], jnp.logical_not(on_y))):

            @pl.when(chosen)
            def _():
                start_blocks(ring, where, mine, 0, *scratch)

    else:
        start_blocks("x", where, blocks, (core if own else 1 - core) * chunk, *scratch)
    if own:
        copy = pltpu.make_async_copy(other, total, other_sem)
        copy.start()
        copy.wait()
    wait_for(base, base_sem)

    @pl.loop(0, chunk // tile)
    def _(i):
        some = pl.ds(pl.multiple_of(i * tile, tile), tile)
        wait_for(held.at[:, some], in_sem.at[i])
        product = lax.dot_general(held[:, some], base[...], (((0,), (0,)), ((), ())), preferred_element_type=F32)
        if own:
            product = product + total[some, :].astype(F32)
        total[some, :] = product.astype(BF)
        if not own:
            pltpu.make_async_copy(total.at[some, :], out.at[some, :], out_sem).start()

    if not own:
        wait_for(total, out_sem)
        return
    stores = []
    for j in range(4):
        done = 0
        for i, (first, size) in enumerate(pieces(group, (place(where, "u%d" % group) + j) % 4)):
            stores.append(
                pltpu.make_async_copy(
                    total.at[rows_at(first, size), :], outs[j].at[pl.ds(done, size), :], out_sem.at[j, i]
                )
            )
            done += size
    wait_all(start_all(stores))


def project(group, where, blocks, basis, other=None):
    chunk = GROUPS[group][0]
    own = other is not None
    shapes = blocks_of(4, (chunk // 4, 512)) if own else jax.ShapeDtypeStruct((chunk, 512), BF)
    return pl.pallas_call(
        functools.partial(project_kernel, group, own),
        out_shape=shapes,
        in_specs=[SMEM] + [ANY] * (len(blocks) + 1 + own),
        out_specs=[ANY] * 4 if own else ANY,
        scratch_shapes=[
            pltpu.VMEM((512, chunk), BF),
            pltpu.VMEM((512, 512), BF),
            pltpu.VMEM((chunk, 512), BF),
            DMA((4,)),
            DMA,
        ]
        + ([DMA, DMA((4, 8))] if own else [DMA]),
        compiler_params=LIMIT,
        cost_estimate=estimate(2 * 512 * 512 * chunk, 512 * chunk * 2 + 512 * 1024 + chunk * 1024),
    )(where, *blocks, basis, *([other] if own else []))


def add_kernel(group, where, a, b, c, d, *refs):
    outs, total, sem = refs[:4], refs[4], refs[5]
    piece = GROUPS[group][1]
    total[...] = (
        (a[...].astype(F32) + b[...].astype(F32)) + (c[...].astype(F32) + d[...].astype(F32))
    ).astype(BF)
    copies = []
    for j in range(4):
        at = (place(where, "v%d" % group) + j) % 4
        copies.append(pltpu.make_async_copy(total.at[rows_at(at * piece, piece), :], outs[j], sem.at[j]))
    wait_all(start_all(copies))


def add_up(group, where, arrays):
    chunk, piece = GROUPS[group]
    return pl.pallas_call(
        functools.partial(add_kernel, group),
        out_shape=[pltpu.HBM((piece, 512), BF)] * 4,
        in_specs=[SMEM] + [VMEM] * 4,
        out_specs=[ANY] * 4,
        scratch_shapes=[pltpu.VMEM((chunk // 4, 512), BF), DMA((4,))],
        compiler_params=LIMIT,
        cost_estimate=estimate(3 * chunk * 128, 5 * chunk * 256),
    )(where, *arrays)


def moments_kernel(where, first, second, new, old, result, half, old_held, out, sem):
    core = place(where, "core")
    columns = pl.ds(pl.multiple_of(core * 256, 256), 256)
    copies = start_all([pltpu.make_async_copy(new.at[:, columns], half, sem.at[0]), pltpu.make_async_copy(old, old_held, sem.at[1])])
    left = lax.broadcasted_iota(jnp.int32, (64, 128), 1) < 64
    for q in range(8):
        for ref, begin in ((first, 0), (second, 128)):
            one = ref[:, q * 128 : q * 128 + 128]
            two = ref[:, 1024 + q // 2 * 128 : 1152 + q // 2 * 128]
            if q % 2:
                two = pltpu.roll(two, 64, 1)
            two = jnp.where(left, two, pltpu.roll(ref[:, 1536:1664], (192 - q * 16) % 128, 1))
            for i, value in enumerate((one, two)):
                high = value.astype(BF)
                out[q, begin : begin + 64, i * 128 : i * 128 + 128] = high
                if begin == 0:
                    out[q, 64:128, i * 128 : i * 128 + 128] = (value - high.astype(F32)).astype(BF)
    wait_all(copies)
    margin = lax.dot_general(half[...], old_held[...], (((0,), (0,)), ((), ())), preferred_element_type=F32)
    margin = margin.astype(BF)
    for q in range(8):
        for i in range(2):
            out[q, 192 + 32 * i : 224 + 32 * i, :] = margin[q * 32 : q * 32 + 32, i * 256 : i * 256 + 256]
    wait_all(start_all([pltpu.make_async_copy(out, result, sem.at[2])]))


def cut_moments(where, first, second, new, old):
    return pl.pallas_call(
        moments_kernel,
        out_shape=pltpu.HBM((8, 256, 256), BF),
        in_specs=[SMEM, VMEM, VMEM, ANY, ANY],
        out_specs=ANY,
        scratch_shapes=[
            pltpu.VMEM((2048, 256), BF),
            pltpu.VMEM((2048, 512), BF),
            pltpu.VMEM((8, 256, 256), BF),
            DMA((3,)),
        ],
        compiler_params=LIMIT,
        cost_estimate=estimate(2 * 2048 * 256 * 512, 6 * 2**20),
        name="cut_moments",
    )(where, first, second, new, old)


def margin_kernel(moments, out, held, sem):
    copy = pltpu.make_async_copy(moments.at[:, pl.ds(192, 64), :], held, sem)
    copy.start()
    copy.wait()
    total = held[0].astype(F32)
    for i in range(1, 8):
        total = total + held[i].astype(F32)
    total = total.astype(BF)
    for i in range(8):
        out[i, :, 0:256] = total[:32]
        out[i, :, 256:512] = total[32:]


def sum_margin(moments):
    return pl.pallas_call(
        margin_kernel,
        out_shape=jax.ShapeDtypeStruct((8, 32, 512), BF),
        in_specs=[ANY],
        out_specs=VMEM,
        scratch_shapes=[pltpu.VMEM((8, 64, 256), BF), DMA],
        compiler_params=LIMIT,
        cost_estimate=estimate(8 * 64 * 256, 2**19),
        name="sum_margin",
    )(moments)


def step_kernel(where, *refs):
    sums, (own, other, moments), lows = refs[:8], refs[8:11], refs[11:13]
    first_out, second_out, margin = refs[13:]
    core = place(where, "core")
    margin[rows_at(core * 256, 256), :] = own[...]
    margin[rows_at(256 - core * 256, 256), :] = other[...]
    projected = jnp.concatenate(
        [sum(ref[...].astype(F32) for ref in sums[4 * g : 4 * g + 4]) for g in range(2)], axis=0
    )
    contract = (((0,), (1,)), ((), ()))
    one, one_low, two = (moments[:, i * 64 : i * 64 + 64, :].reshape(512, 256) for i in range(3))
    rotated_one = lax.dot_general(one, margin[...], contract, preferred_element_type=F32)
    rotated_one = rotated_one + lax.dot_general(one_low, margin[...], contract, preferred_element_type=F32)
    wide = margin[...].astype(F32)
    rotated_two = lax.dot_general(two, (wide * wide).astype(BF), contract, preferred_element_type=F32)
    first_new = 0.9 * rotated_one[:208] + 0.1 * projected
    second_new = 0.999 * rotated_two[:208] + 0.001 * projected * projected
    low_step = (
        first_new / (1.0 - 0.9**STEP) / (jnp.sqrt(second_new / (1.0 - 0.999**STEP)) + 1e-08)
    ).astype(BF)
    begin = 0
    for ref in lows:
        ref[...] = low_step[begin : begin + ref.shape[0], :]
        begin += ref.shape[0]
    first_out[...] = first_new
    second_out[...] = second_new


def take_step(where, sums, *rest):
    return pl.pallas_call(
        step_kernel,
        out_shape=[jax.ShapeDtypeStruct((piece, 512), BF) for _, piece in GROUPS]
        + [jax.ShapeDtypeStruct((208, 512), F32)] * 2,
        in_specs=[SMEM] + [VMEM] * 11,
        out_specs=[VMEM] * 4,
        scratch_shapes=[pltpu.VMEM((512, 512), BF)],
        compiler_params=LIMIT,
        cost_estimate=estimate(6 * 208 * 512 * 512, 4 * 2**20),
        name="step",
    )(where, *sums, *rest)


def turn_kernel(first, second, result, wide, out, sem):
    wide[208:, :] = jnp.zeros((48, 512), F32)
    for i, ref in enumerate((first, second)):
        wide[:208, :] = ref[...]
        out[:, i * 64 : i * 64 + 64, :] = wide[...].T.astype(BF).reshape(8, 64, 256)
    wait_all(start_all([pltpu.make_async_copy(out, result, sem)]))


def turn_back(first, second):
    return pl.pallas_call(
        turn_kernel,
        out_shape=pltpu.HBM((8, 128, 256), BF),
        in_specs=[VMEM] * 2,
        out_specs=ANY,
        scratch_shapes=[pltpu.VMEM((256, 512), F32), pltpu.VMEM((8, 128, 256), BF), DMA],
        compiler_params=LIMIT,
        cost_estimate=estimate(208 * 1024, 3 * 2**19),
        name="turn_back",
    )(first, second)


def finish_kernel(new, *outs):
    lane = lax.broadcasted_iota(jnp.int32, (64, 128), 1)
    for i, out in enumerate(outs):
        rest = []
        for q in range(8):
            block = new[q, i * 64 : i * 64 + 64, :].astype(F32)
            out[:, q * 128 : q * 128 + 128] = block[:, :128]
            rest.append(block[:, 128:])
        for j in range(4):
            out[:, 1024 + j * 128 : 1152 + j * 128] = jnp.where(lane < 64, rest[2 * j], pltpu.roll(rest[2 * j + 1], 64, 1))
        last = pltpu.roll(rest[0], 64, 1)
        for q in range(1, 8):
            last = jnp.where(lane // 16 == q, pltpu.roll(rest[q], (64 + q * 16) % 128, 1) if q != 4 else rest[q], last)
        out[:, 1536:1664] = last


def finish(new):
    return pl.pallas_call(
        finish_kernel,
        out_shape=[jax.ShapeDtypeStruct((64, 1664), F32)] * 2,
        in_specs=[VMEM],
        out_specs=[VMEM] * 2,
        compiler_params=LIMIT,
        cost_estimate=estimate(64 * 1664 * 4, 3 * 2**19),
        name="finish",
    )(new)


def join_kernel(group, where, *refs):
    arrays, out = refs[:4], refs[4]
    piece = GROUPS[group][1]
    for j in range(4):
        at = (place(where, "v%d" % group) + 4 - j) % 4
        out[rows_at(at * piece, piece), :] = arrays[j][...]


def join(group, where, arrays):
    chunk = GROUPS[group][0]
    return pl.pallas_call(
        functools.partial(join_kernel, group),
        out_shape=jax.ShapeDtypeStruct((chunk // 4, 512), BF),
        in_specs=[SMEM] + [VMEM] * 4,
        out_specs=VMEM,
        compiler_params=LIMIT,
        cost_estimate=estimate(0, chunk * 512),
    )(where, *arrays)


def low_copies(group, where, arrays, begin, low, in_sem, core_of_arrays):
    if group == 0:
        u = jnp.where(core_of_arrays == 0, place(where, "x"), place(where, "y"))
    else:
        u = place(where, "u1")
    copies = []
    for j in range(4):
        done = 0
        at = (u + 4 - j) % 4
        for first, size in pieces(group, at):
            copies.append(
                pltpu.make_async_copy(
                    arrays[j].at[pl.ds(done, size), :], low.at[rows_at(begin + first, size), :], in_sem.at[at]
                )
            )
            done += size
    return copies


def update_kernel(ring, where, *refs):
    count = 5
    own, other, bases, outs = refs[:4], refs[4:8], refs[8 : 8 + count], refs[8 + count : 12 + count]
    low, base, held, in_sem, other_sem, base_sem, out_sem = refs[12 + count :]
    core = place(where, "core")
    width = WIDTH[ring]
    for k, step in enumerate(STEPS):
        if with_basis(ring, step):
            source = bases[STEPS.index((4 - step) % 4)].at[:, pl.ds(width, 512)]
        else:
            source = basis_rows(ring, where, step, bases[4])
        pltpu.make_async_copy(source, base.at[pl.ds(k * 128, 128), :], base_sem).start()
    if ring == "x":
        start_all(low_copies(1, where, own, core * 1280, low, in_sem, core))
        start_all(low_copies(1, where, other, (1 - core) * 1280, low, other_sem, 1 - core))
        for at in range(4):
            wait_for(low.at[pl.ds(0, 320), :], in_sem.at[at])
            wait_for(low.at[pl.ds(0, 320), :], other_sem.at[at])
    else:
        part_core = 0 if ring == "y" else 1
        for arrays, chosen in ((own, core == part_core), (other, core != part_core)):

            @pl.when(chosen)
            def _():
                start_all(low_copies(0, where, arrays, 0, low, in_sem, jnp.int32(part_core)))

    wait_for(base, base_sem)

    @pl.loop(0, width // 512)
    def _(i):
        columns = pl.ds(pl.multiple_of(i * 512, 512), 512)
        if ring != "x":
            wait_for(low.at[columns, :], in_sem.at[i])
        product = lax.dot_general(base[...], low[columns, :], (((1,), (1,)), ((), ())), preferred_element_type=F32)
        held[:, columns] = (8.0 * product).astype(BF)
        for k in range(4):
            pltpu.make_async_copy(
                held.at[pl.ds(k * 128, 128), columns], outs[k].at[:, columns], out_sem.at[k]
            ).start()

    for k in range(4):
        wait_for(held.at[pl.ds(k * 128, 128), :], out_sem.at[k])


def update_blocks(ring, where, arrays, bases):
    width = WIDTH[ring]
    return pl.pallas_call(
        functools.partial(update_kernel, ring),
        out_shape=blocks_of(4, (128, width)),
        in_specs=[SMEM] + [ANY] * (8 + len(bases)),
        out_specs=[ANY] * 4,
        scratch_shapes=[
            pltpu.VMEM((width, 512), BF),
            pltpu.VMEM((512, 512), BF),
            pltpu.VMEM((512, width), BF),
            DMA((4,)),
            DMA((4,)),
            DMA,
            DMA((4,)),
        ],
        compiler_params=LIMIT,
        cost_estimate=estimate(2 * 512 * 512 * width, 512 * width * 2 + 512 * 1024 + width * 1024),
    )(where, *arrays, *bases)


def exchange(blocks, rings):
    return [blocks[0]] + [shift(block, rings, step) for block, step in zip(blocks[1:], STEPS[1:])]


def ordered(arrays, rings):
    out = dict([(0, arrays[0])] + [(j, shift(arrays[j], rings, j)) for j in STEPS[1:]])
    return [out[j] for j in range(4)]


def compute(grad, basis_new, basis_old, moment_first, moment_second):
    xl, z, y, xh, core = (lax.axis_index(name).astype(jnp.int32) for name in NAMES)
    x = xh * 2 + xl
    spot = lax.broadcasted_iota(jnp.int32, (8,), 0)
    where = jnp.zeros((8,), jnp.int32)
    for i, value in enumerate((x, y, z, core, xh, jnp.where(core == 0, x, y), jnp.where(core == 0, z, x))):
        where = jnp.where(spot == i, value, where)

    arrived = {}
    for ring in ("x", "z", "y"):
        blocks = pack(ring, where, grad, basis_new)
        arrived[ring] = exchange(blocks, RINGS[ring])

    moments = cut_moments(where, moment_first, moment_second, basis_new, basis_old)
    moments = lax.all_to_all(moments, ROW, 0, 0, tiled=True)
    margin = sum_margin(moments)
    margin = lax.all_to_all(margin, ROW, 0, 0, tiled=True).reshape(256, 512)
    margin_other = shift(margin, RINGS["core"], 1)

    totals = {}
    for group, blocks in ((1, arrived["x"]), (0, arrived["y"] + arrived["z"])):
        other = project(group, where, blocks, basis_new)
        other = shift(other, RINGS["core"], 1)
        partial = project(group, where, blocks, basis_new, other)
        halves = ordered(partial, U[group])
        rest = add_up(group, where, halves)
        totals[group] = ordered(rest, V[group])

    *lows, first_new, second_new = take_step(where, totals[0] + totals[1], margin, margin_other, moments)

    sent = {}
    for group, rings in ((1, ("x",)), (0, ("y", "z"))):
        low = lows[group]
        quarters = ordered([low] * 4, V[group])
        quarter = join(group, where, quarters)
        whole = ordered([quarter] * 4, U[group])
        whole = whole + [shift(array, RINGS["core"], 1) for array in whole]
        for ring in rings:
            blocks = update_blocks(ring, where, whole, arrived[ring] + [basis_new])
            sent[ring] = exchange(blocks, RINGS[ring])
    update = None
    for ring in ("x", "y", "z"):
        update = unpack(ring, where, sent[ring], update, grad.shape[1])

    new = turn_back(first_new, second_new)
    new = lax.all_to_all(new, ROW, 0, 0, tiled=True)
    first, second = finish(new)
    return update, first, second


def solution(mesh):
    fine = Mesh(mesh.devices.reshape(SIZES), NAMES)
    col = ("y", "xh", "core")
    placed = (P(NAMES, None), P(ROW, None), P(ROW, None), P(ROW, col), P(ROW, col))
    return jax.shard_map(
        compute,
        mesh=fine,
        in_specs=placed,
        out_specs=(P(NAMES, None), P(ROW, col), P(ROW, col)),
        check_vma=False,
    )
```

```python
import functools
import itertools

import jax
import jax.numpy as jnp
from jax import lax
from jax.experimental import pallas as pl
from jax.experimental.pallas import tpu as pltpu
from jax.sharding import Mesh, PartitionSpec as P


STEP = 10
BF, F32 = jnp.bfloat16, jnp.float32
NAMES = ("xl", "z", "y", "xh", "core")
SIZES = (2, 4, 4, 2, 2)
ROW = ("xl", "z")
ANY = pl.BlockSpec(memory_space=pl.ANY)
SMEM = pl.BlockSpec(memory_space=pltpu.SMEM)
VMEM = pl.BlockSpec(memory_space=pltpu.VMEM)
HBM = pl.BlockSpec(memory_space=pltpu.HBM)
DMA = pltpu.SemaphoreType.DMA
LIMIT = pltpu.CompilerParams(vmem_limit_bytes=16 * 2**20)
ALL_OF_IT = pltpu.CompilerParams(vmem_limit_bytes=60 * 1024 * 1024)
MOST_OF_IT = pltpu.CompilerParams(vmem_limit_bytes=57 * 2**20)


def blocks_of(count, shape):
    return [pltpu.HBM(shape, BF)] + [jax.ShapeDtypeStruct(shape, BF)] * (count - 1)


STEPS = (0, 1, 3, 2)
WIDTH = {"y": 2048, "z": 2048, "x": 2560}
EXTRA = {"y": 0, "z": 512, "x": 512}


def with_basis(ring, step):
    return ring == "z" or (ring == "x" and step % 2 == 1)


GROUPS = ((2048, 128), (1280, 80))
TILE = (512, 640)
SLOT = {"x": 0, "y": 1, "z": 2, "core": 3, "xh": 4, "u0": 5, "v0": 6, "u1": 2, "v1": 1}
SPOTS = [dict(zip(NAMES, spot)) for spot in itertools.product(*(range(n) for n in SIZES))]


def place(where, axis):
    return where[SLOT[axis]]


def ring_shift(spot, ring, step):
    spot = dict(spot)
    if ring == "x":
        x = (spot["xh"] * 2 + spot["xl"] + step) % 4
        spot["xh"], spot["xl"] = x // 2, x % 2
    elif ring == "core":
        spot["core"] = 1 - spot["core"]
    else:
        spot[ring] = (spot[ring] + step) % 4
    return spot


def shift(array, rings, step):
    pairs = []
    for spot in SPOTS:
        target = ring_shift(spot, rings[spot["core"]], step)
        pairs.append((SPOTS.index(spot), SPOTS.index(target)))
    return lax.ppermute(array, NAMES, pairs)


RINGS = {ring: (ring, ring) for ring in ("x", "y", "z", "core")}
U = (("x", "y"), ("z", "z"))
V = (("z", "x"), ("y", "y"))


def runs(ring, at):
    out, done = [], 0
    if ring == "y":
        for xh in range(2):
            out.append((done, (at * 4 + xh * 2) * 1664, 1024))
            done += 1024
    elif ring == "z":
        for y, xh, xl in itertools.product(range(4), range(2), range(2)):
            out.append((done, (y * 4 + xh * 2 + 1) * 1664 + (xl * 4 + at) * 128, 128))
            done += 128
    else:
        xh, xl = at // 2, at % 2
        for core, y in itertools.product(range(2), range(4)):
            out.append((core * 1280 + y * 256, (y * 4 + xh * 2 + core) * 1664 + (8 + 2 * xl) * 128, 256))
    return out


def pieces(group, u_at):
    if group == 0:
        return [(u_at * 512, 512)]
    return [one for v in range(4) for one in ((v * 256 + u_at * 64, 64), (1024 + v * 64 + u_at * 16, 16))]


def rows_at(first, count):
    return pl.ds(pl.multiple_of(first, 16), count)


def estimate(flops, size):
    return pl.CostEstimate(flops=flops, bytes_accessed=size, transcendentals=0)


def start_all(copies):
    for copy in copies:
        copy.start()
    return copies


def wait_all(copies):
    for copy in copies:
        copy.wait()


def wait_for(ref, sem):
    pltpu.make_async_copy(ref, ref, sem).wait()


def turned(tile):
    return pltpu.roll(tile.astype(F32), 64, 1).astype(BF)


def pack_kernel(ring, where, grad, basis, *refs):
    outs, (held, in_sem, out_sem), more = refs[:4], refs[4:7], refs[7:]
    if ring == "x":
        ends, end_sem = more
        end_copies = start_all(
            [pltpu.make_async_copy(grad.at[:, pl.ds(b * 1664 + 1536, 128)], ends.at[b], end_sem.at[b]) for b in range(16)]
        )
    for at in range(4):
        start_all(
            [
                pltpu.make_async_copy(grad.at[:, pl.ds(source, count)], held.at[at, :, pl.ds(to, count)], in_sem.at[at])
                for to, source, count in runs(ring, at)
            ]
        )
        if EXTRA[ring]:
            rows = basis_rows("x", where, 0, basis)
            pltpu.make_async_copy(rows, held.at[at, :, pl.ds(WIDTH[ring], 512)], in_sem.at[at]).start()
    whole = held
    if ring == "x":
        wait_all(end_copies)
        left = lax.broadcasted_iota(jnp.int32, (128, 128), 1) < 64
        for xh, core, pair in itertools.product(range(2), range(2), range(2)):
            one, two = (ends[(2 * pair + i) * 4 + xh * 2 + core] for i in range(2))
            columns = pl.ds(core * 1280 + 1024 + pair * 128, 128)
            held[xh * 2, :, columns] = jnp.where(left, one, turned(two))
            held[xh * 2 + 1, :, columns] = jnp.where(left, turned(one), two)
        whole = held.at[:, :, pl.ds(0, 2560)]
    t = place(where, ring)
    stores = []
    for k, step in enumerate(STEPS):
        at = (t + step) % 4
        wait_for(whole.at[at], in_sem.at[at])
        source = held.at[at] if with_basis(ring, step) else held.at[at, :, pl.ds(0, WIDTH[ring])]
        copy = pltpu.make_async_copy(source, outs[k], out_sem.at[k])
        copy.start()
        stores.append(copy)
    wait_all(stores)


def pack(ring, where, grad, basis):
    width = WIDTH[ring] + EXTRA[ring]
    return pl.pallas_call(
        functools.partial(pack_kernel, ring),
        out_shape=[
            (jax.ShapeDtypeStruct if step else pltpu.HBM)((128, WIDTH[ring] + 512 * with_basis(ring, step)), BF)
            for step in STEPS
        ],
        in_specs=[SMEM, ANY, ANY],
        out_specs=[ANY] * 4,
        scratch_shapes=[pltpu.VMEM((4, 128, width), BF), DMA((4,)), DMA((4,))]
        + ([pltpu.VMEM((16, 128, 128), BF), DMA((16,))] if ring == "x" else []),
        compiler_params=ALL_OF_IT if ring == "x" else MOST_OF_IT,
        cost_estimate=estimate(0, 4 * 128 * width * 4),
    )(where, grad, basis)


def unpack_kernel(ring, where, *refs):
    blocks = refs[:4]
    if ring == "x":
        out, held, in_sem, out_sem, ends, end_sem = refs[-6:]
    else:
        out, held, in_sem, out_sem = refs[-4:]
    t = place(where, ring)
    if ring != "x":
        stores = []
        for k, step in enumerate(STEPS):
            for j, (to, source, count) in enumerate(runs(ring, (t + 4 - step) % 4)):
                columns = pl.ds(pl.multiple_of(source, 128), count)
                stores.append(pltpu.make_async_copy(blocks[k].at[:, pl.ds(to, count)], out.at[:, columns], out_sem.at[k, j]))
        wait_all(start_all(stores))
        return
    start_all(
        [
            pltpu.make_async_copy(blocks[k], held.at[(t + 4 - step) % 4], in_sem.at[(t + 4 - step) % 4])
            for k, step in enumerate(STEPS)
        ]
    )
    stores = []
    for at in range(4):
        wait_for(held.at[at], in_sem.at[at])
        stores += start_all(
            [
                pltpu.make_async_copy(held.at[at, :, pl.ds(to, count)], out.at[:, pl.ds(source, count)], out_sem.at[at, j])
                for j, (to, source, count) in enumerate(runs(ring, at))
            ]
        )
    if ring == "x":
        left = lax.broadcasted_iota(jnp.int32, (128, 128), 1) < 64
        for xh, core, pair in itertools.product(range(2), range(2), range(2)):
            columns = pl.ds(core * 1280 + 1024 + pair * 128, 128)
            one, two = held[xh * 2, :, columns], held[xh * 2 + 1, :, columns]
            block = 2 * pair * 4 + xh * 2 + core
            ends[block] = jnp.where(left, one, turned(two))
            ends[block + 4] = jnp.where(left, turned(one), two)
        stores += start_all(
            [pltpu.make_async_copy(ends.at[b], out.at[:, pl.ds(b * 1664 + 1536, 128)], end_sem.at[b]) for b in range(16)]
        )
    wait_all(stores)


def unpack(ring, where, blocks, before, columns):
    width = WIDTH[ring]
    more = [] if before is None else [before]
    return pl.pallas_call(
        functools.partial(unpack_kernel, ring),
        out_shape=jax.ShapeDtypeStruct((128, columns), BF),
        in_specs=[SMEM] + [ANY if ring == "x" else VMEM] * 4 + [ANY] * len(more),
        out_specs=ANY,
        scratch_shapes=[pltpu.VMEM((4, 128, width if ring == "x" else 128), BF), DMA((4,)), DMA((4, 16))]
        + ([pltpu.VMEM((16, 128, 128), BF), DMA((16,))] if ring == "x" else []),
        input_output_aliases={5: 0} if more else {},
        compiler_params=LIMIT,
        cost_estimate=estimate(0, 4 * 128 * width * 4),
    )(where, *blocks, *more)


def basis_rows(ring, where, step, base):
    y, xh, core = place(where, "y"), place(where, "xh"), place(where, "core")
    if ring == "y":
        y = (y + step) % 4
    elif step % 4 == 2:
        xh = 1 - xh
    return base.at[pl.ds(pl.multiple_of((y * 4 + xh * 2 + core) * 128, 128), 128), :]


def start_basis(ring, where, blocks, basis, base, base_sem):
    for k, step in enumerate(STEPS):
        if with_basis(ring, step):
            source = blocks[k].at[:, pl.ds(WIDTH[ring], 512)]
        else:
            source = basis_rows(ring, where, 4 - step, basis)
        pltpu.make_async_copy(source, base.at[pl.ds(k * 128, 128), :], base_sem).start()


def project_kernel(group, own, where, *refs):
    count = 8 if group == 0 else 4
    blocks, basis, refs = refs[:count], refs[count], refs[count + 1 :]
    if own:
        other, gathered, outs, (base, total, base_sem, out_sem) = refs[0], refs[1], refs[2:6], refs[6:]
    else:
        total, gathered, base, gather, base_sem, out_sem = refs
    chunk, tile = GROUPS[group][0], TILE[group]
    core = place(where, "core")

    def multiply(mine, base, first):
        @pl.loop(0, chunk // tile)
        def _(i):
            some = pl.ds(pl.multiple_of(i * tile, tile), tile)
            columns = pl.ds(pl.multiple_of(first + i * tile, 128), tile)
            block = jnp.concatenate([ref[:, columns] for ref in mine], axis=0)
            product = lax.dot_general(block, base[...], (((0,), (0,)), ((), ())), preferred_element_type=F32)
            if own:
                product = product + other[some, :].astype(F32)
            total[some, :] = product.astype(BF)

    if own:
        if group == 0:

            @pl.when(core == 0)
            def _():
                start_basis("y", where, blocks[:4], basis, base, base_sem)
                wait_for(base, base_sem)
                multiply(blocks[:4], base, 0)

            @pl.when(core == 1)
            def _():
                wait_all(start_all([pltpu.make_async_copy(gathered, base, base_sem)]))
                multiply(blocks[4:], base, 0)

        else:
            wait_all(start_all([pltpu.make_async_copy(gathered, base, base_sem)]))
            multiply(blocks, base, core * chunk)
    else:
        ring, mine = ("z", blocks[4:]) if group == 0 else ("x", blocks)
        start_basis(ring, where, mine, basis, gather, base_sem)
        wait_for(gather, base_sem)
        copy = pltpu.make_async_copy(gather, gathered, out_sem)
        copy.start()
        if group == 0:

            @pl.when(core == 1)
            def _():
                start_basis("y", where, blocks[:4], basis, base, base_sem)
                wait_for(base, base_sem)
                multiply(blocks[:4], base, 0)

            @pl.when(core == 0)
            def _():
                multiply(mine, gather, 0)

        else:
            multiply(mine, gather, (1 - core) * chunk)
        copy.wait()
        return
    stores = []
    for j in range(4):
        done = 0
        for i, (first, size) in enumerate(pieces(group, (place(where, "u%d" % group) + j) % 4)):
            stores.append(
                pltpu.make_async_copy(
                    total.at[rows_at(first, size), :], outs[j].at[pl.ds(done, size), :], out_sem.at[j, i]
                )
            )
            done += size
    wait_all(start_all(stores))


def project(group, where, blocks, basis, other=None, gathered=None):
    chunk = GROUPS[group][0]
    own = other is not None
    shapes = blocks_of(4, (chunk // 4, 512))
    if not own:
        shapes = [jax.ShapeDtypeStruct((chunk, 512), BF), pltpu.HBM((512, 512), BF)]
    return pl.pallas_call(
        functools.partial(project_kernel, group, own),
        out_shape=shapes,
        in_specs=[SMEM] + [VMEM] * len(blocks) + [ANY] + ([VMEM, ANY] if own else []),
        out_specs=[ANY] * 4 if own else [VMEM, ANY],
        scratch_shapes=[
            pltpu.VMEM((512, 512), BF),
            pltpu.VMEM((chunk if own else 512, 512), BF),
            DMA,
            DMA((4, 8)) if own else DMA,
        ],
        compiler_params=LIMIT,
        cost_estimate=estimate(2 * 512 * 512 * chunk, 512 * chunk * 2 + 512 * 1024 + chunk * 1024),
    )(where, *blocks, basis, *([other, gathered] if own else []))


def add_kernel(group, where, a, b, c, d, *refs):
    outs, total, sem = refs[:4], refs[4], refs[5]
    piece = GROUPS[group][1]
    total[...] = (
        (a[...].astype(F32) + b[...].astype(F32)) + (c[...].astype(F32) + d[...].astype(F32))
    ).astype(BF)
    copies = []
    for j in range(4):
        at = (place(where, "v%d" % group) + j) % 4
        copies.append(pltpu.make_async_copy(total.at[rows_at(at * piece, piece), :], outs[j], sem.at[j]))
    wait_all(start_all(copies))


def add_up(group, where, arrays):
    chunk, piece = GROUPS[group]
    return pl.pallas_call(
        functools.partial(add_kernel, group),
        out_shape=[pltpu.HBM((piece, 512), BF)] * 4,
        in_specs=[SMEM] + [VMEM] * 4,
        out_specs=[ANY] * 4,
        scratch_shapes=[pltpu.VMEM((chunk // 4, 512), BF), DMA((4,))],
        compiler_params=LIMIT,
        cost_estimate=estimate(3 * chunk * 128, 5 * chunk * 256),
    )(where, *arrays)


def moments_kernel(where, first, second, new, old, result, half, old_held, out, sem):
    core = place(where, "core")
    columns = pl.ds(pl.multiple_of(core * 256, 256), 256)
    copies = start_all([pltpu.make_async_copy(new.at[:, columns], half, sem.at[0]), pltpu.make_async_copy(old, old_held, sem.at[1])])
    left = lax.broadcasted_iota(jnp.int32, (64, 128), 1) < 64
    for q in range(8):
        for ref, begin in ((first, 0), (second, 128)):
            one = ref[:, q * 128 : q * 128 + 128]
            two = ref[:, 1024 + q // 2 * 128 : 1152 + q // 2 * 128]
            if q % 2:
                two = pltpu.roll(two, 64, 1)
            two = jnp.where(left, two, pltpu.roll(ref[:, 1536:1664], (192 - q * 16) % 128, 1))
            for i, value in enumerate((one, two)):
                high = value.astype(BF)
                out[q, begin : begin + 64, i * 128 : i * 128 + 128] = high
                if begin == 0:
                    out[q, 64:128, i * 128 : i * 128 + 128] = (value - high.astype(F32)).astype(BF)
    wait_all(copies)
    margin = lax.dot_general(half[...], old_held[...], (((0,), (0,)), ((), ())), preferred_element_type=F32)
    margin = margin.astype(BF)
    for q in range(8):
        for i in range(2):
            out[q, 192 + 32 * i : 224 + 32 * i, :] = margin[q * 32 : q * 32 + 32, i * 256 : i * 256 + 256]
    wait_all(start_all([pltpu.make_async_copy(out, result, sem.at[2])]))


def cut_moments(where, first, second, new, old):
    return pl.pallas_call(
        moments_kernel,
        out_shape=pltpu.HBM((8, 256, 256), BF),
        in_specs=[SMEM, VMEM, VMEM, ANY, ANY],
        out_specs=ANY,
        scratch_shapes=[
            pltpu.VMEM((2048, 256), BF),
            pltpu.VMEM((2048, 512), BF),
            pltpu.VMEM((8, 256, 256), BF),
            DMA((3,)),
        ],
        compiler_params=LIMIT,
        cost_estimate=estimate(2 * 2048 * 256 * 512, 6 * 2**20),
        name="cut_moments",
    )(where, first, second, new, old)


def margin_kernel(moments, out, held, sem):
    copy = pltpu.make_async_copy(moments.at[:, pl.ds(192, 64), :], held, sem)
    copy.start()
    copy.wait()
    total = held[0].astype(F32)
    for i in range(1, 8):
        total = total + held[i].astype(F32)
    total = total.astype(BF)
    for i in range(8):
        out[i, :, 0:256] = total[:32]
        out[i, :, 256:512] = total[32:]


def sum_margin(moments):
    return pl.pallas_call(
        margin_kernel,
        out_shape=jax.ShapeDtypeStruct((8, 32, 512), BF),
        in_specs=[ANY],
        out_specs=VMEM,
        scratch_shapes=[pltpu.VMEM((8, 64, 256), BF), DMA],
        compiler_params=LIMIT,
        cost_estimate=estimate(8 * 64 * 256, 2**19),
        name="sum_margin",
    )(moments)


def step_kernel(where, *refs):
    sums, (own, other, moments), lows = refs[:8], refs[8:11], refs[11:13]
    first_out, second_out, margin = refs[13:]
    core = place(where, "core")
    margin[rows_at(core * 256, 256), :] = own[...]
    margin[rows_at(256 - core * 256, 256), :] = other[...]
    projected = jnp.concatenate(
        [sum(ref[...].astype(F32) for ref in sums[4 * g : 4 * g + 4]) for g in range(2)], axis=0
    )
    contract = (((0,), (1,)), ((), ()))
    one, one_low, two = (moments[:, i * 64 : i * 64 + 64, :].reshape(512, 256) for i in range(3))
    rotated_one = lax.dot_general(one, margin[...], contract, preferred_element_type=F32)
    rotated_one = rotated_one + lax.dot_general(one_low, margin[...], contract, preferred_element_type=F32)
    wide = margin[...].astype(F32)
    rotated_two = lax.dot_general(two, (wide * wide).astype(BF), contract, preferred_element_type=F32)
    first_new = 0.9 * rotated_one[:208] + 0.1 * projected
    second_new = 0.999 * rotated_two[:208] + 0.001 * projected * projected
    low_step = (
        first_new / (1.0 - 0.9**STEP) / (jnp.sqrt(second_new / (1.0 - 0.999**STEP)) + 1e-08)
    ).astype(BF)
    begin = 0
    for ref in lows:
        ref[...] = low_step[begin : begin + ref.shape[0], :]
        begin += ref.shape[0]
    first_out[...] = first_new
    second_out[...] = second_new


def take_step(where, sums, *rest):
    return pl.pallas_call(
        step_kernel,
        out_shape=[jax.ShapeDtypeStruct((piece, 512), BF) for _, piece in GROUPS]
        + [jax.ShapeDtypeStruct((208, 512), F32)] * 2,
        in_specs=[SMEM] + [VMEM] * 11,
        out_specs=[VMEM] * 4,
        scratch_shapes=[pltpu.VMEM((512, 512), BF)],
        compiler_params=LIMIT,
        cost_estimate=estimate(6 * 208 * 512 * 512, 4 * 2**20),
        name="step",
    )(where, *sums, *rest)


def turn_kernel(first, second, result, wide, out, sem):
    wide[208:, :] = jnp.zeros((48, 512), F32)
    for i, ref in enumerate((first, second)):
        wide[:208, :] = ref[...]
        out[:, i * 64 : i * 64 + 64, :] = wide[...].T.astype(BF).reshape(8, 64, 256)
    wait_all(start_all([pltpu.make_async_copy(out, result, sem)]))


def turn_back(first, second):
    return pl.pallas_call(
        turn_kernel,
        out_shape=pltpu.HBM((8, 128, 256), BF),
        in_specs=[VMEM] * 2,
        out_specs=ANY,
        scratch_shapes=[pltpu.VMEM((256, 512), F32), pltpu.VMEM((8, 128, 256), BF), DMA],
        compiler_params=LIMIT,
        cost_estimate=estimate(208 * 1024, 3 * 2**19),
        name="turn_back",
    )(first, second)


def finish_kernel(new, *outs):
    lane = lax.broadcasted_iota(jnp.int32, (64, 128), 1)
    for i, out in enumerate(outs):
        rest = []
        for q in range(8):
            block = new[q, i * 64 : i * 64 + 64, :].astype(F32)
            out[:, q * 128 : q * 128 + 128] = block[:, :128]
            rest.append(block[:, 128:])
        for j in range(4):
            out[:, 1024 + j * 128 : 1152 + j * 128] = jnp.where(lane < 64, rest[2 * j], pltpu.roll(rest[2 * j + 1], 64, 1))
        last = pltpu.roll(rest[0], 64, 1)
        for q in range(1, 8):
            last = jnp.where(lane // 16 == q, pltpu.roll(rest[q], (64 + q * 16) % 128, 1) if q != 4 else rest[q], last)
        out[:, 1536:1664] = last


def finish(new):
    return pl.pallas_call(
        finish_kernel,
        out_shape=[jax.ShapeDtypeStruct((64, 1664), F32)] * 2,
        in_specs=[VMEM],
        out_specs=[VMEM] * 2,
        compiler_params=LIMIT,
        cost_estimate=estimate(64 * 1664 * 4, 3 * 2**19),
        name="finish",
    )(new)


def join_kernel(group, where, *refs):
    arrays, out = refs[:4], refs[4]
    piece = GROUPS[group][1]
    for j in range(4):
        at = (place(where, "v%d" % group) + 4 - j) % 4
        out[rows_at(at * piece, piece), :] = arrays[j][...]


def join(group, where, arrays):
    chunk = GROUPS[group][0]
    return pl.pallas_call(
        functools.partial(join_kernel, group),
        out_shape=jax.ShapeDtypeStruct((chunk // 4, 512), BF),
        in_specs=[SMEM] + [VMEM] * 4,
        out_specs=VMEM,
        compiler_params=LIMIT,
        cost_estimate=estimate(0, chunk * 512),
    )(where, *arrays)


def low_copies(group, where, arrays, begin, low, in_sem, core_of_arrays):
    if group == 0:
        u = jnp.where(core_of_arrays == 0, place(where, "x"), place(where, "y"))
    else:
        u = place(where, "u1")
    copies = []
    for j in range(4):
        done = 0
        at = (u + 4 - j) % 4
        for first, size in pieces(group, at):
            copies.append(
                pltpu.make_async_copy(
                    arrays[j].at[pl.ds(done, size), :], low.at[rows_at(begin + first, size), :], in_sem.at[at]
                )
            )
            done += size
    return copies


def update_kernel(ring, where, *refs):
    own, other, basis, outs = refs[:4], refs[4:8], refs[8], refs[9:13]
    low, base, held, in_sem, other_sem, base_sem, out_sem = refs[13:]
    core = place(where, "core")
    width = WIDTH[ring]
    for k, step in enumerate(STEPS):
        if ring == "y":
            source = basis_rows(ring, where, step, basis)
        else:
            source = basis.at[pl.ds(STEPS.index((4 - step) % 4) * 128, 128), :]
        pltpu.make_async_copy(source, base.at[pl.ds(k * 128, 128), :], base_sem).start()
    if ring == "x":
        start_all(low_copies(1, where, own, core * 1280, low, in_sem, core))
        start_all(low_copies(1, where, other, (1 - core) * 1280, low, other_sem, 1 - core))
        for at in range(4):
            wait_for(low.at[pl.ds(0, 320), :], in_sem.at[at])
            wait_for(low.at[pl.ds(0, 320), :], other_sem.at[at])
    else:
        part_core = 0 if ring == "y" else 1
        for arrays, chosen in ((own, core == part_core), (other, core != part_core)):

            @pl.when(chosen)
            def _():
                start_all(low_copies(0, where, arrays, 0, low, in_sem, jnp.int32(part_core)))

    wait_for(base, base_sem)

    @pl.loop(0, width // 512)
    def _(i):
        columns = pl.ds(pl.multiple_of(i * 512, 512), 512)
        if ring != "x":
            wait_for(low.at[columns, :], in_sem.at[i])
        product = lax.dot_general(base[...], low[columns, :], (((1,), (1,)), ((), ())), preferred_element_type=F32)
        held[:, columns] = (8.0 * product).astype(BF)
        for k in range(4):
            pltpu.make_async_copy(
                held.at[pl.ds(k * 128, 128), columns], outs[k].at[:, columns], out_sem.at[k]
            ).start()

    for k in range(4):
        wait_for(held.at[pl.ds(k * 128, 128), :], out_sem.at[k])


def update_blocks(ring, where, arrays, basis):
    width = WIDTH[ring]
    return pl.pallas_call(
        functools.partial(update_kernel, ring),
        out_shape=blocks_of(4, (128, width)),
        in_specs=[SMEM] + [ANY] * 9,
        out_specs=[ANY] * 4,
        scratch_shapes=[
            pltpu.VMEM((width, 512), BF),
            pltpu.VMEM((512, 512), BF),
            pltpu.VMEM((512, width), BF),
            DMA((4,)),
            DMA((4,)),
            DMA,
            DMA((4,)),
        ],
        compiler_params=LIMIT,
        cost_estimate=estimate(2 * 512 * 512 * width, 512 * width * 2 + 512 * 1024 + width * 1024),
    )(where, *arrays, basis)


def exchange(blocks, rings):
    return [blocks[0]] + [shift(block, rings, step) for block, step in zip(blocks[1:], STEPS[1:])]


def ordered(arrays, rings):
    out = dict([(0, arrays[0])] + [(j, shift(arrays[j], rings, j)) for j in STEPS[1:]])
    return [out[j] for j in range(4)]


def compute(grad, basis_new, basis_old, moment_first, moment_second):
    xl, z, y, xh, core = (lax.axis_index(name).astype(jnp.int32) for name in NAMES)
    x = xh * 2 + xl
    spot = lax.broadcasted_iota(jnp.int32, (8,), 0)
    where = jnp.zeros((8,), jnp.int32)
    for i, value in enumerate((x, y, z, core, xh, jnp.where(core == 0, x, y), jnp.where(core == 0, z, x))):
        where = jnp.where(spot == i, value, where)

    arrived = {}
    for ring in ("x", "z", "y"):
        blocks = pack(ring, where, grad, basis_new)
        arrived[ring] = exchange(blocks, RINGS[ring])

    moments = cut_moments(where, moment_first, moment_second, basis_new, basis_old)
    moments = lax.all_to_all(moments, ROW, 0, 0, tiled=True)
    margin = sum_margin(moments)
    margin = lax.all_to_all(margin, ROW, 0, 0, tiled=True).reshape(256, 512)
    margin_other = shift(margin, RINGS["core"], 1)

    totals, gathered = {}, {"y": basis_new}
    for group, blocks in ((1, arrived["x"]), (0, arrived["y"] + arrived["z"])):
        other, rows = project(group, where, blocks, basis_new)
        gathered["z" if group == 0 else "x"] = rows
        other = shift(other, RINGS["core"], 1)
        partial = project(group, where, blocks, basis_new, other, rows)
        halves = ordered(partial, U[group])
        rest = add_up(group, where, halves)
        totals[group] = ordered(rest, V[group])

    *lows, first_new, second_new = take_step(where, totals[0] + totals[1], margin, margin_other, moments)

    sent = {}
    for group, rings in ((1, ("x",)), (0, ("y", "z"))):
        low = lows[group]
        quarters = ordered([low] * 4, V[group])
        quarter = join(group, where, quarters)
        whole = ordered([quarter] * 4, U[group])
        whole = whole + [shift(array, RINGS["core"], 1) for array in whole]
        for ring in rings:
            blocks = update_blocks(ring, where, whole, gathered[ring])
            sent[ring] = exchange(blocks, RINGS[ring])
    update = None
    for ring in ("x", "y", "z"):
        update = unpack(ring, where, sent[ring], update, grad.shape[1])

    new = turn_back(first_new, second_new)
    new = lax.all_to_all(new, ROW, 0, 0, tiled=True)
    first, second = finish(new)
    return update, first, second


def solution(mesh):
    fine = Mesh(mesh.devices.reshape(SIZES), NAMES)
    col = ("y", "xh", "core")
    placed = (P(NAMES, None), P(ROW, None), P(ROW, None), P(ROW, col), P(ROW, col))
    return jax.shard_map(
        compute,
        mesh=fine,
        in_specs=placed,
        out_specs=(P(NAMES, None), P(ROW, col), P(ROW, col)),
        check_vma=False,
    )
```

```python
import functools
import itertools

import jax
import jax.numpy as jnp
from jax import lax
from jax.experimental import pallas as pl
from jax.experimental.pallas import tpu as pltpu
from jax.sharding import Mesh, PartitionSpec as P


STEP = 10
BF, F32 = jnp.bfloat16, jnp.float32
NAMES = ("xl", "z", "y", "xh", "core")
SIZES = (2, 4, 4, 2, 2)
ROW = ("xl", "z")
ANY = pl.BlockSpec(memory_space=pl.ANY)
SMEM = pl.BlockSpec(memory_space=pltpu.SMEM)
VMEM = pl.BlockSpec(memory_space=pltpu.VMEM)
HBM = pl.BlockSpec(memory_space=pltpu.HBM)
DMA = pltpu.SemaphoreType.DMA
LIMIT = pltpu.CompilerParams(vmem_limit_bytes=16 * 2**20)


def blocks_of(count, shape):
    return [pltpu.HBM(shape, BF)] + [jax.ShapeDtypeStruct(shape, BF)] * (count - 1)


STEPS = (0, 1, 3, 2)
WIDTH = {"y": 2048, "z": 2048, "x": 2560}
EXTRA = {"y": 0, "z": 512, "x": 512}


def with_basis(ring, step):
    return ring == "z" or (ring == "x" and step % 2 == 1)


GROUPS = ((2048, 128), (1280, 80))
TILE = (512, 640)
SLOT = {"x": 0, "y": 1, "z": 2, "core": 3, "xh": 4, "u0": 5, "v0": 6, "u1": 2, "v1": 1}
SPOTS = [dict(zip(NAMES, spot)) for spot in itertools.product(*(range(n) for n in SIZES))]


def place(where, axis):
    return where[SLOT[axis]]


def ring_shift(spot, ring, step):
    spot = dict(spot)
    if ring == "x":
        x = (spot["xh"] * 2 + spot["xl"] + step) % 4
        spot["xh"], spot["xl"] = x // 2, x % 2
    elif ring == "core":
        spot["core"] = 1 - spot["core"]
    else:
        spot[ring] = (spot[ring] + step) % 4
    return spot


def shift(array, rings, step):
    pairs = []
    for spot in SPOTS:
        target = ring_shift(spot, rings[spot["core"]], step)
        pairs.append((SPOTS.index(spot), SPOTS.index(target)))
    return lax.ppermute(array, NAMES, pairs)


RINGS = {ring: (ring, ring) for ring in ("x", "y", "z", "core")}
U = (("x", "y"), ("z", "z"))
V = (("z", "x"), ("y", "y"))


def runs(ring, at):
    out, done = [], 0
    if ring == "y":
        for xh in range(2):
            out.append((done, (at * 4 + xh * 2) * 1664, 1024))
            done += 1024
    elif ring == "z":
        for y, xh, xl in itertools.product(range(4), range(2), range(2)):
            out.append((done, (y * 4 + xh * 2 + 1) * 1664 + (xl * 4 + at) * 128, 128))
            done += 128
    else:
        xh, xl = at // 2, at % 2
        for core, y in itertools.product(range(2), range(4)):
            out.append((core * 1280 + y * 256, (y * 4 + xh * 2 + core) * 1664 + (8 + 2 * xl) * 128, 256))
    return out


def pieces(group, u_at):
    if group == 0:
        return [(u_at * 512, 512)]
    return [one for v in range(4) for one in ((v * 256 + u_at * 64, 64), (1024 + v * 64 + u_at * 16, 16))]


def in_hbm(array):
    return pltpu.with_memory_space_constraint(array, pltpu.HBM)


def rows_at(first, count):
    return pl.ds(pl.multiple_of(first, 16), count)


def estimate(flops, size):
    return pl.CostEstimate(flops=flops, bytes_accessed=size, transcendentals=0)


def start_all(copies):
    for copy in copies:
        copy.start()
    return copies


def wait_all(copies):
    for copy in copies:
        copy.wait()


def wait_for(ref, sem):
    pltpu.make_async_copy(ref, ref, sem).wait()


def turned(tile):
    return pltpu.roll(tile.astype(F32), 64, 1).astype(BF)


def pack_kernel(ring, where, grad, basis, *refs):
    outs, (held, in_sem, out_sem), more = refs[:4], refs[4:7], refs[7:]
    if ring == "x":
        ends, end_sem = more
        end_copies = start_all(
            [pltpu.make_async_copy(grad.at[:, pl.ds(b * 1664 + 1536, 128)], ends.at[b], end_sem.at[b]) for b in range(16)]
        )
    for at in range(4):
        start_all(
            [
                pltpu.make_async_copy(grad.at[:, pl.ds(source, count)], held.at[at, :, pl.ds(to, count)], in_sem.at[at])
                for to, source, count in runs(ring, at)
            ]
        )
        if EXTRA[ring]:
            rows = basis_rows("x", where, 0, basis)
            pltpu.make_async_copy(rows, held.at[at, :, pl.ds(WIDTH[ring], 512)], in_sem.at[at]).start()
    whole = held
    if ring == "x":
        wait_all(end_copies)
        left = lax.broadcasted_iota(jnp.int32, (128, 128), 1) < 64
        for xh, core, pair in itertools.product(range(2), range(2), range(2)):
            one, two = (ends[(2 * pair + i) * 4 + xh * 2 + core] for i in range(2))
            columns = pl.ds(core * 1280 + 1024 + pair * 128, 128)
            held[xh * 2, :, columns] = jnp.where(left, one, turned(two))
            held[xh * 2 + 1, :, columns] = jnp.where(left, turned(one), two)
        whole = held.at[:, :, pl.ds(0, 2560)]
    t = place(where, ring)
    stores = []
    for k, step in enumerate(STEPS):
        at = (t + step) % 4
        wait_for(whole.at[at], in_sem.at[at])
        source = held.at[at] if with_basis(ring, step) else held.at[at, :, pl.ds(0, WIDTH[ring])]
        copy = pltpu.make_async_copy(source, outs[k], out_sem.at[k])
        copy.start()
        stores.append(copy)
    wait_all(stores)


def pack(ring, where, grad, basis):
    width = WIDTH[ring] + EXTRA[ring]
    return pl.pallas_call(
        functools.partial(pack_kernel, ring),
        out_shape=[
            (jax.ShapeDtypeStruct if step else pltpu.HBM)((128, WIDTH[ring] + 512 * with_basis(ring, step)), BF)
            for step in STEPS
        ],
        in_specs=[SMEM, ANY, ANY],
        out_specs=[ANY] * 4,
        scratch_shapes=[pltpu.VMEM((4, 128, width), BF), DMA((4,)), DMA((4,))]
        + ([pltpu.VMEM((16, 128, 128), BF), DMA((16,))] if ring == "x" else []),
        compiler_params=LIMIT,
        cost_estimate=estimate(0, 4 * 128 * width * 4),
    )(where, in_hbm(grad), basis)


def unpack_kernel(ring, where, *refs):
    blocks = refs[:4]
    if ring == "x":
        out, held, in_sem, out_sem, ends, end_sem = refs[-6:]
    else:
        out, held, in_sem, out_sem = refs[-4:]
    t = place(where, ring)
    if ring != "x":
        stores = []
        for k, step in enumerate(STEPS):
            for j, (to, source, count) in enumerate(runs(ring, (t + 4 - step) % 4)):
                columns = pl.ds(pl.multiple_of(source, 128), count)
                stores.append(pltpu.make_async_copy(blocks[k].at[:, pl.ds(to, count)], out.at[:, columns], out_sem.at[k, j]))
        wait_all(start_all(stores))
        return
    start_all(
        [
            pltpu.make_async_copy(blocks[k], held.at[(t + 4 - step) % 4], in_sem.at[(t + 4 - step) % 4])
            for k, step in enumerate(STEPS)
        ]
    )
    stores = []
    for at in range(4):
        wait_for(held.at[at], in_sem.at[at])
        stores += start_all(
            [
                pltpu.make_async_copy(held.at[at, :, pl.ds(to, count)], out.at[:, pl.ds(source, count)], out_sem.at[at, j])
                for j, (to, source, count) in enumerate(runs(ring, at))
            ]
        )
    if ring == "x":
        left = lax.broadcasted_iota(jnp.int32, (128, 128), 1) < 64
        for xh, core, pair in itertools.product(range(2), range(2), range(2)):
            columns = pl.ds(core * 1280 + 1024 + pair * 128, 128)
            one, two = held[xh * 2, :, columns], held[xh * 2 + 1, :, columns]
            block = 2 * pair * 4 + xh * 2 + core
            ends[block] = jnp.where(left, one, turned(two))
            ends[block + 4] = jnp.where(left, turned(one), two)
        stores += start_all(
            [pltpu.make_async_copy(ends.at[b], out.at[:, pl.ds(b * 1664 + 1536, 128)], end_sem.at[b]) for b in range(16)]
        )
    wait_all(stores)


def unpack(ring, where, blocks, before, columns):
    width = WIDTH[ring]
    more = [] if before is None else [before]
    return pl.pallas_call(
        functools.partial(unpack_kernel, ring),
        out_shape=jax.ShapeDtypeStruct((128, columns), BF),
        in_specs=[SMEM] + [ANY if ring == "x" else VMEM] * 4 + [ANY] * len(more),
        out_specs=ANY,
        scratch_shapes=[pltpu.VMEM((4, 128, width if ring == "x" else 128), BF), DMA((4,)), DMA((4, 16))]
        + ([pltpu.VMEM((16, 128, 128), BF), DMA((16,))] if ring == "x" else []),
        input_output_aliases={5: 0} if more else {},
        compiler_params=LIMIT,
        cost_estimate=estimate(0, 4 * 128 * width * 4),
    )(where, *blocks, *more)


def basis_rows(ring, where, step, base):
    y, xh, core = place(where, "y"), place(where, "xh"), place(where, "core")
    if ring == "y":
        y = (y + step) % 4
    elif step % 4 == 2:
        xh = 1 - xh
    return base.at[pl.ds(pl.multiple_of((y * 4 + xh * 2 + core) * 128, 128), 128), :]


def start_basis(ring, where, blocks, basis, base, base_sem):
    for k, step in enumerate(STEPS):
        if with_basis(ring, step):
            source = blocks[k].at[:, pl.ds(WIDTH[ring], 512)]
        else:
            source = basis_rows(ring, where, 4 - step, basis)
        pltpu.make_async_copy(source, base.at[pl.ds(k * 128, 128), :], base_sem).start()


def project_kernel(group, own, where, *refs):
    count = 8 if group == 0 else 4
    blocks, basis, refs = list(refs[:count]), refs[count], refs[count + 1 :]
    if own:
        other, gathered, outs, (base, total, mine, base_sem, out_sem, in_sem) = refs[0], refs[1], refs[2:6], refs[6:]
    else:
        total, gathered, base, gather, mine, base_sem, out_sem, in_sem = refs
    chunk, tile = GROUPS[group][0], TILE[group]
    core, u = place(where, "core"), place(where, "u%d" % group)

    def fetch(block, first):
        copy = pltpu.make_async_copy(block.at[:, pl.ds(pl.multiple_of(first, 128), chunk)], mine, in_sem)
        copy.start()
        return copy

    def multiply(far, base, first):
        @pl.loop(0, chunk // tile)
        def _(i):
            some = pl.ds(pl.multiple_of(i * tile, tile), tile)
            columns = pl.ds(pl.multiple_of(first + i * tile, 128), tile)
            block = jnp.concatenate([mine[:, some]] + [ref[:, columns] for ref in far], axis=0)
            product = lax.dot_general(block, base[...], (((0,), (0,)), ((), ())), preferred_element_type=F32)
            if own:
                product = product + other[some, :].astype(F32)
            total[some, :] = product.astype(BF)
            if own and group == 0:
                for j in range(4):

                    @pl.when((u + j) % 4 == i)
                    def _():
                        pltpu.make_async_copy(total.at[some, :], outs[j], out_sem.at[j]).start()

    def with_y():
        copy = fetch(blocks[0], 0)
        start_basis("y", where, blocks[:4], basis, base, base_sem)
        wait_for(base, base_sem)
        copy.wait()
        multiply(blocks[1:4], base, 0)

    if own:

        def with_gathered(four, first):
            copy = fetch(four[0], first)
            wait_all(start_all([pltpu.make_async_copy(gathered, base, base_sem)]))
            copy.wait()
            multiply(four[1:], base, first)

        if group == 0:
            pl.when(core == 0)(with_y)
            pl.when(core == 1)(lambda: with_gathered(blocks[4:], 0))
            for j in range(4):
                wait_for(outs[j], out_sem.at[j])
            return
        with_gathered(blocks, core * chunk)
    else:
        ring, four = ("z", blocks[4:]) if group == 0 else ("x", blocks)
        start_basis(ring, where, four, basis, gather, base_sem)

        def with_gather(first):
            fetch(four[0], first).wait()
            multiply(four[1:], gather, first)

        wait_for(gather, base_sem)
        out_copy = pltpu.make_async_copy(gather, gathered, out_sem)
        out_copy.start()
        if group == 0:
            pl.when(core == 1)(with_y)
            pl.when(core == 0)(lambda: with_gather(0))
        else:
            with_gather((1 - core) * chunk)
        out_copy.wait()
        return
    stores = []
    for j in range(4):
        done = 0
        for first, size in pieces(group, (u + j) % 4):
            stores.append(
                pltpu.make_async_copy(total.at[rows_at(first, size), :], outs[j].at[pl.ds(done, size), :], out_sem.at[j])
            )
            done += size
    start_all(stores)
    for j in range(4):
        wait_for(outs[j], out_sem.at[j])


def project(group, where, blocks, basis, other=None, gathered=None):
    chunk = GROUPS[group][0]
    own = other is not None
    shapes = blocks_of(4, (chunk // 4, 512))
    if not own:
        shapes = [jax.ShapeDtypeStruct((chunk, 512), BF), pltpu.HBM((512, 512), BF)]
    return pl.pallas_call(
        functools.partial(project_kernel, group, own),
        out_shape=shapes,
        in_specs=[SMEM] + ([ANY] + [VMEM] * 3) * (len(blocks) // 4) + [ANY] + ([VMEM, ANY] if own else []),
        out_specs=[ANY] * 4 if own else [VMEM, ANY],
        scratch_shapes=[
            pltpu.VMEM((512, 512), BF),
            pltpu.VMEM((chunk if own else 512, 512), BF),
            pltpu.VMEM((128, chunk), BF),
            DMA,
            DMA((4,)) if own else DMA,
            DMA,
        ],
        compiler_params=LIMIT,
        cost_estimate=estimate(2 * 512 * 512 * chunk, 512 * chunk * 2 + 512 * 1024 + chunk * 1024),
    )(
        where,
        *(in_hbm(block) if i % 4 == 0 else block for i, block in enumerate(blocks)),
        basis,
        *([other, in_hbm(gathered)] if own else []),
    )


def add_kernel(group, where, mine, b, c, d, *refs):
    outs, total, a, sem, in_sem = refs[:4], refs[4], refs[5], refs[6], refs[7]
    piece = GROUPS[group][1]
    wait_all(start_all([pltpu.make_async_copy(mine, a, in_sem)]))
    total[...] = (
        (a[...].astype(F32) + b[...].astype(F32)) + (c[...].astype(F32) + d[...].astype(F32))
    ).astype(BF)
    copies = []
    for j in range(4):
        at = (place(where, "v%d" % group) + j) % 4
        copies.append(pltpu.make_async_copy(total.at[rows_at(at * piece, piece), :], outs[j], sem.at[j]))
    wait_all(start_all(copies))


def add_up(group, where, arrays):
    chunk, piece = GROUPS[group]
    return pl.pallas_call(
        functools.partial(add_kernel, group),
        out_shape=[pltpu.HBM((piece, 512), BF)] * 4,
        in_specs=[SMEM, ANY] + [VMEM] * 3,
        out_specs=[ANY] * 4,
        scratch_shapes=[pltpu.VMEM((chunk // 4, 512), BF)] * 2 + [DMA((4,)), DMA],
        compiler_params=LIMIT,
        cost_estimate=estimate(3 * chunk * 128, 5 * chunk * 256),
    )(where, in_hbm(arrays[0]), *arrays[1:])


def moments_kernel(where, first, second, new, old, result, half, old_held, out, sem):
    core = place(where, "core")
    columns = pl.ds(pl.multiple_of(core * 256, 256), 256)
    copies = start_all([pltpu.make_async_copy(new.at[:, columns], half, sem.at[0]), pltpu.make_async_copy(old, old_held, sem.at[1])])
    left = lax.broadcasted_iota(jnp.int32, (64, 128), 1) < 64
    for q in range(8):
        for ref, begin in ((first, 0), (second, 128)):
            one = ref[:, q * 128 : q * 128 + 128]
            two = ref[:, 1024 + q // 2 * 128 : 1152 + q // 2 * 128]
            if q % 2:
                two = pltpu.roll(two, 64, 1)
            two = jnp.where(left, two, pltpu.roll(ref[:, 1536:1664], (192 - q * 16) % 128, 1))
            for i, value in enumerate((one, two)):
                high = value.astype(BF)
                out[q, begin : begin + 64, i * 128 : i * 128 + 128] = high
                if begin == 0:
                    out[q, 64:128, i * 128 : i * 128 + 128] = (value - high.astype(F32)).astype(BF)
    wait_all(copies)
    margin = lax.dot_general(half[...], old_held[...], (((0,), (0,)), ((), ())), preferred_element_type=F32)
    margin = margin.astype(BF)
    for q in range(8):
        for i in range(2):
            out[q, 192 + 32 * i : 224 + 32 * i, :] = margin[q * 32 : q * 32 + 32, i * 256 : i * 256 + 256]
    wait_all(start_all([pltpu.make_async_copy(out, result, sem.at[2])]))


def cut_moments(where, first, second, new, old):
    return pl.pallas_call(
        moments_kernel,
        out_shape=pltpu.HBM((8, 256, 256), BF),
        in_specs=[SMEM, VMEM, VMEM, ANY, ANY],
        out_specs=ANY,
        scratch_shapes=[
            pltpu.VMEM((2048, 256), BF),
            pltpu.VMEM((2048, 512), BF),
            pltpu.VMEM((8, 256, 256), BF),
            DMA((3,)),
        ],
        compiler_params=LIMIT,
        cost_estimate=estimate(2 * 2048 * 256 * 512, 6 * 2**20),
        name="cut_moments",
    )(where, first, second, new, in_hbm(old))


def margin_kernel(moments, out, held, sem):
    copy = pltpu.make_async_copy(moments.at[:, pl.ds(192, 64), :], held, sem)
    copy.start()
    copy.wait()
    total = held[0].astype(F32)
    for i in range(1, 8):
        total = total + held[i].astype(F32)
    total = total.astype(BF)
    for i in range(8):
        out[i, :, 0:256] = total[:32]
        out[i, :, 256:512] = total[32:]


def sum_margin(moments):
    return pl.pallas_call(
        margin_kernel,
        out_shape=jax.ShapeDtypeStruct((8, 32, 512), BF),
        in_specs=[ANY],
        out_specs=VMEM,
        scratch_shapes=[pltpu.VMEM((8, 64, 256), BF), DMA],
        compiler_params=LIMIT,
        cost_estimate=estimate(8 * 64 * 256, 2**19),
        name="sum_margin",
    )(moments)


def step_kernel(where, *refs):
    sums, (own, other, moments), lows = refs[:8], refs[8:11], refs[11:13]
    first_out, second_out, margin, mine, in_sem = refs[13:]
    core = place(where, "core")
    copies = [
        pltpu.make_async_copy(sums[0], mine.at[pl.ds(0, 128), :], in_sem.at[0]),
        pltpu.make_async_copy(sums[4], mine.at[pl.ds(128, 80), :], in_sem.at[1]),
    ]
    start_all(copies)
    margin[rows_at(core * 256, 256), :] = own[...]
    margin[rows_at(256 - core * 256, 256), :] = other[...]
    contract = (((0,), (1,)), ((), ()))
    one, one_low, two = (moments[:, i * 64 : i * 64 + 64, :].reshape(512, 256) for i in range(3))
    rotated_one = lax.dot_general(one, margin[...], contract, preferred_element_type=F32)
    rotated_one = rotated_one + lax.dot_general(one_low, margin[...], contract, preferred_element_type=F32)
    wide = margin[...].astype(F32)
    rotated_two = lax.dot_general(two, (wide * wide).astype(BF), contract, preferred_element_type=F32)
    wait_all(copies)
    projected = mine[...].astype(F32) + jnp.concatenate(
        [sum(ref[...].astype(F32) for ref in sums[4 * g + 1 : 4 * g + 4]) for g in range(2)], axis=0
    )
    first_new = 0.9 * rotated_one[:208] + 0.1 * projected
    second_new = 0.999 * rotated_two[:208] + 0.001 * projected * projected
    low_step = (
        first_new / (1.0 - 0.9**STEP) / (jnp.sqrt(second_new / (1.0 - 0.999**STEP)) + 1e-08)
    ).astype(BF)
    begin = 0
    for ref in lows:
        ref[...] = low_step[begin : begin + ref.shape[0], :]
        begin += ref.shape[0]
    first_out[...] = first_new
    second_out[...] = second_new


def take_step(where, sums, *rest):
    return pl.pallas_call(
        step_kernel,
        out_shape=[jax.ShapeDtypeStruct((piece, 512), BF) for _, piece in GROUPS]
        + [jax.ShapeDtypeStruct((208, 512), F32)] * 2,
        in_specs=[SMEM] + ([ANY] + [VMEM] * 3) * 2 + [VMEM] * 3,
        out_specs=[VMEM] * 4,
        scratch_shapes=[pltpu.VMEM((512, 512), BF), pltpu.VMEM((208, 512), BF), DMA((2,))],
        compiler_params=LIMIT,
        cost_estimate=estimate(6 * 208 * 512 * 512, 4 * 2**20),
        name="step",
    )(where, in_hbm(sums[0]), *sums[1:4], in_hbm(sums[4]), *sums[5:], *rest)


def turn_kernel(first, second, result, wide, out, sem):
    wide[208:, :] = jnp.zeros((48, 512), F32)
    for i, ref in enumerate((first, second)):
        wide[:208, :] = ref[...]
        out[:, i * 64 : i * 64 + 64, :] = wide[...].T.astype(BF).reshape(8, 64, 256)
    wait_all(start_all([pltpu.make_async_copy(out, result, sem)]))


def turn_back(first, second):
    return pl.pallas_call(
        turn_kernel,
        out_shape=pltpu.HBM((8, 128, 256), BF),
        in_specs=[VMEM] * 2,
        out_specs=ANY,
        scratch_shapes=[pltpu.VMEM((256, 512), F32), pltpu.VMEM((8, 128, 256), BF), DMA],
        compiler_params=LIMIT,
        cost_estimate=estimate(208 * 1024, 3 * 2**19),
        name="turn_back",
    )(first, second)


def finish_kernel(new, *outs):
    lane = lax.broadcasted_iota(jnp.int32, (64, 128), 1)
    for i, out in enumerate(outs):
        rest = []
        for q in range(8):
            block = new[q, i * 64 : i * 64 + 64, :].astype(F32)
            out[:, q * 128 : q * 128 + 128] = block[:, :128]
            rest.append(block[:, 128:])
        for j in range(4):
            out[:, 1024 + j * 128 : 1152 + j * 128] = jnp.where(lane < 64, rest[2 * j], pltpu.roll(rest[2 * j + 1], 64, 1))
        last = pltpu.roll(rest[0], 64, 1)
        for q in range(1, 8):
            last = jnp.where(lane // 16 == q, pltpu.roll(rest[q], (64 + q * 16) % 128, 1) if q != 4 else rest[q], last)
        out[:, 1536:1664] = last


def finish(new):
    return pl.pallas_call(
        finish_kernel,
        out_shape=[jax.ShapeDtypeStruct((64, 1664), F32)] * 2,
        in_specs=[VMEM],
        out_specs=[VMEM] * 2,
        compiler_params=LIMIT,
        cost_estimate=estimate(64 * 1664 * 4, 3 * 2**19),
        name="finish",
    )(new)


def join_kernel(group, where, *refs):
    arrays, out = refs[:4], refs[4]
    piece = GROUPS[group][1]
    for j in range(4):
        at = (place(where, "v%d" % group) + 4 - j) % 4
        out[rows_at(at * piece, piece), :] = arrays[j][...]


def join(group, where, arrays):
    chunk = GROUPS[group][0]
    return pl.pallas_call(
        functools.partial(join_kernel, group),
        out_shape=jax.ShapeDtypeStruct((chunk // 4, 512), BF),
        in_specs=[SMEM] + [VMEM] * 4,
        out_specs=VMEM,
        compiler_params=LIMIT,
        cost_estimate=estimate(0, chunk * 512),
    )(where, *arrays)


def low_copies(group, where, arrays, begin, low, in_sem, core_of_arrays):
    if group == 0:
        u = jnp.where(core_of_arrays == 0, place(where, "x"), place(where, "y"))
    else:
        u = place(where, "u1")
    copies = []
    for j in range(4):
        done = 0
        at = (u + 4 - j) % 4
        for first, size in pieces(group, at):
            copies.append(
                pltpu.make_async_copy(
                    arrays[j].at[pl.ds(done, size), :], low.at[rows_at(begin + first, size), :], in_sem.at[at]
                )
            )
            done += size
    return copies


def update_kernel(ring, where, *refs):
    own, other, basis, outs = refs[:4], refs[4:8], refs[8], refs[9:13]
    low, base, held, in_sem, other_sem, base_sem, out_sem = refs[13:]
    core = place(where, "core")
    width = WIDTH[ring]
    for k, step in enumerate(STEPS):
        if ring == "y":
            source = basis_rows(ring, where, step, basis)
        else:
            source = basis.at[pl.ds(STEPS.index((4 - step) % 4) * 128, 128), :]
        pltpu.make_async_copy(source, base.at[pl.ds(k * 128, 128), :], base_sem).start()
    if ring == "x":
        start_all(low_copies(1, where, own, core * 1280, low, in_sem, core))
        start_all(low_copies(1, where, other, (1 - core) * 1280, low, other_sem, 1 - core))
        for at in range(4):
            wait_for(low.at[pl.ds(0, 320), :], in_sem.at[at])
            wait_for(low.at[pl.ds(0, 320), :], other_sem.at[at])
    else:
        part_core = 0 if ring == "y" else 1
        for arrays, chosen in ((own, core == part_core), (other, core != part_core)):

            @pl.when(chosen)
            def _():
                start_all(low_copies(0, where, arrays, 0, low, in_sem, jnp.int32(part_core)))

    wait_for(base, base_sem)

    @pl.loop(0, width // 512)
    def _(i):
        columns = pl.ds(pl.multiple_of(i * 512, 512), 512)
        if ring != "x":
            wait_for(low.at[columns, :], in_sem.at[i])
        product = lax.dot_general(base[...], low[columns, :], (((1,), (1,)), ((), ())), preferred_element_type=F32)
        held[:, columns] = (8.0 * product).astype(BF)
        for k in range(4):
            pltpu.make_async_copy(
                held.at[pl.ds(k * 128, 128), columns], outs[k].at[:, columns], out_sem.at[k]
            ).start()

    for k in range(4):
        wait_for(held.at[pl.ds(k * 128, 128), :], out_sem.at[k])


def update_blocks(ring, where, arrays, basis):
    width = WIDTH[ring]
    return pl.pallas_call(
        functools.partial(update_kernel, ring),
        out_shape=blocks_of(4, (128, width)),
        in_specs=[SMEM] + [ANY] * 9,
        out_specs=[ANY] * 4,
        scratch_shapes=[
            pltpu.VMEM((width, 512), BF),
            pltpu.VMEM((512, 512), BF),
            pltpu.VMEM((512, width), BF),
            DMA((4,)),
            DMA((4,)),
            DMA,
            DMA((4,)),
        ],
        compiler_params=LIMIT,
        cost_estimate=estimate(2 * 512 * 512 * width, 512 * width * 2 + 512 * 1024 + width * 1024),
    )(where, *arrays, basis if ring == "y" else in_hbm(basis))


def exchange(blocks, rings):
    return [blocks[0]] + [shift(block, rings, step) for block, step in zip(blocks[1:], STEPS[1:])]


def ordered(arrays, rings):
    out = dict([(0, arrays[0])] + [(j, shift(arrays[j], rings, j)) for j in STEPS[1:]])
    return [out[j] for j in range(4)]


def compute(grad, basis_new, basis_old, moment_first, moment_second):
    xl, z, y, xh, core = (lax.axis_index(name).astype(jnp.int32) for name in NAMES)
    x = xh * 2 + xl
    spot = lax.broadcasted_iota(jnp.int32, (8,), 0)
    where = jnp.zeros((8,), jnp.int32)
    for i, value in enumerate((x, y, z, core, xh, jnp.where(core == 0, x, y), jnp.where(core == 0, z, x))):
        where = jnp.where(spot == i, value, where)

    arrived = {}
    for ring in ("x", "z", "y"):
        blocks = pack(ring, where, grad, basis_new)
        arrived[ring] = exchange(blocks, RINGS[ring])

    moments = cut_moments(where, moment_first, moment_second, basis_new, basis_old)
    moments = lax.all_to_all(moments, ROW, 0, 0, tiled=True)
    margin = sum_margin(moments)
    margin = lax.all_to_all(margin, ROW, 0, 0, tiled=True).reshape(256, 512)
    margin_other = shift(margin, RINGS["core"], 1)

    totals, gathered = {}, {"y": basis_new}
    for group, blocks in ((1, arrived["x"]), (0, arrived["y"] + arrived["z"])):
        other, rows = project(group, where, blocks, basis_new)
        gathered["z" if group == 0 else "x"] = rows
        other = shift(other, RINGS["core"], 1)
        partial = project(group, where, blocks, basis_new, other, rows)
        halves = ordered(partial, U[group])
        rest = add_up(group, where, halves)
        totals[group] = ordered(rest, V[group])

    *lows, first_new, second_new = take_step(where, totals[0] + totals[1], margin, margin_other, moments)

    sent = {}
    for group, rings in ((1, ("x",)), (0, ("y", "z"))):
        low = lows[group]
        quarters = ordered([low] * 4, V[group])
        quarter = join(group, where, quarters)
        whole = ordered([quarter] * 4, U[group])
        whole = whole + [shift(array, RINGS["core"], 1) for array in whole]
        for ring in rings:
            blocks = update_blocks(ring, where, whole, gathered[ring])
            sent[ring] = exchange(blocks, RINGS[ring])
    update = None
    for ring in ("x", "y", "z"):
        update = unpack(ring, where, sent[ring], update, grad.shape[1])

    new = turn_back(first_new, second_new)
    new = lax.all_to_all(new, ROW, 0, 0, tiled=True)
    first, second = finish(new)
    return update, first, second


def solution(mesh):
    fine = Mesh(mesh.devices.reshape(SIZES), NAMES)
    col = ("y", "xh", "core")
    placed = (P(NAMES, None), P(ROW, None), P(ROW, None), P(ROW, col), P(ROW, col))
    return jax.shard_map(
        compute,
        mesh=fine,
        in_specs=placed,
        out_specs=(P(NAMES, None), P(ROW, col), P(ROW, col)),
        check_vma=False,
    )
```

```python
import functools
import itertools

import jax
import jax.numpy as jnp
from jax import lax
from jax.experimental import pallas as pl
from jax.experimental.pallas import tpu as pltpu
from jax.sharding import Mesh, PartitionSpec as P


STEP = 10
BF, F32 = jnp.bfloat16, jnp.float32
NAMES = ("xl", "z", "y", "xh", "core")
SIZES = (2, 4, 4, 2, 2)
ROW = ("xl", "z")
ANY = pl.BlockSpec(memory_space=pl.ANY)
SMEM = pl.BlockSpec(memory_space=pltpu.SMEM)
VMEM = pl.BlockSpec(memory_space=pltpu.VMEM)
HBM = pl.BlockSpec(memory_space=pltpu.HBM)
DMA = pltpu.SemaphoreType.DMA
LIMIT = pltpu.CompilerParams(vmem_limit_bytes=16 * 2**20)


def blocks_of(count, shape):
    return [pltpu.HBM(shape, BF)] + [jax.ShapeDtypeStruct(shape, BF)] * (count - 1)


STEPS = (0, 1, 3, 2)
WIDTH = {"y": 2048, "z": 2048, "x": 2560}
EXTRA = {"y": 0, "z": 512, "x": 512}


def with_basis(ring, step):
    return ring == "z" or (ring == "x" and step % 2 == 1)


GROUPS = ((2048, 128), (1280, 80))
TILE = (512, 640)
SLOT = {"x": 0, "y": 1, "z": 2, "core": 3, "xh": 4, "u0": 5, "v0": 6, "u1": 2, "v1": 1}
SPOTS = [dict(zip(NAMES, spot)) for spot in itertools.product(*(range(n) for n in SIZES))]


def place(where, axis):
    return where[SLOT[axis]]


def ring_shift(spot, ring, step):
    spot = dict(spot)
    if ring == "x":
        x = (spot["xh"] * 2 + spot["xl"] + step) % 4
        spot["xh"], spot["xl"] = x // 2, x % 2
    elif ring == "core":
        spot["core"] = 1 - spot["core"]
    else:
        spot[ring] = (spot[ring] + step) % 4
    return spot


def shift(array, rings, step):
    pairs = []
    for spot in SPOTS:
        target = ring_shift(spot, rings[spot["core"]], step)
        pairs.append((SPOTS.index(spot), SPOTS.index(target)))
    return lax.ppermute(array, NAMES, pairs)


RINGS = {ring: (ring, ring) for ring in ("x", "y", "z", "core")}
U = (("x", "y"), ("z", "z"))
V = (("z", "x"), ("y", "y"))


def runs(ring, at):
    out, done = [], 0
    if ring == "y":
        for xh in range(2):
            out.append((done, (at * 4 + xh * 2) * 1664, 1024))
            done += 1024
    elif ring == "z":
        for y, xh, xl in itertools.product(range(4), range(2), range(2)):
            out.append((done, (y * 4 + xh * 2 + 1) * 1664 + (xl * 4 + at) * 128, 128))
            done += 128
    else:
        xh, xl = at // 2, at % 2
        for core, y in itertools.product(range(2), range(4)):
            out.append((core * 1280 + y * 256, (y * 4 + xh * 2 + core) * 1664 + (8 + 2 * xl) * 128, 256))
    return out


def pieces(group, u_at):
    if group == 0:
        return [(u_at * 512, 512)]
    return [one for v in range(4) for one in ((v * 256 + u_at * 64, 64), (1024 + v * 64 + u_at * 16, 16))]


def in_hbm(array):
    return pltpu.with_memory_space_constraint(array, pltpu.HBM)


def rows_at(first, count):
    return pl.ds(pl.multiple_of(first, 16), count)


def estimate(flops, size):
    return pl.CostEstimate(flops=flops, bytes_accessed=size, transcendentals=0)


def start_all(copies):
    for copy in copies:
        copy.start()
    return copies


def wait_all(copies):
    for copy in copies:
        copy.wait()


def wait_for(ref, sem):
    pltpu.make_async_copy(ref, ref, sem).wait()


def turned(tile):
    return pltpu.roll(tile.astype(F32), 64, 1).astype(BF)


def pack_kernel(ring, where, grad, basis, *refs):
    outs, (held, in_sem, out_sem), more = refs[:4], refs[4:7], refs[7:]
    if ring == "x":
        ends, end_sem = more
        end_copies = start_all(
            [pltpu.make_async_copy(grad.at[:, pl.ds(b * 1664 + 1536, 128)], ends.at[b], end_sem.at[b]) for b in range(16)]
        )
    for at in range(4):
        start_all(
            [
                pltpu.make_async_copy(grad.at[:, pl.ds(source, count)], held.at[at, :, pl.ds(to, count)], in_sem.at[at])
                for to, source, count in runs(ring, at)
            ]
        )
        if EXTRA[ring]:
            rows = basis_rows("x", where, 0, basis)
            pltpu.make_async_copy(rows, held.at[at, :, pl.ds(WIDTH[ring], 512)], in_sem.at[at]).start()
    whole = held
    if ring == "x":
        wait_all(end_copies)
        left = lax.broadcasted_iota(jnp.int32, (128, 128), 1) < 64
        for xh, core, pair in itertools.product(range(2), range(2), range(2)):
            one, two = (ends[(2 * pair + i) * 4 + xh * 2 + core] for i in range(2))
            columns = pl.ds(core * 1280 + 1024 + pair * 128, 128)
            held[xh * 2, :, columns] = jnp.where(left, one, turned(two))
            held[xh * 2 + 1, :, columns] = jnp.where(left, turned(one), two)
        whole = held.at[:, :, pl.ds(0, 2560)]
    t = place(where, ring)
    stores = []
    for k, step in enumerate(STEPS):
        at = (t + step) % 4
        wait_for(whole.at[at], in_sem.at[at])
        source = held.at[at] if with_basis(ring, step) else held.at[at, :, pl.ds(0, WIDTH[ring])]
        copy = pltpu.make_async_copy(source, outs[k], out_sem.at[k])
        copy.start()
        stores.append(copy)
    wait_all(stores)


def pack(ring, where, grad, basis):
    width = WIDTH[ring] + EXTRA[ring]
    return pl.pallas_call(
        functools.partial(pack_kernel, ring),
        out_shape=[
            (jax.ShapeDtypeStruct if step else pltpu.HBM)((128, WIDTH[ring] + 512 * with_basis(ring, step)), BF)
            for step in STEPS
        ],
        in_specs=[SMEM, ANY, ANY],
        out_specs=[ANY] * 4,
        scratch_shapes=[pltpu.VMEM((4, 128, width), BF), DMA((4,)), DMA((4,))]
        + ([pltpu.VMEM((16, 128, 128), BF), DMA((16,))] if ring == "x" else []),
        compiler_params=LIMIT,
        cost_estimate=estimate(0, 4 * 128 * width * 4),
    )(where, in_hbm(grad), basis)


def unpack_kernel(ring, where, *refs):
    blocks = refs[:4]
    if ring == "x":
        out, held, in_sem, out_sem, ends, end_sem = refs[-6:]
    else:
        out, held, in_sem, out_sem = refs[-4:]
    t = place(where, ring)
    if ring != "x":
        stores = []
        for k, step in enumerate(STEPS):
            for j, (to, source, count) in enumerate(runs(ring, (t + 4 - step) % 4)):
                columns = pl.ds(pl.multiple_of(source, 128), count)
                stores.append(pltpu.make_async_copy(blocks[k].at[:, pl.ds(to, count)], out.at[:, columns], out_sem.at[k, j]))
        wait_all(start_all(stores))
        return
    start_all(
        [
            pltpu.make_async_copy(blocks[k], held.at[(t + 4 - step) % 4], in_sem.at[(t + 4 - step) % 4])
            for k, step in enumerate(STEPS)
        ]
    )
    stores = []
    for at in range(4):
        wait_for(held.at[at], in_sem.at[at])
        stores += start_all(
            [
                pltpu.make_async_copy(held.at[at, :, pl.ds(to, count)], out.at[:, pl.ds(source, count)], out_sem.at[at, j])
                for j, (to, source, count) in enumerate(runs(ring, at))
            ]
        )
    if ring == "x":
        left = lax.broadcasted_iota(jnp.int32, (128, 128), 1) < 64
        for xh, core, pair in itertools.product(range(2), range(2), range(2)):
            columns = pl.ds(core * 1280 + 1024 + pair * 128, 128)
            one, two = held[xh * 2, :, columns], held[xh * 2 + 1, :, columns]
            block = 2 * pair * 4 + xh * 2 + core
            ends[block] = jnp.where(left, one, turned(two))
            ends[block + 4] = jnp.where(left, turned(one), two)
        stores += start_all(
            [pltpu.make_async_copy(ends.at[b], out.at[:, pl.ds(b * 1664 + 1536, 128)], end_sem.at[b]) for b in range(16)]
        )
    wait_all(stores)


def unpack(ring, where, blocks, before, columns):
    width = WIDTH[ring]
    more = [] if before is None else [before]
    return pl.pallas_call(
        functools.partial(unpack_kernel, ring),
        out_shape=jax.ShapeDtypeStruct((128, columns), BF),
        in_specs=[SMEM] + [ANY if ring == "x" else VMEM] * 4 + [ANY] * len(more),
        out_specs=ANY,
        scratch_shapes=[pltpu.VMEM((4, 128, width if ring == "x" else 128), BF), DMA((4,)), DMA((4, 16))]
        + ([pltpu.VMEM((16, 128, 128), BF), DMA((16,))] if ring == "x" else []),
        input_output_aliases={5: 0} if more else {},
        compiler_params=LIMIT,
        cost_estimate=estimate(0, 4 * 128 * width * 4),
    )(where, *blocks, *more)


def basis_rows(ring, where, step, base):
    y, xh, core = place(where, "y"), place(where, "xh"), place(where, "core")
    if ring == "y":
        y = (y + step) % 4
    elif step % 4 == 2:
        xh = 1 - xh
    return base.at[pl.ds(pl.multiple_of((y * 4 + xh * 2 + core) * 128, 128), 128), :]


def start_basis(ring, where, blocks, basis, base, base_sem):
    for k, step in enumerate(STEPS):
        if with_basis(ring, step):
            source = blocks[k].at[:, pl.ds(WIDTH[ring], 512)]
        else:
            source = basis_rows(ring, where, 4 - step, basis)
        pltpu.make_async_copy(source, base.at[pl.ds(k * 128, 128), :], base_sem).start()


def project_kernel(group, own, where, *refs):
    count = 8 if group == 0 else 4
    blocks, basis, refs = list(refs[:count]), refs[count], refs[count + 1 :]
    if own:
        other, gathered, outs, (base, total, mine, base_sem, out_sem, in_sem) = refs[0], refs[1], refs[2:6], refs[6:]
    else:
        total, gathered, base, gather, mine, base_sem, out_sem, in_sem, y_sem = refs
    chunk, tile = GROUPS[group][0], TILE[group]
    core, u = place(where, "core"), place(where, "u%d" % group)

    def fetch(block, first):
        copy = pltpu.make_async_copy(block.at[:, pl.ds(pl.multiple_of(first, 128), chunk)], mine, in_sem)
        copy.start()
        return copy

    def multiply(far, base, first):
        @pl.loop(0, chunk // tile)
        def _(i):
            some = pl.ds(pl.multiple_of(i * tile, tile), tile)
            columns = pl.ds(pl.multiple_of(first + i * tile, 128), tile)
            block = jnp.concatenate([mine[:, some]] + [ref[:, columns] for ref in far], axis=0)
            product = lax.dot_general(block, base[...], (((0,), (0,)), ((), ())), preferred_element_type=F32)
            if own:
                product = product + other[some, :].astype(F32)
            total[some, :] = product.astype(BF)
            if own and group == 0:
                for j in range(4):

                    @pl.when((u + j) % 4 == i)
                    def _():
                        pltpu.make_async_copy(total.at[some, :], outs[j], out_sem.at[j]).start()

    def with_y():
        copy = fetch(blocks[0], 0)
        start_basis("y", where, blocks[:4], basis, base, base_sem)
        wait_for(base, base_sem)
        copy.wait()
        multiply(blocks[1:4], base, 0)

    if own:

        def with_gathered(four, first):
            copy = fetch(four[0], first)
            wait_all(start_all([pltpu.make_async_copy(gathered, base, base_sem)]))
            copy.wait()
            multiply(four[1:], base, first)

        if group == 0:
            pl.when(core == 0)(with_y)
            pl.when(core == 1)(lambda: with_gathered(blocks[4:], 0))
            for j in range(4):
                wait_for(outs[j], out_sem.at[j])
            return
        with_gathered(blocks, core * chunk)
    else:
        ring, four = ("z", blocks[4:]) if group == 0 else ("x", blocks)
        start_basis(ring, where, four, basis, gather, base_sem)
        if group == 0:

            @pl.when(core == 1)
            def _():
                fetch(blocks[0], 0)
                start_basis("y", where, blocks[:4], basis, base, y_sem)

            @pl.when(core == 0)
            def _():
                fetch(blocks[4], 0)

        else:
            fetch(blocks[0], (1 - core) * chunk)
        wait_for(gather, base_sem)
        out_copy = pltpu.make_async_copy(gather, gathered, out_sem)
        out_copy.start()
        wait_for(mine, in_sem)
        if group == 0:

            @pl.when(core == 1)
            def _():
                wait_for(base, y_sem)
                multiply(blocks[1:4], base, 0)

            @pl.when(core == 0)
            def _():
                multiply(blocks[5:], gather, 0)

        else:
            multiply(blocks[1:], gather, (1 - core) * chunk)
        out_copy.wait()
        return
    stores = []
    for j in range(4):
        done = 0
        for first, size in pieces(group, (u + j) % 4):
            stores.append(
                pltpu.make_async_copy(total.at[rows_at(first, size), :], outs[j].at[pl.ds(done, size), :], out_sem.at[j])
            )
            done += size
    start_all(stores)
    for j in range(4):
        wait_for(outs[j], out_sem.at[j])


def project(group, where, blocks, basis, other=None, gathered=None):
    chunk = GROUPS[group][0]
    own = other is not None
    shapes = blocks_of(4, (chunk // 4, 512))
    if not own:
        shapes = [jax.ShapeDtypeStruct((chunk, 512), BF), pltpu.HBM((512, 512), BF)]
    return pl.pallas_call(
        functools.partial(project_kernel, group, own),
        out_shape=shapes,
        in_specs=[SMEM] + ([ANY] + [VMEM] * 3) * (len(blocks) // 4) + [ANY] + ([VMEM, ANY] if own else []),
        out_specs=[ANY] * 4 if own else [VMEM, ANY],
        scratch_shapes=[
            pltpu.VMEM((512, 512), BF),
            pltpu.VMEM((chunk if own else 512, 512), BF),
            pltpu.VMEM((128, chunk), BF),
            DMA,
            DMA((4,)) if own else DMA,
            DMA,
        ]
        + ([] if own else [DMA]),
        compiler_params=LIMIT,
        cost_estimate=estimate(2 * 512 * 512 * chunk, 512 * chunk * 2 + 512 * 1024 + chunk * 1024),
    )(
        where,
        *(in_hbm(block) if i % 4 == 0 else block for i, block in enumerate(blocks)),
        basis,
        *([other, in_hbm(gathered)] if own else []),
    )


def add_kernel(group, where, mine, b, c, d, *refs):
    outs, total, a, far, sem, in_sem = refs[:4], refs[4], refs[5], refs[6], refs[7], refs[8]
    piece = GROUPS[group][1]
    loads = start_all([pltpu.make_async_copy(mine, a, in_sem)])
    far[...] = b[...].astype(F32) + (c[...].astype(F32) + d[...].astype(F32))
    wait_all(loads)
    total[...] = (a[...].astype(F32) + far[...]).astype(BF)
    copies = []
    for j in range(4):
        at = (place(where, "v%d" % group) + j) % 4
        copies.append(pltpu.make_async_copy(total.at[rows_at(at * piece, piece), :], outs[j], sem.at[j]))
    wait_all(start_all(copies))


def add_up(group, where, arrays):
    chunk, piece = GROUPS[group]
    return pl.pallas_call(
        functools.partial(add_kernel, group),
        out_shape=[pltpu.HBM((piece, 512), BF)] * 4,
        in_specs=[SMEM, ANY] + [VMEM] * 3,
        out_specs=[ANY] * 4,
        scratch_shapes=[pltpu.VMEM((chunk // 4, 512), BF)] * 2 + [pltpu.VMEM((chunk // 4, 512), F32), DMA((4,)), DMA],
        compiler_params=LIMIT,
        cost_estimate=estimate(3 * chunk * 128, 5 * chunk * 256),
    )(where, in_hbm(arrays[0]), *arrays[1:])


def moments_kernel(where, first, second, new, old, result, half, old_held, out, sem):
    core = place(where, "core")
    columns = pl.ds(pl.multiple_of(core * 256, 256), 256)
    copies = start_all([pltpu.make_async_copy(new.at[:, columns], half, sem.at[0]), pltpu.make_async_copy(old, old_held, sem.at[1])])
    left = lax.broadcasted_iota(jnp.int32, (64, 128), 1) < 64
    for q in range(8):
        for ref, begin in ((first, 0), (second, 128)):
            one = ref[:, q * 128 : q * 128 + 128]
            two = ref[:, 1024 + q // 2 * 128 : 1152 + q // 2 * 128]
            if q % 2:
                two = pltpu.roll(two, 64, 1)
            two = jnp.where(left, two, pltpu.roll(ref[:, 1536:1664], (192 - q * 16) % 128, 1))
            for i, value in enumerate((one, two)):
                high = value.astype(BF)
                out[q, begin : begin + 64, i * 128 : i * 128 + 128] = high
                if begin == 0:
                    out[q, 64:128, i * 128 : i * 128 + 128] = (value - high.astype(F32)).astype(BF)
    wait_all(copies)
    margin = lax.dot_general(half[...], old_held[...], (((0,), (0,)), ((), ())), preferred_element_type=F32)
    margin = margin.astype(BF)
    for q in range(8):
        for i in range(2):
            out[q, 192 + 32 * i : 224 + 32 * i, :] = margin[q * 32 : q * 32 + 32, i * 256 : i * 256 + 256]
    wait_all(start_all([pltpu.make_async_copy(out, result, sem.at[2])]))


def cut_moments(where, first, second, new, old):
    return pl.pallas_call(
        moments_kernel,
        out_shape=pltpu.HBM((8, 256, 256), BF),
        in_specs=[SMEM, VMEM, VMEM, ANY, ANY],
        out_specs=ANY,
        scratch_shapes=[
            pltpu.VMEM((2048, 256), BF),
            pltpu.VMEM((2048, 512), BF),
            pltpu.VMEM((8, 256, 256), BF),
            DMA((3,)),
        ],
        compiler_params=LIMIT,
        cost_estimate=estimate(2 * 2048 * 256 * 512, 6 * 2**20),
        name="cut_moments",
    )(where, first, second, new, in_hbm(old))


def margin_kernel(moments, out, held, sem):
    copy = pltpu.make_async_copy(moments.at[:, pl.ds(192, 64), :], held, sem)
    copy.start()
    copy.wait()
    total = held[0].astype(F32)
    for i in range(1, 8):
        total = total + held[i].astype(F32)
    total = total.astype(BF)
    for i in range(8):
        out[i, :, 0:256] = total[:32]
        out[i, :, 256:512] = total[32:]


def sum_margin(moments):
    return pl.pallas_call(
        margin_kernel,
        out_shape=jax.ShapeDtypeStruct((8, 32, 512), BF),
        in_specs=[ANY],
        out_specs=VMEM,
        scratch_shapes=[pltpu.VMEM((8, 64, 256), BF), DMA],
        compiler_params=LIMIT,
        cost_estimate=estimate(8 * 64 * 256, 2**19),
        name="sum_margin",
    )(moments)


def step_kernel(where, *refs):
    sums, (own, other, moments), lows = refs[:8], refs[8:11], refs[11:13]
    first_out, second_out, margin, mine, in_sem = refs[13:]
    core = place(where, "core")
    copies = [
        pltpu.make_async_copy(sums[0], mine.at[pl.ds(0, 128), :], in_sem.at[0]),
        pltpu.make_async_copy(sums[4], mine.at[pl.ds(128, 80), :], in_sem.at[1]),
    ]
    start_all(copies)
    margin[rows_at(core * 256, 256), :] = own[...]
    margin[rows_at(256 - core * 256, 256), :] = other[...]
    contract = (((0,), (1,)), ((), ()))
    one, one_low, two = (moments[:, i * 64 : i * 64 + 64, :].reshape(512, 256) for i in range(3))
    rotated_one = lax.dot_general(one, margin[...], contract, preferred_element_type=F32)
    rotated_one = rotated_one + lax.dot_general(one_low, margin[...], contract, preferred_element_type=F32)
    wide = margin[...].astype(F32)
    rotated_two = lax.dot_general(two, (wide * wide).astype(BF), contract, preferred_element_type=F32)
    wait_all(copies)
    projected = mine[...].astype(F32) + jnp.concatenate(
        [sum(ref[...].astype(F32) for ref in sums[4 * g + 1 : 4 * g + 4]) for g in range(2)], axis=0
    )
    first_new = 0.9 * rotated_one[:208] + 0.1 * projected
    second_new = 0.999 * rotated_two[:208] + 0.001 * projected * projected
    low_step = (
        first_new / (1.0 - 0.9**STEP) / (jnp.sqrt(second_new / (1.0 - 0.999**STEP)) + 1e-08)
    ).astype(BF)
    begin = 0
    for ref in lows:
        ref[...] = low_step[begin : begin + ref.shape[0], :]
        begin += ref.shape[0]
    first_out[...] = first_new
    second_out[...] = second_new


def take_step(where, sums, *rest):
    return pl.pallas_call(
        step_kernel,
        out_shape=[jax.ShapeDtypeStruct((piece, 512), BF) for _, piece in GROUPS]
        + [jax.ShapeDtypeStruct((208, 512), F32)] * 2,
        in_specs=[SMEM] + ([ANY] + [VMEM] * 3) * 2 + [VMEM] * 3,
        out_specs=[VMEM] * 4,
        scratch_shapes=[pltpu.VMEM((512, 512), BF), pltpu.VMEM((208, 512), BF), DMA((2,))],
        compiler_params=LIMIT,
        cost_estimate=estimate(6 * 208 * 512 * 512, 4 * 2**20),
        name="step",
    )(where, in_hbm(sums[0]), *sums[1:4], in_hbm(sums[4]), *sums[5:], *rest)


def turn_kernel(first, second, result, wide, out, sem):
    wide[208:, :] = jnp.zeros((48, 512), F32)
    for i, ref in enumerate((first, second)):
        wide[:208, :] = ref[...]
        out[:, i * 64 : i * 64 + 64, :] = wide[...].T.astype(BF).reshape(8, 64, 256)
    wait_all(start_all([pltpu.make_async_copy(out, result, sem)]))


def turn_back(first, second):
    return pl.pallas_call(
        turn_kernel,
        out_shape=pltpu.HBM((8, 128, 256), BF),
        in_specs=[VMEM] * 2,
        out_specs=ANY,
        scratch_shapes=[pltpu.VMEM((256, 512), F32), pltpu.VMEM((8, 128, 256), BF), DMA],
        compiler_params=LIMIT,
        cost_estimate=estimate(208 * 1024, 3 * 2**19),
        name="turn_back",
    )(first, second)


def finish_kernel(new, *outs):
    lane = lax.broadcasted_iota(jnp.int32, (64, 128), 1)
    for i, out in enumerate(outs):
        rest = []
        for q in range(8):
            block = new[q, i * 64 : i * 64 + 64, :].astype(F32)
            out[:, q * 128 : q * 128 + 128] = block[:, :128]
            rest.append(block[:, 128:])
        for j in range(4):
            out[:, 1024 + j * 128 : 1152 + j * 128] = jnp.where(lane < 64, rest[2 * j], pltpu.roll(rest[2 * j + 1], 64, 1))
        last = pltpu.roll(rest[0], 64, 1)
        for q in range(1, 8):
            last = jnp.where(lane // 16 == q, pltpu.roll(rest[q], (64 + q * 16) % 128, 1) if q != 4 else rest[q], last)
        out[:, 1536:1664] = last


def finish(new):
    return pl.pallas_call(
        finish_kernel,
        out_shape=[jax.ShapeDtypeStruct((64, 1664), F32)] * 2,
        in_specs=[VMEM],
        out_specs=[VMEM] * 2,
        compiler_params=LIMIT,
        cost_estimate=estimate(64 * 1664 * 4, 3 * 2**19),
        name="finish",
    )(new)


def join_kernel(group, where, *refs):
    arrays, out = refs[:4], refs[4]
    piece = GROUPS[group][1]
    for j in range(4):
        at = (place(where, "v%d" % group) + 4 - j) % 4
        out[rows_at(at * piece, piece), :] = arrays[j][...]


def join(group, where, arrays):
    chunk = GROUPS[group][0]
    return pl.pallas_call(
        functools.partial(join_kernel, group),
        out_shape=jax.ShapeDtypeStruct((chunk // 4, 512), BF),
        in_specs=[SMEM] + [VMEM] * 4,
        out_specs=VMEM,
        compiler_params=LIMIT,
        cost_estimate=estimate(0, chunk * 512),
    )(where, *arrays)


def low_copies(group, where, arrays, begin, low, in_sem, core_of_arrays):
    if group == 0:
        u = jnp.where(core_of_arrays == 0, place(where, "x"), place(where, "y"))
    else:
        u = place(where, "u1")
    copies = []
    for j in range(4):
        done = 0
        at = (u + 4 - j) % 4
        for first, size in pieces(group, at):
            copies.append(
                pltpu.make_async_copy(
                    arrays[j].at[pl.ds(done, size), :], low.at[rows_at(begin + first, size), :], in_sem.at[at]
                )
            )
            done += size
    return copies


def update_kernel(ring, where, *refs):
    own, other, basis, outs = refs[:4], refs[4:8], refs[8], refs[9:13]
    low, base, held, in_sem, other_sem, base_sem, out_sem = refs[13:]
    core = place(where, "core")
    width = WIDTH[ring]
    for k, step in enumerate(STEPS):
        if ring == "y":
            source = basis_rows(ring, where, step, basis)
        else:
            source = basis.at[pl.ds(STEPS.index((4 - step) % 4) * 128, 128), :]
        pltpu.make_async_copy(source, base.at[pl.ds(k * 128, 128), :], base_sem).start()
    if ring == "x":
        start_all(low_copies(1, where, own, core * 1280, low, in_sem, core))
        start_all(low_copies(1, where, other, (1 - core) * 1280, low, other_sem, 1 - core))
        for at in range(4):
            wait_for(low.at[pl.ds(0, 320), :], in_sem.at[at])
            wait_for(low.at[pl.ds(0, 320), :], other_sem.at[at])
    else:
        part_core = 0 if ring == "y" else 1
        for arrays, chosen in ((own, core == part_core), (other, core != part_core)):

            @pl.when(chosen)
            def _():
                start_all(low_copies(0, where, arrays, 0, low, in_sem, jnp.int32(part_core)))

    wait_for(base, base_sem)

    @pl.loop(0, width // 512)
    def _(i):
        columns = pl.ds(pl.multiple_of(i * 512, 512), 512)
        if ring != "x":
            wait_for(low.at[columns, :], in_sem.at[i])
        product = lax.dot_general(base[...], low[columns, :], (((1,), (1,)), ((), ())), preferred_element_type=F32)
        held[:, columns] = (8.0 * product).astype(BF)
        for k in range(4):
            pltpu.make_async_copy(
                held.at[pl.ds(k * 128, 128), columns], outs[k].at[:, columns], out_sem.at[k]
            ).start()

    for k in range(4):
        wait_for(held.at[pl.ds(k * 128, 128), :], out_sem.at[k])


def update_blocks(ring, where, arrays, basis):
    width = WIDTH[ring]
    return pl.pallas_call(
        functools.partial(update_kernel, ring),
        out_shape=blocks_of(4, (128, width)),
        in_specs=[SMEM] + [ANY] * 9,
        out_specs=[ANY] * 4,
        scratch_shapes=[
            pltpu.VMEM((width, 512), BF),
            pltpu.VMEM((512, 512), BF),
            pltpu.VMEM((512, width), BF),
            DMA((4,)),
            DMA((4,)),
            DMA,
            DMA((4,)),
        ],
        compiler_params=LIMIT,
        cost_estimate=estimate(2 * 512 * 512 * width, 512 * width * 2 + 512 * 1024 + width * 1024),
    )(where, *arrays, basis if ring == "y" else in_hbm(basis))


def exchange(blocks, rings):
    return [blocks[0]] + [shift(block, rings, step) for block, step in zip(blocks[1:], STEPS[1:])]


def ordered(arrays, rings):
    out = dict([(0, arrays[0])] + [(j, shift(arrays[j], rings, j)) for j in STEPS[1:]])
    return [out[j] for j in range(4)]


def compute(grad, basis_new, basis_old, moment_first, moment_second):
    xl, z, y, xh, core = (lax.axis_index(name).astype(jnp.int32) for name in NAMES)
    x = xh * 2 + xl
    spot = lax.broadcasted_iota(jnp.int32, (8,), 0)
    where = jnp.zeros((8,), jnp.int32)
    for i, value in enumerate((x, y, z, core, xh, jnp.where(core == 0, x, y), jnp.where(core == 0, z, x))):
        where = jnp.where(spot == i, value, where)

    arrived = {}
    for ring in ("x", "z", "y"):
        blocks = pack(ring, where, grad, basis_new)
        arrived[ring] = exchange(blocks, RINGS[ring])

    moments = cut_moments(where, moment_first, moment_second, basis_new, basis_old)
    moments = lax.all_to_all(moments, ROW, 0, 0, tiled=True)
    margin = sum_margin(moments)
    margin = lax.all_to_all(margin, ROW, 0, 0, tiled=True).reshape(256, 512)
    margin_other = shift(margin, RINGS["core"], 1)

    totals, gathered = {}, {"y": basis_new}
    for group, blocks in ((1, arrived["x"]), (0, arrived["y"] + arrived["z"])):
        other, rows = project(group, where, blocks, basis_new)
        gathered["z" if group == 0 else "x"] = rows
        other = shift(other, RINGS["core"], 1)
        partial = project(group, where, blocks, basis_new, other, rows)
        halves = ordered(partial, U[group])
        rest = add_up(group, where, halves)
        totals[group] = ordered(rest, V[group])

    *lows, first_new, second_new = take_step(where, totals[0] + totals[1], margin, margin_other, moments)

    sent = {}
    for group, rings in ((1, ("x",)), (0, ("y", "z"))):
        low = lows[group]
        quarters = ordered([low] * 4, V[group])
        quarter = join(group, where, quarters)
        whole = ordered([quarter] * 4, U[group])
        whole = whole + [shift(array, RINGS["core"], 1) for array in whole]
        for ring in rings:
            blocks = update_blocks(ring, where, whole, gathered[ring])
            sent[ring] = exchange(blocks, RINGS[ring])
    update = None
    for ring in ("x", "y", "z"):
        update = unpack(ring, where, sent[ring], update, grad.shape[1])

    new = turn_back(first_new, second_new)
    new = lax.all_to_all(new, ROW, 0, 0, tiled=True)
    first, second = finish(new)
    return update, first, second


def solution(mesh):
    fine = Mesh(mesh.devices.reshape(SIZES), NAMES)
    col = ("y", "xh", "core")
    placed = (P(NAMES, None), P(ROW, None), P(ROW, None), P(ROW, col), P(ROW, col))
    return jax.shard_map(
        compute,
        mesh=fine,
        in_specs=placed,
        out_specs=(P(NAMES, None), P(ROW, col), P(ROW, col)),
        check_vma=False,
    )
```

```python
import functools
import itertools

import jax
import jax.numpy as jnp
from jax import lax
from jax.experimental import pallas as pl
from jax.experimental.pallas import tpu as pltpu
from jax.sharding import Mesh, PartitionSpec as P


STEP = 10
BF, F32 = jnp.bfloat16, jnp.float32
NAMES = ("xl", "z", "y", "xh", "core")
SIZES = (2, 4, 4, 2, 2)
ROW = ("xl", "z")
ANY = pl.BlockSpec(memory_space=pl.ANY)
SMEM = pl.BlockSpec(memory_space=pltpu.SMEM)
VMEM = pl.BlockSpec(memory_space=pltpu.VMEM)
HBM = pl.BlockSpec(memory_space=pltpu.HBM)
DMA = pltpu.SemaphoreType.DMA
LIMIT = pltpu.CompilerParams(vmem_limit_bytes=16 * 2**20)


def blocks_of(count, shape):
    return [pltpu.HBM(shape, BF)] + [jax.ShapeDtypeStruct(shape, BF)] * (count - 1)


STEPS = (0, 1, 3, 2)
WIDTH = {"y": 2048, "z": 2048, "x": 2560}
EXTRA = {"y": 0, "z": 512, "x": 512}


def with_basis(ring, step):
    return ring == "z" or (ring == "x" and step % 2 == 1)


GROUPS = ((2048, 128), (1280, 80))
TILE = (512, 640)
SLOT = {"x": 0, "y": 1, "z": 2, "core": 3, "xh": 4, "u0": 5, "v0": 6, "u1": 2, "v1": 1}
SPOTS = [dict(zip(NAMES, spot)) for spot in itertools.product(*(range(n) for n in SIZES))]


def place(where, axis):
    return where[SLOT[axis]]


def ring_shift(spot, ring, step):
    spot = dict(spot)
    if ring == "x":
        x = (spot["xh"] * 2 + spot["xl"] + step) % 4
        spot["xh"], spot["xl"] = x // 2, x % 2
    elif ring == "core":
        spot["core"] = 1 - spot["core"]
    else:
        spot[ring] = (spot[ring] + step) % 4
    return spot


def shift(array, rings, step):
    pairs = []
    for spot in SPOTS:
        target = ring_shift(spot, rings[spot["core"]], step)
        pairs.append((SPOTS.index(spot), SPOTS.index(target)))
    return lax.ppermute(array, NAMES, pairs)


RINGS = {ring: (ring, ring) for ring in ("x", "y", "z", "core")}
U = (("x", "y"), ("z", "z"))
V = (("z", "x"), ("y", "y"))


def runs(ring, at):
    out, done = [], 0
    if ring == "y":
        for xh in range(2):
            out.append((done, (at * 4 + xh * 2) * 1664, 1024))
            done += 1024
    elif ring == "z":
        for y, xh, xl in itertools.product(range(4), range(2), range(2)):
            out.append((done, (y * 4 + xh * 2 + 1) * 1664 + (xl * 4 + at) * 128, 128))
            done += 128
    else:
        xh, xl = at // 2, at % 2
        for core, y in itertools.product(range(2), range(4)):
            out.append((core * 1280 + y * 256, (y * 4 + xh * 2 + core) * 1664 + (8 + 2 * xl) * 128, 256))
    return out


def pieces(group, u_at):
    if group == 0:
        return [(u_at * 512, 512)]
    return [one for v in range(4) for one in ((v * 256 + u_at * 64, 64), (1024 + v * 64 + u_at * 16, 16))]


def in_hbm(array):
    return pltpu.with_memory_space_constraint(array, pltpu.HBM)


def rows_at(first, count):
    return pl.ds(pl.multiple_of(first, 16), count)


def estimate(flops, size):
    return pl.CostEstimate(flops=flops, bytes_accessed=size, transcendentals=0)


def start_all(copies):
    for copy in copies:
        copy.start()
    return copies


def wait_all(copies):
    for copy in copies:
        copy.wait()


def wait_for(ref, sem):
    pltpu.make_async_copy(ref, ref, sem).wait()


def turned(tile):
    return pltpu.roll(tile.astype(F32), 64, 1).astype(BF)


def pack_kernel(ring, where, grad, basis, *refs):
    outs, (held, in_sem, out_sem), more = refs[:4], refs[4:7], refs[7:]
    if ring == "x":
        ends, end_sem = more
        end_copies = start_all(
            [pltpu.make_async_copy(grad.at[:, pl.ds(b * 1664 + 1536, 128)], ends.at[b], end_sem.at[b]) for b in range(16)]
        )
    for at in range(4):
        start_all(
            [
                pltpu.make_async_copy(grad.at[:, pl.ds(source, count)], held.at[at, :, pl.ds(to, count)], in_sem.at[at])
                for to, source, count in runs(ring, at)
            ]
        )
        if EXTRA[ring]:
            rows = basis_rows("x", where, 0, basis)
            pltpu.make_async_copy(rows, held.at[at, :, pl.ds(WIDTH[ring], 512)], in_sem.at[at]).start()
    whole = held
    if ring == "x":
        wait_all(end_copies)
        left = lax.broadcasted_iota(jnp.int32, (128, 128), 1) < 64
        for xh, core, pair in itertools.product(range(2), range(2), range(2)):
            one, two = (ends[(2 * pair + i) * 4 + xh * 2 + core] for i in range(2))
            columns = pl.ds(core * 1280 + 1024 + pair * 128, 128)
            held[xh * 2, :, columns] = jnp.where(left, one, turned(two))
            held[xh * 2 + 1, :, columns] = jnp.where(left, turned(one), two)
        whole = held.at[:, :, pl.ds(0, 2560)]
    t = place(where, ring)
    stores = []
    for k, step in enumerate(STEPS):
        at = (t + step) % 4
        wait_for(whole.at[at], in_sem.at[at])
        source = held.at[at] if with_basis(ring, step) else held.at[at, :, pl.ds(0, WIDTH[ring])]
        copy = pltpu.make_async_copy(source, outs[k], out_sem.at[k])
        copy.start()
        stores.append(copy)
    wait_all(stores)


def pack(ring, where, grad, basis):
    width = WIDTH[ring] + EXTRA[ring]
    return pl.pallas_call(
        functools.partial(pack_kernel, ring),
        out_shape=[
            (jax.ShapeDtypeStruct if step else pltpu.HBM)((128, WIDTH[ring] + 512 * with_basis(ring, step)), BF)
            for step in STEPS
        ],
        in_specs=[SMEM, ANY, ANY],
        out_specs=[ANY] * 4,
        scratch_shapes=[pltpu.VMEM((4, 128, width), BF), DMA((4,)), DMA((4,))]
        + ([pltpu.VMEM((16, 128, 128), BF), DMA((16,))] if ring == "x" else []),
        compiler_params=LIMIT,
        cost_estimate=estimate(0, 4 * 128 * width * 4),
    )(where, in_hbm(grad), in_hbm(basis))


def unpack_kernel(ring, where, *refs):
    blocks = refs[:4]
    if ring == "x":
        out, held, in_sem, out_sem, ends, end_sem = refs[-6:]
    else:
        out, held, in_sem, out_sem = refs[-4:]
    t = place(where, ring)
    if ring != "x":
        stores = []
        for k, step in enumerate(STEPS):
            for j, (to, source, count) in enumerate(runs(ring, (t + 4 - step) % 4)):
                columns = pl.ds(pl.multiple_of(source, 128), count)
                stores.append(pltpu.make_async_copy(blocks[k].at[:, pl.ds(to, count)], out.at[:, columns], out_sem.at[k, j]))
        wait_all(start_all(stores))
        return
    start_all(
        [
            pltpu.make_async_copy(blocks[k], held.at[(t + 4 - step) % 4], in_sem.at[(t + 4 - step) % 4])
            for k, step in enumerate(STEPS)
        ]
    )
    stores = []
    for at in range(4):
        wait_for(held.at[at], in_sem.at[at])
        stores += start_all(
            [
                pltpu.make_async_copy(held.at[at, :, pl.ds(to, count)], out.at[:, pl.ds(source, count)], out_sem.at[at, j])
                for j, (to, source, count) in enumerate(runs(ring, at))
            ]
        )
    if ring == "x":
        left = lax.broadcasted_iota(jnp.int32, (128, 128), 1) < 64
        for xh, core, pair in itertools.product(range(2), range(2), range(2)):
            columns = pl.ds(core * 1280 + 1024 + pair * 128, 128)
            one, two = held[xh * 2, :, columns], held[xh * 2 + 1, :, columns]
            block = 2 * pair * 4 + xh * 2 + core
            ends[block] = jnp.where(left, one, turned(two))
            ends[block + 4] = jnp.where(left, turned(one), two)
        stores += start_all(
            [pltpu.make_async_copy(ends.at[b], out.at[:, pl.ds(b * 1664 + 1536, 128)], end_sem.at[b]) for b in range(16)]
        )
    wait_all(stores)


def unpack(ring, where, blocks, before, columns):
    width = WIDTH[ring]
    more = [] if before is None else [before]
    return pl.pallas_call(
        functools.partial(unpack_kernel, ring),
        out_shape=jax.ShapeDtypeStruct((128, columns), BF),
        in_specs=[SMEM] + [ANY if ring == "x" else VMEM] * 4 + [ANY] * len(more),
        out_specs=ANY,
        scratch_shapes=[pltpu.VMEM((4, 128, width if ring == "x" else 128), BF), DMA((4,)), DMA((4, 16))]
        + ([pltpu.VMEM((16, 128, 128), BF), DMA((16,))] if ring == "x" else []),
        input_output_aliases={5: 0} if more else {},
        compiler_params=LIMIT,
        cost_estimate=estimate(0, 4 * 128 * width * 4),
    )(where, *blocks, *more)


def basis_rows(ring, where, step, base):
    y, xh, core = place(where, "y"), place(where, "xh"), place(where, "core")
    if ring == "y":
        y = (y + step) % 4
    elif step % 4 == 2:
        xh = 1 - xh
    return base.at[pl.ds(pl.multiple_of((y * 4 + xh * 2 + core) * 128, 128), 128), :]


def start_basis(ring, where, blocks, basis, base, base_sem):
    for k, step in enumerate(STEPS):
        if with_basis(ring, step):
            source = blocks[k].at[:, pl.ds(WIDTH[ring], 512)]
        else:
            source = basis_rows(ring, where, 4 - step, basis)
        pltpu.make_async_copy(source, base.at[pl.ds(k * 128, 128), :], base_sem).start()


def project_kernel(group, own, where, *refs):
    count = 8 if group == 0 else 4
    blocks, basis, refs = list(refs[:count]), refs[count], refs[count + 1 :]
    if own:
        other, gathered, outs, (base, total, mine, base_sem, out_sem, in_sem) = refs[0], refs[1], refs[2:6], refs[6:]
    else:
        total, gathered, base, gather, mine, base_sem, out_sem, in_sem, y_sem = refs
    chunk, tile = GROUPS[group][0], TILE[group]
    core, u = place(where, "core"), place(where, "u%d" % group)

    def fetch(block, first):
        copy = pltpu.make_async_copy(block.at[:, pl.ds(pl.multiple_of(first, 128), chunk)], mine, in_sem)
        copy.start()
        return copy

    def multiply(far, base, first):
        @pl.loop(0, chunk // tile)
        def _(i):
            some = pl.ds(pl.multiple_of(i * tile, tile), tile)
            columns = pl.ds(pl.multiple_of(first + i * tile, 128), tile)
            block = jnp.concatenate([mine[:, some]] + [ref[:, columns] for ref in far], axis=0)
            product = lax.dot_general(block, base[...], (((0,), (0,)), ((), ())), preferred_element_type=F32)
            if own:
                product = product + other[some, :].astype(F32)
            total[some, :] = product.astype(BF)
            if own and group == 0:
                for j in range(4):

                    @pl.when((u + j) % 4 == i)
                    def _():
                        pltpu.make_async_copy(total.at[some, :], outs[j], out_sem.at[j]).start()

    def with_y():
        copy = fetch(blocks[0], 0)
        start_basis("y", where, blocks[:4], basis, base, base_sem)
        wait_for(base, base_sem)
        copy.wait()
        multiply(blocks[1:4], base, 0)

    if own:

        def with_gathered(four, first):
            copy = fetch(four[0], first)
            wait_all(start_all([pltpu.make_async_copy(gathered, base, base_sem)]))
            copy.wait()
            multiply(four[1:], base, first)

        if group == 0:
            pl.when(core == 0)(with_y)
            pl.when(core == 1)(lambda: with_gathered(blocks[4:], 0))
            for j in range(4):
                wait_for(outs[j], out_sem.at[j])
            return
        with_gathered(blocks, core * chunk)
    else:
        ring, four = ("z", blocks[4:]) if group == 0 else ("x", blocks)
        start_basis(ring, where, four, basis, gather, base_sem)
        if group == 0:

            @pl.when(core == 1)
            def _():
                fetch(blocks[0], 0)
                start_basis("y", where, blocks[:4], basis, base, y_sem)

            @pl.when(core == 0)
            def _():
                fetch(blocks[4], 0)

        else:
            fetch(blocks[0], (1 - core) * chunk)
        wait_for(gather, base_sem)
        out_copy = pltpu.make_async_copy(gather, gathered, out_sem)
        out_copy.start()
        wait_for(mine, in_sem)
        if group == 0:

            @pl.when(core == 1)
            def _():
                wait_for(base, y_sem)
                multiply(blocks[1:4], base, 0)

            @pl.when(core == 0)
            def _():
                multiply(blocks[5:], gather, 0)

        else:
            multiply(blocks[1:], gather, (1 - core) * chunk)
        out_copy.wait()
        return
    stores = []
    for j in range(4):
        done = 0
        for first, size in pieces(group, (u + j) % 4):
            stores.append(
                pltpu.make_async_copy(total.at[rows_at(first, size), :], outs[j].at[pl.ds(done, size), :], out_sem.at[j])
            )
            done += size
    start_all(stores)
    for j in range(4):
        wait_for(outs[j], out_sem.at[j])


def project(group, where, blocks, basis, other=None, gathered=None):
    chunk = GROUPS[group][0]
    own = other is not None
    shapes = blocks_of(4, (chunk // 4, 512))
    if not own:
        shapes = [jax.ShapeDtypeStruct((chunk, 512), BF), pltpu.HBM((512, 512), BF)]
    return pl.pallas_call(
        functools.partial(project_kernel, group, own),
        out_shape=shapes,
        in_specs=[SMEM] + ([ANY] + [VMEM] * 3) * (len(blocks) // 4) + [ANY] + ([VMEM, ANY] if own else []),
        out_specs=[ANY] * 4 if own else [VMEM, ANY],
        scratch_shapes=[
            pltpu.VMEM((512, 512), BF),
            pltpu.VMEM((chunk if own else 512, 512), BF),
            pltpu.VMEM((128, chunk), BF),
            DMA,
            DMA((4,)) if own else DMA,
            DMA,
        ]
        + ([] if own else [DMA]),
        compiler_params=LIMIT,
        cost_estimate=estimate(2 * 512 * 512 * chunk, 512 * chunk * 2 + 512 * 1024 + chunk * 1024),
    )(
        where,
        *(in_hbm(block) if i % 4 == 0 else block for i, block in enumerate(blocks)),
        basis,
        *([other, in_hbm(gathered)] if own else []),
    )


def add_kernel(group, where, mine, b, c, d, *refs):
    outs, total, a, far, sem, in_sem = refs[:4], refs[4], refs[5], refs[6], refs[7], refs[8]
    piece = GROUPS[group][1]
    loads = start_all([pltpu.make_async_copy(mine, a, in_sem)])
    far[...] = b[...].astype(F32) + (c[...].astype(F32) + d[...].astype(F32))
    wait_all(loads)
    total[...] = (a[...].astype(F32) + far[...]).astype(BF)
    copies = []
    for j in range(4):
        at = (place(where, "v%d" % group) + j) % 4
        copies.append(pltpu.make_async_copy(total.at[rows_at(at * piece, piece), :], outs[j], sem.at[j]))
    wait_all(start_all(copies))


def add_up(group, where, arrays):
    chunk, piece = GROUPS[group]
    return pl.pallas_call(
        functools.partial(add_kernel, group),
        out_shape=[pltpu.HBM((piece, 512), BF)] * 4,
        in_specs=[SMEM, ANY] + [VMEM] * 3,
        out_specs=[ANY] * 4,
        scratch_shapes=[pltpu.VMEM((chunk // 4, 512), BF)] * 2 + [pltpu.VMEM((chunk // 4, 512), F32), DMA((4,)), DMA],
        compiler_params=LIMIT,
        cost_estimate=estimate(3 * chunk * 128, 5 * chunk * 256),
    )(where, in_hbm(arrays[0]), *arrays[1:])


def moments_kernel(where, first, second, new, old, result, half, old_held, out, sem):
    core = place(where, "core")
    columns = pl.ds(pl.multiple_of(core * 256, 256), 256)
    copies = start_all([pltpu.make_async_copy(new.at[:, columns], half, sem.at[0]), pltpu.make_async_copy(old, old_held, sem.at[1])])
    left = lax.broadcasted_iota(jnp.int32, (64, 128), 1) < 64
    for q in range(8):
        for ref, begin in ((first, 0), (second, 128)):
            one = ref[:, q * 128 : q * 128 + 128]
            two = ref[:, 1024 + q // 2 * 128 : 1152 + q // 2 * 128]
            if q % 2:
                two = pltpu.roll(two, 64, 1)
            two = jnp.where(left, two, pltpu.roll(ref[:, 1536:1664], (192 - q * 16) % 128, 1))
            for i, value in enumerate((one, two)):
                high = value.astype(BF)
                out[q, begin : begin + 64, i * 128 : i * 128 + 128] = high
                if begin == 0:
                    out[q, 64:128, i * 128 : i * 128 + 128] = (value - high.astype(F32)).astype(BF)
    wait_all(copies)
    margin = lax.dot_general(half[...], old_held[...], (((0,), (0,)), ((), ())), preferred_element_type=F32)
    margin = margin.astype(BF)
    for q in range(8):
        for i in range(2):
            out[q, 192 + 32 * i : 224 + 32 * i, :] = margin[q * 32 : q * 32 + 32, i * 256 : i * 256 + 256]
    wait_all(start_all([pltpu.make_async_copy(out, result, sem.at[2])]))


def cut_moments(where, first, second, new, old):
    return pl.pallas_call(
        moments_kernel,
        out_shape=pltpu.HBM((8, 256, 256), BF),
        in_specs=[SMEM, VMEM, VMEM, ANY, ANY],
        out_specs=ANY,
        scratch_shapes=[
            pltpu.VMEM((2048, 256), BF),
            pltpu.VMEM((2048, 512), BF),
            pltpu.VMEM((8, 256, 256), BF),
            DMA((3,)),
        ],
        compiler_params=LIMIT,
        cost_estimate=estimate(2 * 2048 * 256 * 512, 6 * 2**20),
        name="cut_moments",
    )(where, first, second, new, in_hbm(old))


def margin_kernel(moments, out, held, sem):
    copy = pltpu.make_async_copy(moments.at[:, pl.ds(192, 64), :], held, sem)
    copy.start()
    copy.wait()
    total = held[0].astype(F32)
    for i in range(1, 8):
        total = total + held[i].astype(F32)
    total = total.astype(BF)
    for i in range(8):
        out[i, :, 0:256] = total[:32]
        out[i, :, 256:512] = total[32:]


def sum_margin(moments):
    return pl.pallas_call(
        margin_kernel,
        out_shape=jax.ShapeDtypeStruct((8, 32, 512), BF),
        in_specs=[ANY],
        out_specs=VMEM,
        scratch_shapes=[pltpu.VMEM((8, 64, 256), BF), DMA],
        compiler_params=LIMIT,
        cost_estimate=estimate(8 * 64 * 256, 2**19),
        name="sum_margin",
    )(moments)


def step_kernel(where, *refs):
    sums, (own, other, moments), lows = refs[:8], refs[8:11], refs[11:13]
    first_out, second_out, margin, mine, in_sem = refs[13:]
    core = place(where, "core")
    copies = [
        pltpu.make_async_copy(sums[0], mine.at[pl.ds(0, 128), :], in_sem.at[0]),
        pltpu.make_async_copy(sums[4], mine.at[pl.ds(128, 80), :], in_sem.at[1]),
    ]
    start_all(copies)
    margin[rows_at(core * 256, 256), :] = own[...]
    margin[rows_at(256 - core * 256, 256), :] = other[...]
    contract = (((0,), (1,)), ((), ()))
    one, one_low, two = (moments[:, i * 64 : i * 64 + 64, :].reshape(512, 256) for i in range(3))
    rotated_one = lax.dot_general(one, margin[...], contract, preferred_element_type=F32)
    rotated_one = rotated_one + lax.dot_general(one_low, margin[...], contract, preferred_element_type=F32)
    wide = margin[...].astype(F32)
    rotated_two = lax.dot_general(two, (wide * wide).astype(BF), contract, preferred_element_type=F32)
    wait_all(copies)
    projected = mine[...].astype(F32) + jnp.concatenate(
        [sum(ref[...].astype(F32) for ref in sums[4 * g + 1 : 4 * g + 4]) for g in range(2)], axis=0
    )
    first_new = 0.9 * rotated_one[:208] + 0.1 * projected
    second_new = 0.999 * rotated_two[:208] + 0.001 * projected * projected
    low_step = (
        first_new / (1.0 - 0.9**STEP) / (jnp.sqrt(second_new / (1.0 - 0.999**STEP)) + 1e-08)
    ).astype(BF)
    begin = 0
    for ref in lows:
        ref[...] = low_step[begin : begin + ref.shape[0], :]
        begin += ref.shape[0]
    first_out[...] = first_new
    second_out[...] = second_new


def take_step(where, sums, *rest):
    return pl.pallas_call(
        step_kernel,
        out_shape=[jax.ShapeDtypeStruct((piece, 512), BF) for _, piece in GROUPS]
        + [jax.ShapeDtypeStruct((208, 512), F32)] * 2,
        in_specs=[SMEM] + ([ANY] + [VMEM] * 3) * 2 + [VMEM] * 3,
        out_specs=[VMEM] * 4,
        scratch_shapes=[pltpu.VMEM((512, 512), BF), pltpu.VMEM((208, 512), BF), DMA((2,))],
        compiler_params=LIMIT,
        cost_estimate=estimate(6 * 208 * 512 * 512, 4 * 2**20),
        name="step",
    )(where, in_hbm(sums[0]), *sums[1:4], in_hbm(sums[4]), *sums[5:], *rest)


def turn_kernel(first, second, result, wide, out, sem):
    wide[208:, :] = jnp.zeros((48, 512), F32)
    for i, ref in enumerate((first, second)):
        wide[:208, :] = ref[...]
        out[:, i * 64 : i * 64 + 64, :] = wide[...].T.astype(BF).reshape(8, 64, 256)
    wait_all(start_all([pltpu.make_async_copy(out, result, sem)]))


def turn_back(first, second):
    return pl.pallas_call(
        turn_kernel,
        out_shape=pltpu.HBM((8, 128, 256), BF),
        in_specs=[VMEM] * 2,
        out_specs=ANY,
        scratch_shapes=[pltpu.VMEM((256, 512), F32), pltpu.VMEM((8, 128, 256), BF), DMA],
        compiler_params=LIMIT,
        cost_estimate=estimate(208 * 1024, 3 * 2**19),
        name="turn_back",
    )(first, second)


def finish_kernel(new, *outs):
    lane = lax.broadcasted_iota(jnp.int32, (64, 128), 1)
    for i, out in enumerate(outs):
        rest = []
        for q in range(8):
            block = new[q, i * 64 : i * 64 + 64, :].astype(F32)
            out[:, q * 128 : q * 128 + 128] = block[:, :128]
            rest.append(block[:, 128:])
        for j in range(4):
            out[:, 1024 + j * 128 : 1152 + j * 128] = jnp.where(lane < 64, rest[2 * j], pltpu.roll(rest[2 * j + 1], 64, 1))
        last = pltpu.roll(rest[0], 64, 1)
        for q in range(1, 8):
            last = jnp.where(lane // 16 == q, pltpu.roll(rest[q], (64 + q * 16) % 128, 1) if q != 4 else rest[q], last)
        out[:, 1536:1664] = last


def finish(new):
    return pl.pallas_call(
        finish_kernel,
        out_shape=[jax.ShapeDtypeStruct((64, 1664), F32)] * 2,
        in_specs=[VMEM],
        out_specs=[VMEM] * 2,
        compiler_params=LIMIT,
        cost_estimate=estimate(64 * 1664 * 4, 3 * 2**19),
        name="finish",
    )(new)


def join_kernel(group, where, *refs):
    arrays, out = refs[:4], refs[4]
    piece = GROUPS[group][1]
    for j in range(4):
        at = (place(where, "v%d" % group) + 4 - j) % 4
        out[rows_at(at * piece, piece), :] = arrays[j][...]


def join(group, where, arrays):
    chunk = GROUPS[group][0]
    return pl.pallas_call(
        functools.partial(join_kernel, group),
        out_shape=jax.ShapeDtypeStruct((chunk // 4, 512), BF),
        in_specs=[SMEM] + [VMEM] * 4,
        out_specs=VMEM,
        compiler_params=LIMIT,
        cost_estimate=estimate(0, chunk * 512),
    )(where, *arrays)


def low_copies(group, where, arrays, begin, low, in_sem, core_of_arrays):
    if group == 0:
        u = jnp.where(core_of_arrays == 0, place(where, "x"), place(where, "y"))
    else:
        u = place(where, "u1")
    copies = []
    for j in range(4):
        done = 0
        at = (u + 4 - j) % 4
        for first, size in pieces(group, at):
            copies.append(
                pltpu.make_async_copy(
                    arrays[j].at[pl.ds(done, size), :], low.at[rows_at(begin + first, size), :], in_sem.at[at]
                )
            )
            done += size
    return copies


def start_update(ring, where, own, other, basis, low, base, in_sem, other_sem, base_sem):
    core = place(where, "core")
    for k, step in enumerate(STEPS):
        if ring == "y":
            source = basis_rows(ring, where, step, basis)
        else:
            source = basis.at[pl.ds(STEPS.index((4 - step) % 4) * 128, 128), :]
        pltpu.make_async_copy(source, base.at[pl.ds(k * 128, 128), :], base_sem).start()
    if ring == "x":
        start_all(low_copies(1, where, own, core * 1280, low, in_sem, core))
        start_all(low_copies(1, where, other, (1 - core) * 1280, low, other_sem, 1 - core))
        return
    part_core = 0 if ring == "y" else 1
    for arrays, chosen in ((own, core == part_core), (other, core != part_core)):

        @pl.when(chosen)
        def _():
            start_all(low_copies(0, where, arrays, 0, low, in_sem, jnp.int32(part_core)))


def end_update(ring, outs, low, base, held, in_sem, other_sem, base_sem, out_sem):
    if ring == "x":
        for at in range(4):
            wait_for(low.at[pl.ds(0, 320), :], in_sem.at[at])
            wait_for(low.at[pl.ds(0, 320), :], other_sem.at[at])
    wait_for(base, base_sem)

    @pl.loop(0, WIDTH[ring] // 512)
    def _(i):
        columns = pl.ds(pl.multiple_of(i * 512, 512), 512)
        if ring != "x":
            wait_for(low.at[columns, :], in_sem.at[i])
        product = lax.dot_general(base[...], low[columns, :], (((1,), (1,)), ((), ())), preferred_element_type=F32)
        held[:, columns] = (8.0 * product).astype(BF)
        for k in range(4):
            pltpu.make_async_copy(
                held.at[pl.ds(k * 128, 128), columns], outs[k].at[:, columns], out_sem.at[k]
            ).start()


def update_kernel(rings, where, *refs):
    n = len(rings)
    own, other, bases, outs, refs = refs[:4], refs[4:8], refs[8 : 8 + n], refs[8 + n : 8 + 5 * n], refs[8 + 5 * n :]
    scratch = [refs[7 * i : 7 * i + 7] for i in range(n)]
    for i, ring in enumerate(rings):
        low, base, _, in_sem, other_sem, base_sem, _ = scratch[i]
        start_update(ring, where, own, other, bases[i], low, base, in_sem, other_sem, base_sem)
    for i, ring in enumerate(rings):
        end_update(ring, outs[4 * i : 4 * i + 4], *scratch[i])
    for i in range(n):
        for k in range(4):
            wait_for(scratch[i][2].at[pl.ds(k * 128, 128), :], scratch[i][6].at[k])


def update_blocks(rings, where, arrays, bases):
    widths = [WIDTH[ring] for ring in rings]
    out = pl.pallas_call(
        functools.partial(update_kernel, rings),
        out_shape=[shape for width in widths for shape in blocks_of(4, (128, width))],
        in_specs=[SMEM] + [ANY] * (8 + len(rings)),
        out_specs=[ANY] * (4 * len(rings)),
        scratch_shapes=[
            shape
            for width in widths
            for shape in (
                pltpu.VMEM((width, 512), BF),
                pltpu.VMEM((512, 512), BF),
                pltpu.VMEM((512, width), BF),
                DMA((4,)),
                DMA((4,)),
                DMA,
                DMA((4,)),
            )
        ],
        compiler_params=LIMIT,
        cost_estimate=estimate(2 * 512 * 512 * sum(widths), sum(512 * w * 2 + 512 * 1024 + w * 1024 for w in widths)),
    )(where, *arrays, *(basis if ring == "y" else in_hbm(basis) for ring, basis in zip(rings, bases)))
    return [out[4 * i : 4 * i + 4] for i in range(len(rings))]


def exchange(blocks, rings):
    return [blocks[0]] + [shift(block, rings, step) for block, step in zip(blocks[1:], STEPS[1:])]


def ordered(arrays, rings):
    out = dict([(0, arrays[0])] + [(j, shift(arrays[j], rings, j)) for j in STEPS[1:]])
    return [out[j] for j in range(4)]


def compute(grad, basis_new, basis_old, moment_first, moment_second):
    xl, z, y, xh, core = (lax.axis_index(name).astype(jnp.int32) for name in NAMES)
    x = xh * 2 + xl
    spot = lax.broadcasted_iota(jnp.int32, (8,), 0)
    where = jnp.zeros((8,), jnp.int32)
    for i, value in enumerate((x, y, z, core, xh, jnp.where(core == 0, x, y), jnp.where(core == 0, z, x))):
        where = jnp.where(spot == i, value, where)

    arrived = {}
    for ring in ("x", "z", "y"):
        blocks = pack(ring, where, grad, basis_new)
        arrived[ring] = exchange(blocks, RINGS[ring])

    moments = cut_moments(where, moment_first, moment_second, basis_new, basis_old)
    moments = lax.all_to_all(moments, ROW, 0, 0, tiled=True)
    margin = sum_margin(moments)
    margin = lax.all_to_all(margin, ROW, 0, 0, tiled=True).reshape(256, 512)
    margin_other = shift(margin, RINGS["core"], 1)

    totals, gathered = {}, {"y": basis_new}
    for group, blocks in ((1, arrived["x"]), (0, arrived["y"] + arrived["z"])):
        other, rows = project(group, where, blocks, basis_new)
        gathered["z" if group == 0 else "x"] = rows
        other = shift(other, RINGS["core"], 1)
        partial = project(group, where, blocks, basis_new, other, rows)
        halves = ordered(partial, U[group])
        rest = add_up(group, where, halves)
        totals[group] = ordered(rest, V[group])

    *lows, first_new, second_new = take_step(where, totals[0] + totals[1], margin, margin_other, moments)

    sent = {}
    for group, rings in ((1, "x"), (0, "yz")):
        low = lows[group]
        quarters = ordered([low] * 4, V[group])
        quarter = join(group, where, quarters)
        whole = ordered([quarter] * 4, U[group])
        whole = whole + [shift(array, RINGS["core"], 1) for array in whole]
        blocks = update_blocks(rings, where, whole, [gathered[ring] for ring in rings])
        for i, ring in enumerate(rings):
            sent[ring] = exchange(blocks[i], RINGS[ring])
    update = None
    for ring in ("x", "y", "z"):
        update = unpack(ring, where, sent[ring], update, grad.shape[1])

    new = turn_back(first_new, second_new)
    new = lax.all_to_all(new, ROW, 0, 0, tiled=True)
    first, second = finish(new)
    return update, first, second


def solution(mesh):
    fine = Mesh(mesh.devices.reshape(SIZES), NAMES)
    col = ("y", "xh", "core")
    placed = (P(NAMES, None), P(ROW, None), P(ROW, None), P(ROW, col), P(ROW, col))
    return jax.shard_map(
        compute,
        mesh=fine,
        in_specs=placed,
        out_specs=(P(NAMES, None), P(ROW, col), P(ROW, col)),
        check_vma=False,
    )
```
